32 devices in a mesh: ctx: 16 (over z, y, x), fsdp: 2 (over core).
Axes of the slice: x: 2, y: 2, z: 4, core: 2. Of those that a mesh axis runs over, the one named last changes fastest.
Arguments:
- rotated_query_rows: bfloat16 [3072, 1024], P('ctx', 'fsdp'), may hold values from -6 to 6
- rotated_key_rows: bfloat16 [3072, 1024], P('ctx', 'fsdp'), may hold values from -6 to 6
- saved_value_rows: bfloat16 [3072, 1024], P('ctx', 'fsdp'), may hold values from -6 to 6
- projection_output_gradient: bfloat16 [3072, 5120], P('ctx', 'fsdp'), may hold values from -6 to 6
- frozen_weight_codes: int32 [5120, 1024], P('ctx', 'fsdp'), may hold values from 0 to 15
- block_scale_index: int32 [5120, 16], P('ctx', 'fsdp'), may hold values from 0 to 255
- block_scale_table: float32 [256], replicated, may hold values from 0.008385255 to 0.08385255
- adapter_down_matrix: bfloat16 [64, 1024], P('ctx', 'fsdp'), may hold values from -0.75 to 0.75
- adapter_up_matrix: bfloat16 [64, 5120], P('ctx', 'fsdp'), may hold values from -0.078125 to 0.078125
Outputs:
- query_grad: bfloat16 [3072, 1024], P('ctx', 'fsdp')
- key_grad: bfloat16 [3072, 1024], P('ctx', 'fsdp')
- value_grad: bfloat16 [3072, 1024], P('ctx', 'fsdp')
- down_matrix_gradient: float32 [64, 1024], P('ctx', 'fsdp')
- up_matrix_gradient: float32 [64, 5120], P('ctx', 'fsdp')
The draws below stay inside these ranges and needn't reach their ends.
All inputs are finite; a program needn't handle non-finite values.
Results may differ from the reference program's by a relative error of at most 0.0093.
Values may be sent and summed in bfloat16 or wider, within the bound.
No kernel may reach another device: no remote copies, remote signals or barrier semaphores. Data moves between devices by JAX's collectives and lax.ppermute only.
A program may use at most 64 MiB of HBM per device.

```python
import math
import jax
import jax.numpy as jnp
from jax import lax

MODEL_WIDTH = 5120
HEAD_WIDTH = 128
HPD = 4
ADAPTER_RANK = 64
QBLOCK = 64
LEVELS = 256
ATTENTION_HEADS = 8
SEQ = 3072
GROUP = 1536
SHIFT = 768


def drawn_pair(key):
    base_key = jax.random.fold_in(key, 7)
    query_key, key_key = jax.random.split(base_key, 2)
    full_shape = (SEQ, ATTENTION_HEADS * HEAD_WIDTH)
    query_base = 1.6 * jax.random.truncated_normal(query_key, -3.75, 3.75, full_shape, jnp.float32)
    key_base = 1.6 * jax.random.truncated_normal(key_key, -3.75, 3.75, full_shape, jnp.float32)
    return (query_base, key_base)


def draw_rotated_query_rows(key, part):
    return drawn_pair(key)[0].astype(jnp.bfloat16)


def draw_rotated_key_rows(key, part):
    return drawn_pair(key)[1].astype(jnp.bfloat16)


def place_ends(drawn, own_key, smallest, largest):
    extent = drawn.shape
    index_at = [jax.random.randint(jax.random.fold_in(own_key, axis), (), 0, extent[axis]) for axis in range(len(extent))]
    drawn = drawn.at[tuple(index_at)].set(smallest)
    longest = extent.index(max(extent))
    index_at[longest] = (index_at[longest] + 1) % extent[longest]
    return drawn.at[tuple(index_at)].set(largest)


def levels(stream_key, dims, cuts, least, top_value):
    def one(position, blocks):
        heights = jax.random.uniform(jax.random.fold_in(jax.random.fold_in(stream_key, 6), position), (blocks,), jnp.float32, least / len(cuts), top_value / len(cuts))
        return jnp.repeat(jnp.exp(heights), dims[position] // blocks).reshape((-1,) + (1,) * (len(dims) - position - 1))

    level = one(*cuts[0])
    for cut in cuts[1:]:
        level = level * one(*cut)
    return level


def bell_draw(rng, dims, spread, limit, shards=(), held_as=jnp.bfloat16):
    entries = spread * jax.random.normal(rng, dims, jnp.float32)
    if shards:
        entries = entries * levels(rng, dims, shards, -0.22, 0.18)
    return jnp.clip(entries, -limit, limit).astype(held_as)


def setup_inputs(seed: int = 0) -> dict:
    splits = jax.random.split(jax.random.key(seed), 10)
    rotated_query_rows = draw_rotated_query_rows(jax.random.fold_in(splits[9], 71), 0)
    rotated_key_rows = draw_rotated_key_rows(jax.random.fold_in(splits[9], 71), 0)
    saved_value_rows = bell_draw(splits[2], (SEQ, ATTENTION_HEADS * HEAD_WIDTH), 1.0, 6.0, ((0, 16), (1, 2)))
    projection_output_gradient = bell_draw(splits[3], (SEQ, MODEL_WIDTH), 1.0, 6.0, ((0, 16), (1, 2)))
    frozen_weight_codes = place_ends(jax.random.randint(splits[4], (MODEL_WIDTH, ATTENTION_HEADS * HEAD_WIDTH), 0, 16), jax.random.fold_in(splits[4], 1), 0, 15).astype(jnp.int32)
    block_scale_index = place_ends(jax.random.randint(splits[5], (MODEL_WIDTH, ATTENTION_HEADS * HEAD_WIDTH // QBLOCK), 0, LEVELS), jax.random.fold_in(splits[5], 1), 0, LEVELS - 1).astype(jnp.int32)
    block_scale_table = jnp.clip(jnp.exp(jax.random.uniform(splits[6], (LEVELS,), jnp.float32, math.log(0.008385255), math.log(0.08385255))), 0.008385255, 0.08385255)
    adapter_down_matrix = bell_draw(splits[7], (ADAPTER_RANK, ATTENTION_HEADS * HEAD_WIDTH), ADAPTER_RANK ** -0.5, 0.75, ((0, 16), (1, 2)))
    adapter_up_matrix = bell_draw(splits[8], (ADAPTER_RANK, MODEL_WIDTH), MODEL_WIDTH ** -0.5, 0.078125, ((0, 16), (1, 2)))
    return dict(rotated_query_rows=rotated_query_rows, rotated_key_rows=rotated_key_rows, saved_value_rows=saved_value_rows, projection_output_gradient=projection_output_gradient, frozen_weight_codes=frozen_weight_codes, block_scale_index=block_scale_index, block_scale_table=block_scale_table, adapter_down_matrix=adapter_down_matrix, adapter_up_matrix=adapter_up_matrix)


nf4_values = (-1.0, -0.6961928009986877, -0.5250730514526367, -0.39491748809814453, -0.28444138169288635, -0.18477343022823334, -0.09105003625154495, 0.0, 0.07958029955625534, 0.16093020141124725, 0.24611230194568634, 0.33791524171829224, 0.44070982933044434, 0.5626170039176941, 0.7229568362236023, 1.0)
adapter_scale = 0.25
masked = -1.0e30


def dequantize(frozen_weight_codes, block_scale_index, block_scale_table):
    table = jnp.asarray(nf4_values, dtype=jnp.float32)
    values = table[frozen_weight_codes]
    scales = jnp.repeat(block_scale_table[block_scale_index], QBLOCK, axis=1)
    return (values * scales).astype(jnp.bfloat16)


def attend_one(blocks_in):
    query_blk, key_blk, value_blk, grad_blk = blocks_in
    group_len = query_blk.shape[0]
    score_scale = HEAD_WIDTH ** -0.5
    scores = jnp.dot(query_blk, key_blk.T, preferred_element_type=jnp.float32) * score_scale
    row_iota = lax.broadcasted_iota(jnp.int32, (group_len, group_len), 0)
    col_iota = lax.broadcasted_iota(jnp.int32, (group_len, group_len), 1)
    scores = jnp.where(col_iota <= row_iota, scores, masked)
    row_max = jnp.max(scores, axis=-1, keepdims=True)
    row_sum = jnp.sum(jnp.exp(scores - row_max), axis=-1, keepdims=True)
    log_norm = row_max + jnp.log(row_sum)
    prob_full = jnp.exp(scores - log_norm)
    prob_half = prob_full.astype(jnp.bfloat16)
    attention_output = jnp.dot(prob_half, value_blk, preferred_element_type=jnp.float32).astype(jnp.bfloat16)
    prob_grad = jnp.dot(grad_blk, value_blk.T, preferred_element_type=jnp.float32)
    row_delta = jnp.sum(prob_full * prob_grad, axis=-1, keepdims=True)
    score_grad = (prob_full * (prob_grad - row_delta) * score_scale).astype(jnp.bfloat16)
    query_grad = jnp.dot(score_grad, key_blk, preferred_element_type=jnp.float32)
    key_grad = jnp.dot(score_grad.T, query_blk, preferred_element_type=jnp.float32)
    value_grad = jnp.dot(prob_half.T, grad_blk, preferred_element_type=jnp.float32)
    return query_grad, key_grad, value_grad, attention_output


def reference(rotated_query_rows, rotated_key_rows, saved_value_rows, projection_output_gradient, frozen_weight_codes, block_scale_index, block_scale_table, adapter_down_matrix, adapter_up_matrix):
    decoded_weight = dequantize(frozen_weight_codes, block_scale_index, block_scale_table)
    adapter_backward = (adapter_scale * jnp.dot(projection_output_gradient, adapter_up_matrix.T, preferred_element_type=jnp.float32)).astype(jnp.bfloat16)
    attention_gradient = (jnp.dot(projection_output_gradient, decoded_weight, preferred_element_type=jnp.float32) + jnp.dot(adapter_backward, adapter_down_matrix, preferred_element_type=jnp.float32)).astype(jnp.bfloat16)
    seq_len = rotated_query_rows.shape[0]
    head_ids = jnp.arange(ATTENTION_HEADS)
    shifted = (head_ids % HPD) >= HPD // 2

    def arrange(tensor):
        tensor = tensor.reshape(seq_len, ATTENTION_HEADS, HEAD_WIDTH)
        tensor = jnp.where(shifted[None, :, None], jnp.roll(tensor, -SHIFT, axis=0), tensor)
        tensor = tensor.reshape(seq_len // GROUP, GROUP, ATTENTION_HEADS, HEAD_WIDTH).transpose(0, 2, 1, 3)
        return tensor.reshape(-1, GROUP, HEAD_WIDTH)

    def restore(tensor):
        tensor = tensor.reshape(seq_len // GROUP, ATTENTION_HEADS, GROUP, HEAD_WIDTH).transpose(0, 2, 1, 3)
        tensor = tensor.reshape(seq_len, ATTENTION_HEADS, HEAD_WIDTH)
        tensor = jnp.where(shifted[None, :, None], jnp.roll(tensor, SHIFT, axis=0), tensor)
        return tensor.reshape(seq_len, ATTENTION_HEADS * HEAD_WIDTH)

    results = lax.map(attend_one, (arrange(rotated_query_rows), arrange(rotated_key_rows), arrange(saved_value_rows), arrange(attention_gradient)))
    query_grad = restore(results[0]).astype(jnp.bfloat16)
    key_grad = restore(results[1]).astype(jnp.bfloat16)
    value_grad = restore(results[2]).astype(jnp.bfloat16)
    attention_output = restore(results[3])
    adapter_middle = jnp.dot(attention_output, adapter_down_matrix.T, preferred_element_type=jnp.float32).astype(jnp.bfloat16)
    up_matrix_gradient = adapter_scale * jnp.dot(adapter_middle.T, projection_output_gradient, preferred_element_type=jnp.float32)
    down_matrix_gradient = jnp.dot(adapter_backward.T, attention_output, preferred_element_type=jnp.float32)
    return (query_grad, key_grad, value_grad, down_matrix_gradient, up_matrix_gradient)
```

```python
import functools

import jax
import jax.numpy as jnp
from jax import lax
from jax.experimental import pallas as pl
from jax.experimental.pallas import tpu as pltpu
from jax.sharding import PartitionSpec as P

HEAD_WIDTH = 128
HALF_GROUP_DEV = 4
LANES = 128
QUERY_BLOCK = 256

nf4_values = (
    -1.0,
    -0.6961928009986877,
    -0.5250730514526367,
    -0.39491748809814453,
    -0.28444138169288635,
    -0.18477343022823334,
    -0.09105003625154495,
    0.0,
    0.07958029955625534,
    0.16093020141124725,
    0.24611230194568634,
    0.33791524171829224,
    0.44070982933044434,
    0.5626170039176941,
    0.7229568362236023,
    1.0,
)
adapter_scale = 0.25
masked = -1e30


BF = jnp.bfloat16
F32 = jnp.float32
VM = pl.BlockSpec(memory_space=pltpu.VMEM)
SM = pl.BlockSpec(memory_space=pltpu.SMEM)


def sds(shape, dtype):
    return jax.ShapeDtypeStruct(shape, dtype)


def nt(a, b):
    return lax.dot_general(a, b, (((1,), (1,)), ((), ())), preferred_element_type=F32)


def nn(a, b):
    return jnp.dot(a, b, preferred_element_type=F32)


def call(body, outs, scratch, *args, n_scalar=0):
    return pl.pallas_call(
        body,
        out_shape=outs,
        in_specs=[SM] * n_scalar + [VM] * (len(args) - n_scalar),
        out_specs=jax.tree.map(lambda _: VM, outs),
        scratch_shapes=scratch,
    )(*args)


def dequant_body(codes_ref, index_ref, table_ref, nf4_ref, out_ref):
    rows, cols = codes_ref.shape
    per_tile = index_ref.shape[1] * LANES // cols
    width = LANES // per_tile
    lane = lax.broadcasted_iota(jnp.int32, (rows, LANES), 1)
    levels = jnp.broadcast_to(nf4_ref[...], (rows, LANES))
    parts = table_ref.shape[0]
    tables = [jnp.broadcast_to(table_ref[i : i + 1, :], (rows, LANES)) for i in range(parts)]
    for b in range(cols // LANES):
        code = codes_ref[:, b * LANES : (b + 1) * LANES]
        value = jnp.take_along_axis(levels, code, axis=1)
        idx = jnp.broadcast_to(index_ref[:, b * per_tile : b * per_tile + 1], (rows, LANES))
        for i in range(1, per_tile):
            at = b * per_tile + i
            idx = jnp.where(lane >= i * width, index_ref[:, at : at + 1], idx)
        low = idx % LANES
        scale = jnp.take_along_axis(tables[0], low, axis=1)
        for i in range(1, parts):
            scale = jnp.where(
                idx >= i * LANES, jnp.take_along_axis(tables[i], low, axis=1), scale
            )
        out_ref[:, b * LANES : (b + 1) * LANES] = (value * scale).astype(BF)


def pack_body(half, strips, blocks, pos_ref, q_ref, k_ref, v_ref, g_ref, *out_refs):
    mine = pos_ref[0]
    rows = q_ref.shape[0]
    step = g_ref.shape[1] // strips
    width = step // half
    for s in range(half):
        to = mine ^ s
        for jv in range(half):

            @pl.when(to == jv)
            def _(s=s, jv=jv):
                out = out_refs[s]
                cols = slice(jv * LANES, (jv + 1) * LANES)
                out[0] = q_ref[:, cols]
                out[1] = k_ref[:, cols]
                out[2] = v_ref[:, cols]
                pieces = [
                    g_ref[:, i * step + jv * width : i * step + (jv + 1) * width]
                    for i in range(strips)
                ]
                short = blocks * LANES - strips * width
                if short:
                    pieces.append(jnp.zeros((rows, short), BF))
                wide = jnp.concatenate(pieces, axis=1)
                for b in range(blocks):
                    out[3 + b] = wide[:, b * LANES : (b + 1) * LANES]


def assemble_body(half, blocks, pos_ref, *refs):
    pieces, (q_out, kv_out, g_out) = refs[:half], refs[half:]
    mine = pos_ref[0]
    rows = pieces[0].shape[1]
    for s in range(half):
        at = pl.ds(pl.multiple_of((mine ^ s) * rows, rows), rows)
        q_out[at, :] = pieces[s][0]
        kv_out[0, at, :] = pieces[s][1]
        kv_out[1, at, :] = pieces[s][2]
        for b in range(blocks):
            g_out[at, b * LANES : (b + 1) * LANES] = pieces[s][3 + b]


def project_body(half, planes, fsdp, slot, pos_ref, *refs):
    n_in = 2 * fsdp + planes + 1
    grads, ups = refs[:fsdp], refs[fsdp : 2 * fsdp]
    weights = refs[2 * fsdp : 2 * fsdp + planes]
    down_ref = refs[n_in - 1]
    outs, lora_ref = refs[n_in : n_in + half], refs[n_in + half]
    w_scr, acc_scr = refs[n_in + half + 1 :]
    mine, plane, core = pos_ref[0], pos_ref[1], pos_ref[2]
    rows_each = weights[0].shape[0]
    tail = w_scr.shape[0] - planes * rows_each
    if tail:
        w_scr[planes * rows_each :, :] = jnp.zeros((tail, w_scr.shape[1]), BF)
    for s in range(planes):
        src = lax.rem(plane + (planes - s), planes)
        w_scr[pl.ds(pl.multiple_of(src * rows_each, rows_each), rows_each), :] = weights[s][...]
    acc = None
    lora = None
    for s in range(fsdp):
        src = lax.rem(core + (fsdp - s), fsdp)
        depth = grads[s].shape[1]
        part = nn(grads[s][...], w_scr[pl.ds(pl.multiple_of(src * slot, 16), depth), :])
        lora_part = nt(grads[s][...], ups[s][...])
        acc = part if acc is None else acc + part
        lora = lora_part if lora is None else lora + lora_part
    lora = adapter_scale * lora
    lora_ref[...] = lora
    acc_scr[...] = acc + nn(lora.astype(BF), down_ref[...])
    for s in range(half):
        at = pl.ds(pl.multiple_of((mine ^ s) * LANES, LANES), LANES)
        outs[s][...] = acc_scr[:, at].astype(BF)


def score_block(key, query, k0, q0):
    scores = nt(key, query) * (HEAD_WIDTH**-0.5)
    if k0 is None or k0 + key.shape[0] - 1 <= q0:
        return scores
    kpos = k0 + lax.broadcasted_iota(jnp.int32, scores.shape, 0)
    qpos = q0 + lax.broadcasted_iota(jnp.int32, scores.shape, 1)
    return jnp.where(kpos <= qpos, scores, masked)


def forward_body(pos_ref, q_ref, kv_ref, far_ref, down_ref, o_ref, lse_ref, mid_ref, vt_scr, oft_scr):
    later = pos_ref[3]
    tokens = q_ref.shape[0]
    block = min(QUERY_BLOCK, tokens)
    vt_scr[...] = kv_ref[1].T

    def finish(q0, block_out, norm):
        qs = slice(q0, q0 + block)
        out = block_out.T
        o_ref[qs, :] = out
        lse_ref[:, qs] = norm
        mid_ref[qs, :] = nt(out.astype(BF), down_ref[...])

    def near(q0):
        return score_block(kv_ref[0, : q0 + block, :], q_ref[q0 : q0 + block, :], 0, q0)

    @pl.when(later == 0)
    def _():
        for q0 in range(0, tokens, block):
            scores = near(q0)
            top = jnp.max(scores, axis=0, keepdims=True)
            prob = jnp.exp(scores - top)
            total = jnp.sum(prob, axis=0, keepdims=True)
            out = nn(vt_scr[:, : q0 + block], prob.astype(BF)) / total
            finish(q0, out, top + jnp.log(total))

    @pl.when(later != 0)
    def _():
        oft_scr[...] = far_ref[1].T
        for q0 in range(0, tokens, block):
            scores = near(q0)
            far = score_block(far_ref[0], q_ref[q0 : q0 + block, :], None, q0)
            top = jnp.maximum(
                jnp.max(scores, axis=0, keepdims=True), jnp.max(far, axis=0, keepdims=True)
            )
            prob = jnp.exp(scores - top)
            far_prob = jnp.exp(far - top)
            total = jnp.sum(prob, axis=0, keepdims=True) + jnp.sum(far_prob, axis=0, keepdims=True)
            out = nn(vt_scr[:, : q0 + block], prob.astype(BF)) + nn(
                oft_scr[...], far_prob.astype(BF)
            )
            finish(q0, out / total, top + jnp.log(total))


def backward_body(half, pos_ref, *refs):
    parts = refs[:half]
    (q_ref, kv_ref, far_ref, o_ref, lse_ref) = refs[half : half + 5]
    dq_refs = refs[half + 5 : 2 * half + 5]
    near_ref, far_out = refs[2 * half + 5 : 2 * half + 7]
    do_scr, dq_scr, kt_scr, delta_scr = refs[2 * half + 7 :]
    mine, later = pos_ref[0], pos_ref[3]
    tokens = q_ref.shape[0]
    block = min(QUERY_BLOCK, tokens)
    score_scale = HEAD_WIDTH**-0.5
    total = parts[0][...].astype(F32)
    for s in range(1, half):
        total = total + parts[s][...].astype(F32)
    grad = total.astype(BF)
    do_scr[...] = grad
    delta_scr[...] = jnp.sum((grad.astype(F32) * o_ref[...]).T, axis=0, keepdims=True)
    kt_scr[...] = kv_ref[0].T

    def pair(key, value, k0, q0):
        qs = slice(q0, q0 + block)
        scores = score_block(key, q_ref[qs, :], k0, q0)
        prob = jnp.exp(scores - lse_ref[:, qs])
        prob_grad = nt(value, do_scr[qs, :])
        score_grad = (prob * (prob_grad - delta_scr[:, qs]) * score_scale).astype(BF)
        return prob.astype(BF), score_grad

    for q0 in range(0, tokens, block):
        qs = slice(q0, q0 + block)
        depth = q0 + block
        prob, score_grad = pair(kv_ref[0, :depth, :], kv_ref[1, :depth, :], 0, q0)
        dk = nn(score_grad, q_ref[qs, :])
        dv = nn(prob, do_scr[qs, :])
        if q0:
            near_ref[0, :q0, :] += dk[:q0]
            near_ref[1, :q0, :] += dv[:q0]
        near_ref[0, qs, :] = dk[q0:]
        near_ref[1, qs, :] = dv[q0:]
        dq_scr[:, qs] = nn(kt_scr[:, :depth], score_grad)

    @pl.when(later != 0)
    def _():
        kt_scr[...] = far_ref[0].T
        for k0 in range(0, tokens, block):
            ks = slice(k0, k0 + block)
            prob, score_grad = [], []
            for q0 in range(0, tokens, block):
                one = pair(far_ref[0, ks, :], far_ref[1, ks, :], None, q0)
                prob.append(one[0])
                score_grad.append(one[1])
            prob = jnp.concatenate(prob, axis=1)
            score_grad = jnp.concatenate(score_grad, axis=1)
            far_out[0, ks, :] = nn(score_grad, q_ref[...]).astype(BF)
            far_out[1, ks, :] = nn(prob, do_scr[...]).astype(BF)
            dq_scr[...] += nn(kt_scr[:, ks], score_grad)

    @pl.when(later == 0)
    def _():
        far_out[...] = jnp.zeros(far_out.shape, BF)

    do_scr[...] = dq_scr[...].T.astype(BF)
    rows = tokens // half
    for s in range(half):
        at = pl.ds(pl.multiple_of((mine ^ s) * rows, rows), rows)
        dq_refs[s][...] = do_scr[at, :]


def merge_body(half, pos_ref, near_ref, back_ref, *out_refs):
    mine = pos_ref[0]
    rows = near_ref.shape[1] // half
    for s in range(half):
        at = pl.ds(pl.multiple_of((mine ^ s) * rows, rows), rows)
        out_refs[s][...] = (near_ref[:, at, :] + back_ref[:, at, :].astype(F32)).astype(BF)


def unpack_body(half, pos_ref, *refs):
    dq, dkv = refs[:half], refs[half : 2 * half]
    q_out, k_out, v_out = refs[2 * half :]
    mine = pos_ref[0]
    for s in range(half):
        at = pl.ds(pl.multiple_of((mine ^ s) * LANES, LANES), LANES)
        q_out[:, at] = dq[s][...]
        k_out[:, at] = dkv[s][0]
        v_out[:, at] = dkv[s][1]


def adapters_body(half, o_ref, g_ref, *refs):
    both, out_ref = refs[:half], refs[half]
    rank = out_ref.shape[0]
    total = both[0][...].astype(F32)
    for s in range(1, half):
        total = total + both[s][...].astype(F32)
    total_t = total.T.astype(BF)
    wide = g_ref.shape[1]
    out_ref[:, :wide] = adapter_scale * nn(total_t[rank:, :], g_ref[...])
    out_ref[:, wide:] = nn(total_t[:rank, :], o_ref[...].astype(BF))


def on_device(
    sizes,
    rotated_query_rows,
    rotated_key_rows,
    saved_value_rows,
    projection_output_gradient,
    frozen_weight_codes,
    block_scale_index,
    block_scale_table,
    adapter_down_matrix,
    adapter_up_matrix,
):
    n_ctx, fsdp = sizes
    half = HALF_GROUP_DEV
    planes = n_ctx // half
    rows = rotated_query_rows.shape[0]
    heads = rotated_query_rows.shape[1] // HEAD_WIDTH
    assert heads == half
    tokens = rows * half
    w_rows, w_cols = frozen_weight_codes.shape
    grad_cols = projection_output_gradient.shape[1]
    strips = grad_cols // (half * w_rows)
    slot = strips * w_rows
    blocks = -(-slot // LANES)
    wide = blocks * LANES
    rank_rows = adapter_down_matrix.shape[0]
    rank = rank_rows * n_ctx

    ctx = lax.axis_index("ctx")
    core = lax.axis_index("fsdp")
    mine = ctx % half
    plane = ctx // half
    plain = mine < heads // 2
    later = jnp.where(plain, plane % 2, 1 - plane % 2)
    pos = jnp.stack([mine, plane, core, later]).astype(jnp.int32)

    def in_plane(x, s):
        if s == 0:
            return x
        return lax.ppermute(x, "ctx", [(i, i ^ s) for i in range(n_ctx)])

    def along(x, s):
        if s == 0:
            return x
        return lax.ppermute(x, "ctx", [(i, (i + s * half) % n_ctx) for i in range(n_ctx)])

    def across(x, s):
        if s == 0:
            return x
        return lax.ppermute(x, "fsdp", [(i, (i + s) % fsdp) for i in range(fsdp)])

    def earlier(i):
        p, j = divmod(i, half)
        return (p % 2 == 0) if j < heads // 2 else (p % 2 == 1)

    pairs = [(i, (i + half) % n_ctx) for i in range(n_ctx) if earlier(i)]

    levels = jnp.zeros((1, LANES), F32).at[0, : len(nf4_values)].set(jnp.array(nf4_values, F32))
    weight = call(
        dequant_body,
        sds((w_rows, w_cols), BF),
        [],
        frozen_weight_codes,
        block_scale_index,
        block_scale_table.reshape(-1, LANES),
        levels,
    )
    weights = [along(weight, s) for s in range(planes)]

    packed = call(
        functools.partial(pack_body, half, strips, blocks),
        [sds((3 + blocks, rows, LANES), BF)] * half,
        [],
        pos,
        rotated_query_rows,
        rotated_key_rows,
        saved_value_rows,
        projection_output_gradient,
        n_scalar=1,
    )
    packed = [in_plane(x, s) for s, x in enumerate(packed)]
    query, key_value, grad = call(
        functools.partial(assemble_body, half, blocks),
        [sds((tokens, LANES), BF), sds((2, tokens, LANES), BF), sds((tokens, wide), BF)],
        [],
        pos,
        *packed,
        n_scalar=1,
    )

    up_chunks = adapter_up_matrix.reshape(rank_rows, strips, half, w_rows).transpose(2, 0, 1, 3)
    up_chunks = up_chunks.reshape(half, rank_rows, slot)
    up_chunks = jnp.pad(up_chunks, ((0, 0), (0, 0), (0, wide - slot)))
    down_chunks = jnp.broadcast_to(adapter_down_matrix, (half,) + adapter_down_matrix.shape)
    chunks = jnp.concatenate([up_chunks, down_chunks], axis=2)
    chunks = jnp.broadcast_to(chunks, (planes,) + chunks.shape).reshape(n_ctx * rank_rows, -1)
    adapters = lax.all_to_all(chunks, "ctx", split_axis=0, concat_axis=0, tiled=True)
    up = adapters[:, :wide]
    down = adapters[:, wide:]

    grads = [across(grad, s) for s in range(fsdp)]
    ups = [across(up, s) for s in range(fsdp)]
    far = lax.ppermute(key_value, "ctx", pairs)
    down_head = lax.dynamic_slice_in_dim(down, mine * HEAD_WIDTH, HEAD_WIDTH, 1)

    *partial, lora = call(
        functools.partial(project_body, half, planes, fsdp, slot),
        [sds((tokens, LANES), BF)] * half + [sds((tokens, rank), F32)],
        [
            pltpu.VMEM((planes * w_rows + wide - slot, w_cols), BF),
            pltpu.VMEM((tokens, w_cols), F32),
        ],
        pos,
        *grads,
        *ups,
        *weights,
        down,
        n_scalar=1,
    )
    partial = [in_plane(x, s) for s, x in enumerate(partial)]

    out, norm, mid = call(
        forward_body,
        [sds((tokens, LANES), F32), sds((1, tokens), F32), sds((tokens, rank), F32)],
        [pltpu.VMEM((LANES, tokens), BF), pltpu.VMEM((LANES, tokens), BF)],
        pos,
        query,
        key_value,
        far,
        down_head,
        n_scalar=1,
    )
    mid = sum(across(mid, s) for s in range(fsdp))
    both = jnp.concatenate([lora, mid], axis=1).astype(BF)
    both = [in_plane(both, s) for s in range(half)]
    adapter_grads = call(
        functools.partial(adapters_body, half),
        sds((rank, wide + HEAD_WIDTH), F32),
        [],
        out,
        grad,
        *both,
    )

    *dq, near, far_part = call(
        functools.partial(backward_body, half),
        [sds((rows, LANES), BF)] * half
        + [sds((2, tokens, LANES), F32), sds((2, tokens, LANES), BF)],
        [
            pltpu.VMEM((tokens, LANES), BF),
            pltpu.VMEM((LANES, tokens), F32),
            pltpu.VMEM((LANES, tokens), BF),
            pltpu.VMEM((1, tokens), F32),
        ],
        pos,
        *partial,
        query,
        key_value,
        far,
        out,
        norm,
        n_scalar=1,
    )
    back = lax.ppermute(far_part, "ctx", [(b, a) for a, b in pairs])
    dq = [in_plane(x, s) for s, x in enumerate(dq)]

    reduced = lax.all_to_all(adapter_grads, "ctx", split_axis=0, concat_axis=0, tiled=True)
    reduced = jnp.sum(reduced.reshape(planes, half, rank_rows, -1), axis=0)
    up_grad = reduced[:, :, :slot].reshape(half, rank_rows, strips, w_rows)
    up_grad = up_grad.transpose(1, 2, 0, 3).reshape(rank_rows, grad_cols)
    down_grad = reduced[:, :, wide:].transpose(1, 0, 2).reshape(rank_rows, heads * HEAD_WIDTH)

    dkv = call(
        functools.partial(merge_body, half),
        [sds((2, rows, LANES), BF)] * half,
        [],
        pos,
        near,
        back,
        n_scalar=1,
    )
    dkv = [in_plane(x, s) for s, x in enumerate(dkv)]
    query_grad, key_grad, value_grad = call(
        functools.partial(unpack_body, half),
        [sds((rows, heads * HEAD_WIDTH), BF)] * 3,
        [],
        pos,
        *dq,
        *dkv,
        n_scalar=1,
    )
    return query_grad, key_grad, value_grad, down_grad, up_grad


def solution(mesh):
    split = P("ctx", "fsdp")
    in_specs = (split,) * 6 + (P(),) + (split,) * 2
    body = functools.partial(on_device, (mesh.shape["ctx"], mesh.shape["fsdp"]))
    return jax.shard_map(
        body, mesh=mesh, in_specs=in_specs, out_specs=(split,) * 5, check_vma=False
    )
```

```python
import functools

import jax
import jax.numpy as jnp
import numpy as np
from jax import lax
from jax.experimental import pallas as pl
from jax.experimental.pallas import tpu as pltpu
from jax.sharding import PartitionSpec as P

HEAD_WIDTH = 128
HALF_GROUP_DEV = 4
LANES = 128
QUERY_BLOCK = 256

nf4_values = (
    -1.0,
    -0.6961928009986877,
    -0.5250730514526367,
    -0.39491748809814453,
    -0.28444138169288635,
    -0.18477343022823334,
    -0.09105003625154495,
    0.0,
    0.07958029955625534,
    0.16093020141124725,
    0.24611230194568634,
    0.33791524171829224,
    0.44070982933044434,
    0.5626170039176941,
    0.7229568362236023,
    1.0,
)
adapter_scale = 0.25
masked = -1e30


BF = jnp.bfloat16
F32 = jnp.float32
VM = pl.BlockSpec(memory_space=pltpu.VMEM)
SM = pl.BlockSpec(memory_space=pltpu.SMEM)


def sds(shape, dtype):
    return jax.ShapeDtypeStruct(shape, dtype)


def nt(a, b):
    return lax.dot_general(a, b, (((1,), (1,)), ((), ())), preferred_element_type=F32)


def nn(a, b):
    return jnp.dot(a, b, preferred_element_type=F32)


def call(body, outs, scratch, *args, n_scalar=0):
    return pl.pallas_call(
        body,
        out_shape=outs,
        in_specs=[SM] * n_scalar + [VM] * (len(args) - n_scalar),
        out_specs=jax.tree.map(lambda _: VM, outs),
        scratch_shapes=scratch,
    )(*args)


def dequant_body(codes_ref, index_ref, table_ref, nf4_ref, out_ref):
    rows, cols = codes_ref.shape
    per_tile = index_ref.shape[1] * LANES // cols
    width = LANES // per_tile
    lane = lax.broadcasted_iota(jnp.int32, (rows, LANES), 1)
    levels = jnp.broadcast_to(nf4_ref[...], (rows, LANES))
    parts = table_ref.shape[0]
    tables = [jnp.broadcast_to(table_ref[i : i + 1, :], (rows, LANES)) for i in range(parts)]
    for b in range(cols // LANES):
        code = codes_ref[:, b * LANES : (b + 1) * LANES]
        value = jnp.take_along_axis(levels, code, axis=1)
        idx = jnp.broadcast_to(index_ref[:, b * per_tile : b * per_tile + 1], (rows, LANES))
        for i in range(1, per_tile):
            at = b * per_tile + i
            idx = jnp.where(lane >= i * width, index_ref[:, at : at + 1], idx)
        low = idx % LANES
        scale = jnp.take_along_axis(tables[0], low, axis=1)
        for i in range(1, parts):
            scale = jnp.where(
                idx >= i * LANES, jnp.take_along_axis(tables[i], low, axis=1), scale
            )
        out_ref[:, b * LANES : (b + 1) * LANES] = (value * scale).astype(BF)


def pack_grad_body(half, strips, pos_ref, g_ref, *out_refs):
    mine = pos_ref[0]
    rows = g_ref.shape[0]
    step = g_ref.shape[1] // strips
    width = step // half
    for s in range(half):
        to = mine ^ s
        for jv in range(half):

            @pl.when(to == jv)
            def _(s=s, jv=jv):
                pieces = [
                    g_ref[:, i * step + jv * width : i * step + (jv + 1) * width]
                    for i in range(strips)
                ]
                short = out_refs[s].shape[1] - strips * width
                if short:
                    pieces.append(jnp.zeros((rows, short), BF))
                out_refs[s][...] = jnp.concatenate(pieces, axis=1)


def pack_heads_body(half, pos_ref, q_ref, k_ref, v_ref, *out_refs):
    own = pos_ref[4]
    for s in range(half):
        cols = pl.ds(pl.multiple_of((own ^ s) * LANES, LANES), LANES)
        out_refs[s][0] = q_ref[:, cols]
        out_refs[s][1] = k_ref[:, cols]
        out_refs[s][2] = v_ref[:, cols]


def assemble_body(half, pos_ref, *refs):
    pieces, (q_out, kv_out) = refs[:half], refs[half:]
    mine = pos_ref[0]
    rows = pieces[0].shape[1]
    for s in range(half):
        at = pl.ds(pl.multiple_of((mine ^ s) * rows, rows), rows)
        q_out[at, :] = pieces[s][0]
        kv_out[0, at, :] = pieces[s][1]
        kv_out[1, at, :] = pieces[s][2]


def lora_body(half, fsdp, pos_ref, *refs):
    ups, grads, out_ref = refs[:fsdp], refs[fsdp:-1], refs[-1]
    mine = pos_ref[0]
    rows = grads[0].shape[0]
    for s in range(half):
        total = None
        for f in range(fsdp):
            part = nt(grads[s * fsdp + f][...], ups[f][...])
            total = part if total is None else total + part
        at = pl.ds(pl.multiple_of((mine ^ s) * rows, rows), rows)
        out_ref[at, :] = adapter_scale * total


def project_body(half, planes, fsdp, slot, targets, pos_ref, *refs):
    lora_ref, down_ref = refs[:2]
    grads = refs[2 : 2 + half * fsdp]
    weights = refs[2 + half * fsdp : 2 + half * fsdp + planes]
    outs = refs[2 + half * fsdp + planes : -2]
    w_scr, d_scr = refs[-2:]
    mine, plane, core, own = pos_ref[0], pos_ref[1], pos_ref[2], pos_ref[4]
    rows_each = weights[0].shape[0]
    tail = w_scr.shape[0] - planes * rows_each
    if tail:
        w_scr[planes * rows_each :, :] = jnp.zeros((tail, w_scr.shape[1]), BF)
    for i, t in enumerate(targets):
        cols = pl.ds(pl.multiple_of((own ^ t) * LANES, LANES), LANES)
        to = slice(i * LANES, (i + 1) * LANES)
        d_scr[:, to] = down_ref[:, cols]
        for s in range(planes):
            src = lax.rem(plane + (planes - s), planes)
            at = pl.ds(pl.multiple_of(src * rows_each, rows_each), rows_each)
            w_scr[at, to] = weights[s][:, cols]
    rows = grads[0].shape[0]
    depth = grads[0].shape[1]
    for s in range(half):
        at = pl.ds(pl.multiple_of((mine ^ s) * rows, rows), rows)
        acc = nn(lora_ref[at, :].astype(BF), d_scr[...])
        for f in range(fsdp):
            src = lax.rem(core + (fsdp - f), fsdp)
            w_at = pl.ds(pl.multiple_of(src * slot, 16), depth)
            acc = acc + nn(grads[s * fsdp + f][...], w_scr[w_at, :])
        for i in range(len(targets)):
            outs[i][at, :] = acc[:, i * LANES : (i + 1) * LANES].astype(BF)


def score_block(key, query, k0, q0):
    scores = nt(key, query) * (HEAD_WIDTH**-0.5)
    if k0 is None or k0 + key.shape[0] - 1 <= q0:
        return scores
    kpos = k0 + lax.broadcasted_iota(jnp.int32, scores.shape, 0)
    qpos = q0 + lax.broadcasted_iota(jnp.int32, scores.shape, 1)
    return jnp.where(kpos <= qpos, scores, masked)


def forward_body(pos_ref, q_ref, kv_ref, far_ref, down_ref, o_ref, lse_ref, mid_ref, vt_scr, oft_scr):
    later = pos_ref[3]
    tokens = q_ref.shape[0]
    block = min(QUERY_BLOCK, tokens)
    vt_scr[...] = kv_ref[1].T

    def finish(q0, block_out, norm):
        qs = slice(q0, q0 + block)
        out = block_out.T
        o_ref[qs, :] = out
        lse_ref[:, qs] = norm
        mid_ref[qs, :] = nt(out.astype(BF), down_ref[...])

    def near(q0):
        return score_block(kv_ref[0, : q0 + block, :], q_ref[q0 : q0 + block, :], 0, q0)

    @pl.when(later == 0)
    def _():
        for q0 in range(0, tokens, block):
            scores = near(q0)
            top = jnp.max(scores, axis=0, keepdims=True)
            prob = jnp.exp(scores - top)
            total = jnp.sum(prob, axis=0, keepdims=True)
            out = nn(vt_scr[:, : q0 + block], prob.astype(BF)) / total
            finish(q0, out, top + jnp.log(total))

    @pl.when(later != 0)
    def _():
        oft_scr[...] = far_ref[1].T
        for q0 in range(0, tokens, block):
            scores = near(q0)
            far = score_block(far_ref[0], q_ref[q0 : q0 + block, :], None, q0)
            top = jnp.maximum(
                jnp.max(scores, axis=0, keepdims=True), jnp.max(far, axis=0, keepdims=True)
            )
            prob = jnp.exp(scores - top)
            far_prob = jnp.exp(far - top)
            total = jnp.sum(prob, axis=0, keepdims=True) + jnp.sum(far_prob, axis=0, keepdims=True)
            out = nn(vt_scr[:, : q0 + block], prob.astype(BF)) + nn(
                oft_scr[...], far_prob.astype(BF)
            )
            finish(q0, out / total, top + jnp.log(total))


def grad_block(key, value, query, grad, norm, delta, k0, q0):
    prob = jnp.exp(score_block(key, query, k0, q0) - norm)
    prob_grad = nt(value, grad)
    score_grad = prob * (prob_grad - delta) * (HEAD_WIDTH**-0.5)
    return prob.astype(BF), score_grad.astype(BF)


def far_body(half, pos_ref, *refs):
    parts = refs[:half]
    q_ref, far_ref, o_ref, norm_ref = refs[half : half + 4]
    far_out, dq_ref, do_ref, delta_ref, kt_scr = refs[half + 4 :]
    later = pos_ref[3]
    tokens = q_ref.shape[0]
    block = min(QUERY_BLOCK, tokens)
    total = parts[0][...].astype(F32)
    for s in range(1, half):
        total = total + parts[s][...].astype(F32)
    grad = total.astype(BF)
    do_ref[...] = grad
    delta_ref[...] = jnp.sum((grad.astype(F32) * o_ref[...]).T, axis=0, keepdims=True)

    @pl.when(later != 0)
    def _():
        kt_scr[...] = far_ref[0].T
        for k0 in range(0, tokens, block):
            ks = slice(k0, k0 + block)
            prob, score_grad = grad_block(
                far_ref[0, ks, :],
                far_ref[1, ks, :],
                q_ref[...],
                do_ref[...],
                norm_ref[...],
                delta_ref[...],
                None,
                0,
            )
            far_out[0, ks, :] = nn(score_grad, q_ref[...]).astype(BF)
            far_out[1, ks, :] = nn(prob, do_ref[...]).astype(BF)
            part = nn(kt_scr[:, ks], score_grad)
            if k0:
                dq_ref[...] += part
            else:
                dq_ref[...] = part

    @pl.when(later == 0)
    def _():
        far_out[...] = jnp.zeros(far_out.shape, BF)
        dq_ref[...] = jnp.zeros(dq_ref.shape, F32)


def near_body(pos_ref, q_ref, kv_ref, do_ref, norm_ref, delta_ref, dq_in, dq_ref, near_ref, kt_scr):
    tokens = q_ref.shape[0]
    block = min(QUERY_BLOCK, tokens)
    kt_scr[...] = kv_ref[0].T
    for q0 in range(0, tokens, block):
        qs = slice(q0, q0 + block)
        depth = q0 + block
        prob, score_grad = grad_block(
            kv_ref[0, :depth, :],
            kv_ref[1, :depth, :],
            q_ref[qs, :],
            do_ref[qs, :],
            norm_ref[:, qs],
            delta_ref[:, qs],
            0,
            q0,
        )
        dk = nn(score_grad, q_ref[qs, :])
        dv = nn(prob, do_ref[qs, :])
        if q0:
            near_ref[0, :q0, :] += dk[:q0]
            near_ref[1, :q0, :] += dv[:q0]
        near_ref[0, qs, :] = dk[q0:]
        near_ref[1, qs, :] = dv[q0:]
        dq = dq_in[:, qs] + nn(kt_scr[:, :depth], score_grad)
        dq_ref[qs, :] = dq.T.astype(BF)


def merge_body(half, pos_ref, dq_ref, near_ref, back_ref, *out_refs):
    mine = pos_ref[0]
    rows = near_ref.shape[1] // half
    for s in range(half):
        at = pl.ds(pl.multiple_of((mine ^ s) * rows, rows), rows)
        out_refs[s][0] = dq_ref[at, :]
        for i in range(2):
            merged = near_ref[i, at, :] + back_ref[i, at, :].astype(F32)
            out_refs[s][1 + i] = merged.astype(BF)


def unpack_body(half, pos_ref, *refs):
    pieces, outs = refs[:half], refs[half:]
    own = pos_ref[4]
    for s in range(half):
        at = pl.ds(pl.multiple_of((own ^ s) * LANES, LANES), LANES)
        for i in range(3):
            outs[i][:, at] = pieces[s][i]


def adapters_body(half, pos_ref, o_ref, *refs):
    both, grads, out_ref, scr = refs[:half], refs[half : 2 * half], refs[-2], refs[-1]
    mine = pos_ref[0]
    rank = out_ref.shape[0]
    rows, wide = grads[0].shape
    total = both[0][...].astype(F32)
    for s in range(1, half):
        total = total + both[s][...].astype(F32)
    total = total.astype(BF)
    scr[...] = total
    acc = None
    for s in range(half):
        at = pl.ds(pl.multiple_of((mine ^ s) * rows, rows), rows)
        part = nn(scr[at, :].T[rank:, :], grads[s][...])
        acc = part if acc is None else acc + part
    out_ref[:, :wide] = adapter_scale * acc
    out_ref[:, wide:] = nn(total.T[:rank, :], o_ref[...].astype(BF))


def on_device(
    sizes,
    rotated_query_rows,
    rotated_key_rows,
    saved_value_rows,
    projection_output_gradient,
    frozen_weight_codes,
    block_scale_index,
    block_scale_table,
    adapter_down_matrix,
    adapter_up_matrix,
):
    n_ctx, fsdp = sizes
    half = HALF_GROUP_DEV
    planes = n_ctx // half
    rows = rotated_query_rows.shape[0]
    heads = rotated_query_rows.shape[1] // HEAD_WIDTH
    assert heads == half
    tokens = rows * half
    w_rows, w_cols = frozen_weight_codes.shape
    grad_cols = projection_output_gradient.shape[1]
    strips = grad_cols // (half * w_rows)
    slot = strips * w_rows
    wide = -(-slot // LANES) * LANES
    rank_rows = adapter_down_matrix.shape[0]
    rank = rank_rows * n_ctx

    def head_of(j, f):
        return j ^ ((f & 1) * (half // 2))

    ctx = lax.axis_index("ctx")
    core = lax.axis_index("fsdp")
    mine = ctx % half
    plane = ctx // half
    own = head_of(mine, core)
    later = jnp.where(own < heads // 2, plane % 2, 1 - plane % 2)
    pos = jnp.stack([mine, plane, core, later, own]).astype(jnp.int32)

    def in_plane(x, s):
        if s == 0:
            return x
        return lax.ppermute(x, "ctx", [(i, i ^ s) for i in range(n_ctx)])

    def along(x, s):
        if s == 0:
            return x
        return lax.ppermute(x, "ctx", [(i, (i + s * half) % n_ctx) for i in range(n_ctx)])

    def across(x, s):
        if s == 0:
            return x
        return lax.ppermute(x, "fsdp", [(i, (i + s) % fsdp) for i in range(fsdp)])

    pairs = []
    for i in range(n_ctx):
        for f in range(fsdp):
            p, j = divmod(i, half)
            if (p % 2 == 0) == (head_of(j, f) < heads // 2):
                pairs.append((i * fsdp + f, (i + half) % n_ctx * fsdp + f))

    def to_later(x):
        return lax.ppermute(x, ("ctx", "fsdp"), pairs)

    def to_earlier(x):
        return lax.ppermute(x, ("ctx", "fsdp"), [(b, a) for a, b in pairs])

    levels = np.zeros((1, LANES), np.float32)
    levels[0, : len(nf4_values)] = nf4_values
    weight = call(
        dequant_body,
        sds((w_rows, w_cols), BF),
        [],
        frozen_weight_codes,
        block_scale_index,
        block_scale_table.reshape(-1, LANES),
        jnp.asarray(levels),
    )
    weights = [along(weight, s) for s in range(planes)]

    grads = call(
        functools.partial(pack_grad_body, half, strips),
        [sds((rows, wide), BF)] * half,
        [],
        pos,
        projection_output_gradient,
        n_scalar=1,
    )
    grads = [in_plane(x, s) for s, x in enumerate(grads)]
    swapped = [across(g, f) for g in grads for f in range(fsdp)]

    packed = call(
        functools.partial(pack_heads_body, half),
        [sds((3, rows, LANES), BF)] * half,
        [],
        pos,
        rotated_query_rows,
        rotated_key_rows,
        saved_value_rows,
        n_scalar=1,
    )
    packed = [in_plane(x, s) for s, x in enumerate(packed)]
    query, key_value = call(
        functools.partial(assemble_body, half),
        [sds((tokens, LANES), BF), sds((2, tokens, LANES), BF)],
        [],
        pos,
        *packed,
        n_scalar=1,
    )
    far = to_later(key_value)

    up_chunks = adapter_up_matrix.reshape(rank_rows, strips, half, w_rows).transpose(2, 0, 1, 3)
    up_chunks = up_chunks.reshape(half, rank_rows, slot)
    up_chunks = jnp.pad(up_chunks, ((0, 0), (0, 0), (0, wide - slot)))
    down_chunks = jnp.broadcast_to(adapter_down_matrix, (half,) + adapter_down_matrix.shape)
    chunks = jnp.concatenate([up_chunks, down_chunks], axis=2)
    chunks = jnp.broadcast_to(chunks, (planes,) + chunks.shape).reshape(n_ctx * rank_rows, -1)
    adapters = lax.all_to_all(chunks, "ctx", split_axis=0, concat_axis=0, tiled=True)
    up = adapters[:, :wide]
    down = adapters[:, wide:]
    down_head = lax.dynamic_slice_in_dim(down, own * HEAD_WIDTH, HEAD_WIDTH, 1)
    ups = [across(up, f) for f in range(fsdp)]
    lora = call(
        functools.partial(lora_body, half, fsdp),
        sds((tokens, rank), F32),
        [],
        pos,
        *ups,
        *swapped,
        n_scalar=1,
    )

    def project(targets):
        return call(
            functools.partial(project_body, half, planes, fsdp, slot, targets),
            [sds((tokens, LANES), BF)] * len(targets),
            [
                pltpu.VMEM((planes * w_rows + wide - slot, LANES * len(targets)), BF),
                pltpu.VMEM((rank, LANES * len(targets)), BF),
            ],
            pos,
            lora,
            down,
            *swapped,
            *weights,
            n_scalar=1,
        )

    first, second = range(half // 2, half), range(half // 2)
    partial = dict(zip(first, project(tuple(first))))
    partial = {s: in_plane(x, s) for s, x in partial.items()}
    rest = dict(zip(second, project(tuple(second))))
    partial.update({s: in_plane(x, s) for s, x in rest.items()})

    out, norm, mid = call(
        forward_body,
        [sds((tokens, LANES), F32), sds((1, tokens), F32), sds((tokens, rank), F32)],
        [pltpu.VMEM((LANES, tokens), BF), pltpu.VMEM((LANES, tokens), BF)],
        pos,
        query,
        key_value,
        far,
        down_head,
        n_scalar=1,
    )
    mid = sum(across(mid, f) for f in range(fsdp))
    both = jnp.concatenate([lora, mid], axis=1).astype(BF)
    both = [in_plane(both, s) for s in range(half)]
    adapter_grads = call(
        functools.partial(adapters_body, half),
        sds((rank, wide + HEAD_WIDTH), F32),
        [pltpu.VMEM((tokens, 2 * rank), BF)],
        pos,
        out,
        *both,
        *grads,
        n_scalar=1,
    )
    reduced = lax.all_to_all(adapter_grads, "ctx", split_axis=0, concat_axis=0, tiled=True)
    reduced = jnp.sum(reduced.reshape(planes, half, rank_rows, -1), axis=0)
    up_grad = reduced[:, :, :slot].reshape(half, rank_rows, strips, w_rows)
    up_grad = up_grad.transpose(1, 2, 0, 3).reshape(rank_rows, grad_cols)
    down_grad = reduced[:, :, wide:]
    down_grad = jnp.where(core % 2 == 0, down_grad, jnp.roll(down_grad, half // 2, axis=0))
    down_grad = down_grad.transpose(1, 0, 2).reshape(rank_rows, heads * HEAD_WIDTH)

    far_part, dq_far, grad_out, delta = call(
        functools.partial(far_body, half),
        [
            sds((2, tokens, LANES), BF),
            sds((LANES, tokens), F32),
            sds((tokens, LANES), BF),
            sds((1, tokens), F32),
        ],
        [pltpu.VMEM((LANES, tokens), BF)],
        pos,
        *[partial[s] for s in range(half)],
        query,
        far,
        out,
        norm,
        n_scalar=1,
    )
    back = to_earlier(far_part)
    dq, near = call(
        near_body,
        [sds((tokens, LANES), BF), sds((2, tokens, LANES), F32)],
        [pltpu.VMEM((LANES, tokens), BF)],
        pos,
        query,
        key_value,
        grad_out,
        norm,
        delta,
        dq_far,
        n_scalar=1,
    )
    merged = call(
        functools.partial(merge_body, half),
        [sds((3, rows, LANES), BF)] * half,
        [],
        pos,
        dq,
        near,
        back,
        n_scalar=1,
    )
    merged = [in_plane(x, s) for s, x in enumerate(merged)]
    query_grad, key_grad, value_grad = call(
        functools.partial(unpack_body, half),
        [sds((rows, heads * HEAD_WIDTH), BF)] * 3,
        [],
        pos,
        *merged,
        n_scalar=1,
    )
    return query_grad, key_grad, value_grad, down_grad, up_grad


def solution(mesh):
    split = P("ctx", "fsdp")
    in_specs = (split,) * 6 + (P(),) + (split,) * 2

    def body(*args):
        return on_device((mesh.shape["ctx"], mesh.shape["fsdp"]), *args)

    return jax.shard_map(
        body, mesh=mesh, in_specs=in_specs, out_specs=(split,) * 5, check_vma=False
    )
```

```python
import functools

import jax
import jax.numpy as jnp
import numpy as np
from jax import lax
from jax.experimental import pallas as pl
from jax.experimental.pallas import tpu as pltpu
from jax.sharding import PartitionSpec as P

HEAD_WIDTH = 128
HALF_GROUP_DEV = 4
LANES = 128
QUERY_BLOCK = 256
KERNEL_VMEM = 16 << 20

nf4_values = (
    -1.0,
    -0.6961928009986877,
    -0.5250730514526367,
    -0.39491748809814453,
    -0.28444138169288635,
    -0.18477343022823334,
    -0.09105003625154495,
    0.0,
    0.07958029955625534,
    0.16093020141124725,
    0.24611230194568634,
    0.33791524171829224,
    0.44070982933044434,
    0.5626170039176941,
    0.7229568362236023,
    1.0,
)
adapter_scale = 0.25
masked = -1e30


BF = jnp.bfloat16
F32 = jnp.float32
VM = pl.BlockSpec(memory_space=pltpu.VMEM)
SM = pl.BlockSpec(memory_space=pltpu.SMEM)


def sds(shape, dtype):
    return jax.ShapeDtypeStruct(shape, dtype)


def nt(a, b):
    return lax.dot_general(a, b, (((1,), (1,)), ((), ())), preferred_element_type=F32)


def nn(a, b):
    return jnp.dot(a, b, preferred_element_type=F32)


def call(body, outs, scratch, *args, n_scalar=0):
    return pl.pallas_call(
        body,
        out_shape=outs,
        in_specs=[SM] * n_scalar + [VM] * (len(args) - n_scalar),
        out_specs=jax.tree.map(lambda _: VM, outs),
        scratch_shapes=scratch,
        compiler_params=pltpu.CompilerParams(vmem_limit_bytes=KERNEL_VMEM),
    )(*args)


def dequant_body(codes_ref, index_ref, table_ref, nf4_ref, out_ref):
    rows, cols = codes_ref.shape
    groups = index_ref.shape[0]
    parts = table_ref.shape[0]
    per_tile = groups * LANES // cols
    width = LANES // per_tile
    tables = [jnp.broadcast_to(table_ref[i : i + 1, :], (groups, LANES)) for i in range(parts)]
    scales = []
    for r0 in range(0, rows, LANES):
        idx = index_ref[:, r0 : min(r0 + LANES, rows)]
        short = LANES - idx.shape[1]
        if short:
            idx = jnp.concatenate([idx, jnp.zeros((groups, short), jnp.int32)], axis=1)
        low = idx % LANES
        scale = jnp.take_along_axis(tables[0], low, axis=1)
        for i in range(1, parts):
            scale = jnp.where(
                idx >= i * LANES, jnp.take_along_axis(tables[i], low, axis=1), scale
            )
        scales.append(scale)
    scales = jnp.concatenate(scales, axis=1).T[:rows, :]
    lane = lax.broadcasted_iota(jnp.int32, (rows, LANES), 1)
    levels = jnp.broadcast_to(nf4_ref[...], (rows, LANES))
    for b in range(cols // LANES):
        code = codes_ref[:, b * LANES : (b + 1) * LANES]
        value = jnp.take_along_axis(levels, code, axis=1)
        at = b * per_tile
        scale = jnp.broadcast_to(scales[:, at : at + 1], (rows, LANES))
        for i in range(1, per_tile):
            scale = jnp.where(lane >= i * width, scales[:, at + i : at + i + 1], scale)
        out_ref[:, b * LANES : (b + 1) * LANES] = (value * scale).astype(BF)


def adapter_chunks_body(half, strips, wide, up_ref, down_ref, out_ref):
    count, rank_rows = out_ref.shape[:2]
    step = up_ref.shape[1] // strips
    width = step // half
    short = wide - strips * width
    for j in range(half):
        pieces = [
            up_ref[:, i * step + j * width : i * step + (j + 1) * width] for i in range(strips)
        ]
        if short:
            pieces.append(jnp.zeros((rank_rows, short), BF))
        chunk = jnp.concatenate(pieces, axis=1)
        for p in range(count // half):
            out_ref[p * half + j, :, :wide] = chunk
            out_ref[p * half + j, :, wide:] = down_ref[...]


def adapter_grads_body(half, strips, slot, wide, pos_ref, in_ref, up_ref, down_ref):
    core = pos_ref[2]
    planes = in_ref.shape[0] // half
    width = slot // strips
    step = half * width
    for j in range(half):
        total = in_ref[j]
        for p in range(1, planes):
            total = total + in_ref[p * half + j]
        for i in range(strips):
            to = i * step + j * width
            up_ref[:, to : to + width] = total[:, i * width : (i + 1) * width]
        head = j ^ ((core & 1) * (half // 2))
        down_ref[:, pl.ds(pl.multiple_of(head * LANES, LANES), LANES)] = total[:, wide:]


def pack_grad_body(half, strips, pos_ref, g_ref, *out_refs):
    mine = pos_ref[0]
    rows = g_ref.shape[0]
    step = g_ref.shape[1] // strips
    width = step // half
    for s in range(half):
        to = mine ^ s
        for jv in range(half):

            @pl.when(to == jv)
            def _(s=s, jv=jv):
                pieces = [
                    g_ref[:, i * step + jv * width : i * step + (jv + 1) * width]
                    for i in range(strips)
                ]
                short = out_refs[s].shape[1] - strips * width
                if short:
                    pieces.append(jnp.zeros((rows, short), BF))
                out_refs[s][...] = jnp.concatenate(pieces, axis=1)


def pack_heads_body(half, pos_ref, q_ref, k_ref, v_ref, *out_refs):
    own = pos_ref[4]
    for s in range(half):
        cols = pl.ds(pl.multiple_of((own ^ s) * LANES, LANES), LANES)
        out_refs[s][0] = q_ref[:, cols]
        out_refs[s][1] = k_ref[:, cols]
        out_refs[s][2] = v_ref[:, cols]


def assemble_body(half, pos_ref, *refs):
    pieces, (q_out, kv_out) = refs[:half], refs[half:]
    mine = pos_ref[0]
    rows = pieces[0].shape[1]
    for s in range(half):
        at = pl.ds(pl.multiple_of((mine ^ s) * rows, rows), rows)
        q_out[at, :] = pieces[s][0]
        kv_out[0, at, :] = pieces[s][1]
        kv_out[1, at, :] = pieces[s][2]


def lora_body(half, fsdp, pos_ref, *refs):
    ups, grads, out_ref = refs[:fsdp], refs[fsdp:-1], refs[-1]
    mine = pos_ref[0]
    rows, wide = grads[0].shape
    for s in range(half):
        total = None
        for f in range(fsdp):
            part = nt(grads[s * fsdp + f][...], ups[f][:, :wide])
            total = part if total is None else total + part
        at = pl.ds(pl.multiple_of((mine ^ s) * rows, rows), rows)
        out_ref[at, :] = adapter_scale * total


def join_body(lora_ref, *refs):
    mids, out_ref = refs[:-1], refs[-1]
    mid = mids[0][...]
    for m in mids[1:]:
        mid = mid + m[...]
    out_ref[...] = jnp.concatenate([lora_ref[...], mid], axis=1).astype(BF)


def project_body(half, planes, fsdp, slot, targets, pos_ref, *refs):
    ups = refs[:fsdp]
    grads = refs[fsdp : fsdp + half * fsdp]
    weights = refs[fsdp + half * fsdp : fsdp + half * fsdp + planes]
    outs = refs[fsdp + half * fsdp + planes : -2]
    w_scr, d_scr = refs[-2:]
    mine, plane, core, own = pos_ref[0], pos_ref[1], pos_ref[2], pos_ref[4]
    rows_each = weights[0].shape[0]
    rows, wide = grads[0].shape
    tail = w_scr.shape[0] - planes * rows_each
    if tail:
        w_scr[planes * rows_each :, :] = jnp.zeros((tail, w_scr.shape[1]), BF)
    for i, t in enumerate(targets):
        cols = pl.ds(pl.multiple_of((own ^ t) * LANES, LANES), LANES)
        d_cols = pl.ds(pl.multiple_of(wide + (own ^ t) * LANES, LANES), LANES)
        to = slice(i * LANES, (i + 1) * LANES)
        d_scr[:, to] = ups[0][:, d_cols]
        for s in range(planes):
            src = lax.rem(plane + (planes - s), planes)
            at = pl.ds(pl.multiple_of(src * rows_each, rows_each), rows_each)
            w_scr[at, to] = weights[s][:, cols]
    for f in range(fsdp):
        src = lax.rem(core + (fsdp - f), fsdp)
        at = pl.ds(pl.multiple_of(src * slot, 16), slot)
        low = lax.dot_general(
            ups[f][:, :wide], d_scr[...], (((0,), (0,)), ((), ())), preferred_element_type=F32
        )
        w_scr[at, :] = (w_scr[at, :].astype(F32) + adapter_scale * low[:slot]).astype(BF)
    for s in range(half):
        at = pl.ds(pl.multiple_of((mine ^ s) * rows, rows), rows)
        acc = None
        for f in range(fsdp):
            src = lax.rem(core + (fsdp - f), fsdp)
            w_at = pl.ds(pl.multiple_of(src * slot, 16), wide)
            part = nn(grads[s * fsdp + f][...], w_scr[w_at, :])
            acc = part if acc is None else acc + part
        for i in range(len(targets)):
            outs[i][at, :] = acc[:, i * LANES : (i + 1) * LANES].astype(BF)


def score_block(key, query, k0, q0):
    scores = nt(key, query) * (HEAD_WIDTH**-0.5)
    if k0 is None or k0 + key.shape[0] - 1 <= q0:
        return scores
    kpos = k0 + lax.broadcasted_iota(jnp.int32, scores.shape, 0)
    qpos = q0 + lax.broadcasted_iota(jnp.int32, scores.shape, 1)
    return jnp.where(kpos <= qpos, scores, masked)


def forward_body(
    wide, pos_ref, q_ref, kv_ref, far_ref, adapt_ref, o_ref, lse_ref, mid_ref, vt_scr, oft_scr
):
    later, own = pos_ref[3], pos_ref[4]
    down = adapt_ref[:, pl.ds(pl.multiple_of(wide + own * LANES, LANES), LANES)]
    tokens = q_ref.shape[0]
    block = min(QUERY_BLOCK, tokens)
    vt_scr[...] = kv_ref[1].T

    def finish(q0, block_out, norm):
        qs = slice(q0, q0 + block)
        out = block_out.T
        o_ref[qs, :] = out
        lse_ref[:, qs] = norm
        mid_ref[qs, :] = nt(out.astype(BF), down)

    def near(q0):
        return score_block(kv_ref[0, : q0 + block, :], q_ref[q0 : q0 + block, :], 0, q0)

    @pl.when(later == 0)
    def _():
        for q0 in range(0, tokens, block):
            scores = near(q0)
            top = jnp.max(scores, axis=0, keepdims=True)
            prob = jnp.exp(scores - top)
            total = jnp.sum(prob, axis=0, keepdims=True)
            out = nn(vt_scr[:, : q0 + block], prob.astype(BF)) / total
            finish(q0, out, top + jnp.log(total))

    @pl.when(later != 0)
    def _():
        oft_scr[...] = far_ref[1].T
        for q0 in range(0, tokens, block):
            scores = near(q0)
            far = score_block(far_ref[0], q_ref[q0 : q0 + block, :], None, q0)
            top = jnp.maximum(
                jnp.max(scores, axis=0, keepdims=True), jnp.max(far, axis=0, keepdims=True)
            )
            prob = jnp.exp(scores - top)
            far_prob = jnp.exp(far - top)
            total = jnp.sum(prob, axis=0, keepdims=True) + jnp.sum(far_prob, axis=0, keepdims=True)
            out = nn(vt_scr[:, : q0 + block], prob.astype(BF)) + nn(
                oft_scr[...], far_prob.astype(BF)
            )
            finish(q0, out / total, top + jnp.log(total))


def grad_block(key, value, query, grad, norm, delta, k0, q0):
    prob = jnp.exp(score_block(key, query, k0, q0) - norm)
    prob_grad = nt(value, grad)
    score_grad = prob * (prob_grad - delta) * (HEAD_WIDTH**-0.5)
    return prob.astype(BF), score_grad.astype(BF)


def far_body(half, pos_ref, *refs):
    parts = refs[:half]
    q_ref, far_ref, o_ref, norm_ref = refs[half : half + 4]
    far_out, dq_ref, do_ref, delta_ref, kt_scr = refs[half + 4 :]
    later = pos_ref[3]
    tokens = q_ref.shape[0]
    block = min(QUERY_BLOCK, tokens)
    total = parts[0][...].astype(F32)
    for s in range(1, half):
        total = total + parts[s][...].astype(F32)
    grad = total.astype(BF)
    do_ref[...] = grad
    delta_ref[...] = jnp.sum((grad.astype(F32) * o_ref[...]).T, axis=0, keepdims=True)

    @pl.when(later != 0)
    def _():
        kt_scr[...] = far_ref[0].T
        for k0 in range(0, tokens, block):
            ks = slice(k0, k0 + block)
            prob, score_grad = grad_block(
                far_ref[0, ks, :],
                far_ref[1, ks, :],
                q_ref[...],
                do_ref[...],
                norm_ref[...],
                delta_ref[...],
                None,
                0,
            )
            far_out[0, ks, :] = nn(score_grad, q_ref[...]).astype(BF)
            far_out[1, ks, :] = nn(prob, do_ref[...]).astype(BF)
            part = nn(kt_scr[:, ks], score_grad)
            if k0:
                dq_ref[...] += part
            else:
                dq_ref[...] = part

    @pl.when(later == 0)
    def _():
        far_out[...] = jnp.zeros(far_out.shape, BF)
        dq_ref[...] = jnp.zeros(dq_ref.shape, F32)


def near_body(pos_ref, q_ref, kv_ref, do_ref, norm_ref, delta_ref, dq_in, dq_ref, near_ref, kt_scr):
    tokens = q_ref.shape[0]
    block = min(QUERY_BLOCK, tokens)
    kt_scr[...] = kv_ref[0].T
    for q0 in range(0, tokens, block):
        qs = slice(q0, q0 + block)
        depth = q0 + block
        prob, score_grad = grad_block(
            kv_ref[0, :depth, :],
            kv_ref[1, :depth, :],
            q_ref[qs, :],
            do_ref[qs, :],
            norm_ref[:, qs],
            delta_ref[:, qs],
            0,
            q0,
        )
        dk = nn(score_grad, q_ref[qs, :])
        dv = nn(prob, do_ref[qs, :])
        if q0:
            near_ref[0, :q0, :] += dk[:q0]
            near_ref[1, :q0, :] += dv[:q0]
        near_ref[0, qs, :] = dk[q0:]
        near_ref[1, qs, :] = dv[q0:]
        dq = dq_in[:, qs] + nn(kt_scr[:, :depth], score_grad)
        dq_ref[qs, :] = dq.T.astype(BF)


def merge_body(half, pos_ref, dq_ref, near_ref, back_ref, *out_refs):
    mine = pos_ref[0]
    rows = near_ref.shape[1] // half
    for s in range(half):
        at = pl.ds(pl.multiple_of((mine ^ s) * rows, rows), rows)
        out_refs[s][0] = dq_ref[at, :]
        for i in range(2):
            merged = near_ref[i, at, :] + back_ref[i, at, :].astype(F32)
            out_refs[s][1 + i] = merged.astype(BF)


def unpack_body(half, pos_ref, *refs):
    pieces, outs = refs[:half], refs[half:]
    own = pos_ref[4]
    for s in range(half):
        at = pl.ds(pl.multiple_of((own ^ s) * LANES, LANES), LANES)
        for i in range(3):
            outs[i][:, at] = pieces[s][i]


def adapters_body(half, pos_ref, o_ref, *refs):
    both, grads, out_ref, scr = refs[:half], refs[half : 2 * half], refs[-2], refs[-1]
    mine = pos_ref[0]
    count, rank_rows = out_ref.shape[:2]
    rank = count * rank_rows
    rows, wide = grads[0].shape
    total = both[0][...].astype(F32)
    for s in range(1, half):
        total = total + both[s][...].astype(F32)
    total = total.astype(BF)
    scr[...] = total
    acc = None
    for s in range(half):
        at = pl.ds(pl.multiple_of((mine ^ s) * rows, rows), rows)
        part = nn(scr[at, :].T[rank:, :], grads[s][...])
        acc = part if acc is None else acc + part
    acc = adapter_scale * acc
    low = nn(total.T[:rank, :], o_ref[...].astype(BF))
    for c in range(count):
        out_ref[c, :, :wide] = acc[c * rank_rows : (c + 1) * rank_rows, :]
        out_ref[c, :, wide:] = low[c * rank_rows : (c + 1) * rank_rows, :]


def on_device(
    sizes,
    rotated_query_rows,
    rotated_key_rows,
    saved_value_rows,
    projection_output_gradient,
    frozen_weight_codes,
    block_scale_index,
    block_scale_table,
    adapter_down_matrix,
    adapter_up_matrix,
):
    n_ctx, fsdp = sizes
    half = HALF_GROUP_DEV
    planes = n_ctx // half
    rows = rotated_query_rows.shape[0]
    heads = rotated_query_rows.shape[1] // HEAD_WIDTH
    assert heads == half
    tokens = rows * half
    w_rows, w_cols = frozen_weight_codes.shape
    grad_cols = projection_output_gradient.shape[1]
    strips = grad_cols // (half * w_rows)
    slot = strips * w_rows
    wide = -(-slot // LANES) * LANES
    rank_rows = adapter_down_matrix.shape[0]
    rank = rank_rows * n_ctx

    def head_of(j, f):
        return j ^ ((f & 1) * (half // 2))

    ctx = lax.axis_index("ctx")
    core = lax.axis_index("fsdp")
    mine = ctx % half
    plane = ctx // half
    own = head_of(mine, core)
    later = jnp.where(own < heads // 2, plane % 2, 1 - plane % 2)
    pos = jnp.stack([mine, plane, core, later, own]).astype(jnp.int32)

    def in_plane(x, s):
        if s == 0:
            return x
        return lax.ppermute(x, "ctx", [(i, i ^ s) for i in range(n_ctx)])

    def along(x, s):
        if s == 0:
            return x
        return lax.ppermute(x, "ctx", [(i, (i + s * half) % n_ctx) for i in range(n_ctx)])

    def across(x, s):
        if s == 0:
            return x
        return lax.ppermute(x, "fsdp", [(i, (i + s) % fsdp) for i in range(fsdp)])

    pairs = []
    for i in range(n_ctx):
        for f in range(fsdp):
            p, j = divmod(i, half)
            if (p % 2 == 0) == (head_of(j, f) < heads // 2):
                pairs.append((i * fsdp + f, (i + half) % n_ctx * fsdp + f))

    def to_later(x):
        return lax.ppermute(x, ("ctx", "fsdp"), pairs)

    def to_earlier(x):
        return lax.ppermute(x, ("ctx", "fsdp"), [(b, a) for a, b in pairs])

    levels = np.zeros((1, LANES), np.float32)
    levels[0, : len(nf4_values)] = nf4_values
    weight = call(
        dequant_body,
        sds((w_rows, w_cols), BF),
        [],
        frozen_weight_codes,
        block_scale_index.T,
        block_scale_table.reshape(-1, LANES),
        jnp.asarray(levels),
    )
    weights = [along(weight, s) for s in range(planes)]

    grads = call(
        functools.partial(pack_grad_body, half, strips),
        [sds((rows, wide), BF)] * half,
        [],
        pos,
        projection_output_gradient,
        n_scalar=1,
    )
    grads = [in_plane(x, s) for s, x in enumerate(grads)]
    swapped = [across(g, f) for g in grads for f in range(fsdp)]

    packed = call(
        functools.partial(pack_heads_body, half),
        [sds((3, rows, LANES), BF)] * half,
        [],
        pos,
        rotated_query_rows,
        rotated_key_rows,
        saved_value_rows,
        n_scalar=1,
    )
    packed = [in_plane(x, s) for s, x in enumerate(packed)]
    query, key_value = call(
        functools.partial(assemble_body, half),
        [sds((tokens, LANES), BF), sds((2, tokens, LANES), BF)],
        [],
        pos,
        *packed,
        n_scalar=1,
    )
    far = to_later(key_value)

    chunks = call(
        functools.partial(adapter_chunks_body, half, strips, wide),
        sds((n_ctx, rank_rows, wide + heads * HEAD_WIDTH), BF),
        [],
        adapter_up_matrix,
        adapter_down_matrix,
    )
    adapters = lax.all_to_all(chunks, "ctx", split_axis=0, concat_axis=0, tiled=True)
    adapters = adapters.reshape(rank, -1)
    ups = [across(adapters, f) for f in range(fsdp)]
    lora = call(
        functools.partial(lora_body, half, fsdp),
        sds((tokens, rank), F32),
        [],
        pos,
        *ups,
        *swapped,
        n_scalar=1,
    )

    def project(targets):
        return call(
            functools.partial(project_body, half, planes, fsdp, slot, targets),
            [sds((tokens, LANES), BF)] * len(targets),
            [
                pltpu.VMEM((planes * w_rows + wide - slot, LANES * len(targets)), BF),
                pltpu.VMEM((rank, LANES * len(targets)), BF),
            ],
            pos,
            *ups,
            *swapped,
            *weights,
            n_scalar=1,
        )

    first, second = range(half // 2, half), range(half // 2)
    partial = dict(zip(first, project(tuple(first))))
    partial = {s: in_plane(x, s) for s, x in partial.items()}
    rest = dict(zip(second, project(tuple(second))))
    partial.update({s: in_plane(x, s) for s, x in rest.items()})

    out, norm, mid = call(
        functools.partial(forward_body, wide),
        [sds((tokens, LANES), F32), sds((1, tokens), F32), sds((tokens, rank), F32)],
        [pltpu.VMEM((LANES, tokens), BF), pltpu.VMEM((LANES, tokens), BF)],
        pos,
        query,
        key_value,
        far,
        adapters,
        n_scalar=1,
    )
    mids = [across(mid, f) for f in range(fsdp)]
    both = call(join_body, sds((tokens, 2 * rank), BF), [], lora, *mids)
    both = [in_plane(both, s) for s in range(half)]
    adapter_grads = call(
        functools.partial(adapters_body, half),
        sds((n_ctx, rank_rows, wide + HEAD_WIDTH), F32),
        [pltpu.VMEM((tokens, 2 * rank), BF)],
        pos,
        out,
        *both,
        *grads,
        n_scalar=1,
    )
    reduced = lax.all_to_all(adapter_grads, "ctx", split_axis=0, concat_axis=0, tiled=True)
    up_grad, down_grad = call(
        functools.partial(adapter_grads_body, half, strips, slot, wide),
        [sds((rank_rows, grad_cols), F32), sds((rank_rows, heads * HEAD_WIDTH), F32)],
        [],
        pos,
        reduced,
        n_scalar=1,
    )

    far_part, dq_far, grad_out, delta = call(
        functools.partial(far_body, half),
        [
            sds((2, tokens, LANES), BF),
            sds((LANES, tokens), F32),
            sds((tokens, LANES), BF),
            sds((1, tokens), F32),
        ],
        [pltpu.VMEM((LANES, tokens), BF)],
        pos,
        *[partial[s] for s in range(half)],
        query,
        far,
        out,
        norm,
        n_scalar=1,
    )
    back = to_earlier(far_part)
    dq, near = call(
        near_body,
        [sds((tokens, LANES), BF), sds((2, tokens, LANES), F32)],
        [pltpu.VMEM((LANES, tokens), BF)],
        pos,
        query,
        key_value,
        grad_out,
        norm,
        delta,
        dq_far,
        n_scalar=1,
    )
    merged = call(
        functools.partial(merge_body, half),
        [sds((3, rows, LANES), BF)] * half,
        [],
        pos,
        dq,
        near,
        back,
        n_scalar=1,
    )
    merged = [in_plane(x, s) for s, x in enumerate(merged)]
    query_grad, key_grad, value_grad = call(
        functools.partial(unpack_body, half),
        [sds((rows, heads * HEAD_WIDTH), BF)] * 3,
        [],
        pos,
        *merged,
        n_scalar=1,
    )
    return query_grad, key_grad, value_grad, down_grad, up_grad


def solution(mesh):
    split = P("ctx", "fsdp")
    in_specs = (split,) * 6 + (P(),) + (split,) * 2

    def body(*args):
        return on_device((mesh.shape["ctx"], mesh.shape["fsdp"]), *args)

    return jax.shard_map(
        body, mesh=mesh, in_specs=in_specs, out_specs=(split,) * 5, check_vma=False
    )
```

```python
import functools

import jax
import jax.numpy as jnp
from jax import lax
from jax.experimental import pallas as pl
from jax.experimental.pallas import tpu as pltpu
from jax.sharding import PartitionSpec as P

HEAD_WIDTH = 128
HALF_GROUP_DEV = 4
LANES = 128
QUERY_BLOCK = 256
KERNEL_VMEM = 16 << 20

nf4_values = (
    -1.0,
    -0.6961928009986877,
    -0.5250730514526367,
    -0.39491748809814453,
    -0.28444138169288635,
    -0.18477343022823334,
    -0.09105003625154495,
    0.0,
    0.07958029955625534,
    0.16093020141124725,
    0.24611230194568634,
    0.33791524171829224,
    0.44070982933044434,
    0.5626170039176941,
    0.7229568362236023,
    1.0,
)
adapter_scale = 0.25
masked = -1e30


BF = jnp.bfloat16
F32 = jnp.float32
VM = pl.BlockSpec(memory_space=pltpu.VMEM)
SM = pl.BlockSpec(memory_space=pltpu.SMEM)
HB = pl.BlockSpec(memory_space=pltpu.HBM)


def sds(shape, dtype):
    return jax.ShapeDtypeStruct(shape, dtype)


def nt(a, b):
    return lax.dot_general(a, b, (((1,), (1,)), ((), ())), preferred_element_type=F32)


def nn(a, b):
    return jnp.dot(a, b, preferred_element_type=F32)


def call(body, outs, scratch, *args, n_scalar=0, in_hbm=False):
    if in_hbm:
        args = args[:n_scalar] + tuple(
            pltpu.with_memory_space_constraint(x, pltpu.HBM) for x in args[n_scalar:]
        )
    spec = HB if in_hbm else VM
    return pl.pallas_call(
        body,
        out_shape=outs,
        in_specs=[SM] * n_scalar + [spec] * (len(args) - n_scalar),
        out_specs=jax.tree.map(lambda _: VM, outs),
        scratch_shapes=scratch,
        compiler_params=pltpu.CompilerParams(vmem_limit_bytes=KERNEL_VMEM),
    )(*args)


def fetch(sources, targets, sem):
    copies = [
        pltpu.make_async_copy(src, to, sem.at[i])
        for i, (src, to) in enumerate(zip(sources, targets))
    ]
    for copy in copies:
        copy.start()
    for copy in copies:
        copy.wait()


def dequant_body(codes_in, index_in, table_in, out_ref, codes_ref, index_ref, table_ref, sem):
    fetch((codes_in, index_in, table_in), (codes_ref, index_ref, table_ref), sem)
    rows, cols = codes_ref.shape
    groups = index_ref.shape[0]
    parts = table_ref.shape[0]
    per_tile = groups * LANES // cols
    width = LANES // per_tile
    tables = [jnp.broadcast_to(table_ref[i : i + 1, :], (groups, LANES)) for i in range(parts)]
    scales = []
    for r0 in range(0, rows, LANES):
        idx = index_ref[:, r0 : min(r0 + LANES, rows)]
        short = LANES - idx.shape[1]
        if short:
            idx = jnp.concatenate([idx, jnp.zeros((groups, short), jnp.int32)], axis=1)
        low = idx % LANES
        scale = jnp.take_along_axis(tables[0], low, axis=1)
        for i in range(1, parts):
            scale = jnp.where(
                idx >= i * LANES, jnp.take_along_axis(tables[i], low, axis=1), scale
            )
        scales.append(scale)
    scales = jnp.concatenate(scales, axis=1).T[:rows, :]
    lane = lax.broadcasted_iota(jnp.int32, (rows, LANES), 1)
    place = lax.broadcasted_iota(jnp.int32, (8, LANES), 1)
    levels = jnp.zeros((8, LANES), F32)
    for i, level in enumerate(nf4_values):
        levels = jnp.where(place == i, level, levels)
    levels = jnp.broadcast_to(levels[:1], (rows, LANES))
    for b in range(cols // LANES):
        code = codes_ref[:, b * LANES : (b + 1) * LANES]
        value = jnp.take_along_axis(levels, code, axis=1)
        at = b * per_tile
        scale = jnp.broadcast_to(scales[:, at : at + 1], (rows, LANES))
        for i in range(1, per_tile):
            scale = jnp.where(lane >= i * width, scales[:, at + i : at + i + 1], scale)
        out_ref[:, b * LANES : (b + 1) * LANES] = (value * scale).astype(BF)


def adapter_chunks_body(half, strips, wide, up_ref, down_ref, out_ref):
    count, rank_rows = out_ref.shape[:2]
    step = up_ref.shape[1] // strips
    width = step // half
    short = wide - strips * width
    for j in range(half):
        pieces = [
            up_ref[:, i * step + j * width : i * step + (j + 1) * width] for i in range(strips)
        ]
        if short:
            pieces.append(jnp.zeros((rank_rows, short), BF))
        chunk = jnp.concatenate(pieces, axis=1)
        for p in range(count // half):
            out_ref[p * half + j, :, :wide] = chunk
            out_ref[p * half + j, :, wide:] = down_ref[...]


def adapter_grads_body(half, strips, slot, wide, pos_ref, in_ref, up_ref, down_ref):
    core = pos_ref[2]
    planes = in_ref.shape[0] // half
    width = slot // strips
    step = half * width
    for j in range(half):
        total = in_ref[j]
        for p in range(1, planes):
            total = total + in_ref[p * half + j]
        for i in range(strips):
            to = i * step + j * width
            up_ref[:, to : to + width] = total[:, i * width : (i + 1) * width]
        head = j ^ ((core & 1) * (half // 2))
        down_ref[:, pl.ds(pl.multiple_of(head * LANES, LANES), LANES)] = total[:, wide:]


def pack_grad_body(half, strips, pos_ref, g_ref, *out_refs):
    mine = pos_ref[0]
    rows = g_ref.shape[0]
    step = g_ref.shape[1] // strips
    width = step // half
    for s in range(half):
        to = mine ^ s
        for jv in range(half):

            @pl.when(to == jv)
            def _(s=s, jv=jv):
                pieces = [
                    g_ref[:, i * step + jv * width : i * step + (jv + 1) * width]
                    for i in range(strips)
                ]
                short = out_refs[s].shape[1] - strips * width
                if short:
                    pieces.append(jnp.zeros((rows, short), BF))
                out_refs[s][...] = jnp.concatenate(pieces, axis=1)


def pack_heads_body(half, pos_ref, q_in, k_in, v_in, *refs):
    out_refs, (q_ref, k_ref, v_ref, sem) = refs[:half], refs[half:]
    fetch((q_in, k_in, v_in), (q_ref, k_ref, v_ref), sem)
    own = pos_ref[4]
    for s in range(half):
        cols = pl.ds(pl.multiple_of((own ^ s) * LANES, LANES), LANES)
        out_refs[s][0] = q_ref[:, cols]
        out_refs[s][1] = k_ref[:, cols]
        out_refs[s][2] = v_ref[:, cols]


def assemble_body(half, pos_ref, *refs):
    pieces, (q_out, kv_out) = refs[:half], refs[half:]
    mine = pos_ref[0]
    rows = pieces[0].shape[1]
    for s in range(half):
        at = pl.ds(pl.multiple_of((mine ^ s) * rows, rows), rows)
        q_out[at, :] = pieces[s][0]
        kv_out[0, at, :] = pieces[s][1]
        kv_out[1, at, :] = pieces[s][2]


def lora_body(half, fsdp, pos_ref, *refs):
    ups, grads, out_ref = refs[:fsdp], refs[fsdp:-1], refs[-1]
    mine = pos_ref[0]
    rows, wide = grads[0].shape
    for s in range(half):
        total = None
        for f in range(fsdp):
            part = nt(grads[s * fsdp + f][...], ups[f][:, :wide])
            total = part if total is None else total + part
        at = pl.ds(pl.multiple_of((mine ^ s) * rows, rows), rows)
        out_ref[at, :] = adapter_scale * total


def join_body(pos_ref, lora_ref, *refs):
    mids, out_ref = refs[:-1], refs[-1]
    rows = out_ref.shape[0]
    mid = mids[0][...]
    for m in mids[1:]:
        mid = mid + m[...]
    lora = lora_ref[pl.ds(pl.multiple_of(pos_ref[2] * rows, rows), rows), :]
    out_ref[...] = jnp.concatenate([lora, mid], axis=1).astype(BF)


def total_body(*refs):
    total = refs[0][...].astype(F32)
    for ref in refs[1:-1]:
        total = total + ref[...].astype(F32)
    refs[-1][...] = total.astype(BF)


def project_body(half, planes, fsdp, slot, targets, pos_ref, *refs):
    ups = refs[:fsdp]
    grads = refs[fsdp : fsdp + half * fsdp]
    weights = refs[fsdp + half * fsdp : fsdp + half * fsdp + planes]
    outs = refs[fsdp + half * fsdp + planes : -2]
    w_scr, d_scr = refs[-2:]
    mine, plane, core, own = pos_ref[0], pos_ref[1], pos_ref[2], pos_ref[4]
    rows_each = weights[0].shape[0]
    rows, wide = grads[0].shape
    tail = w_scr.shape[0] - planes * rows_each
    if tail:
        w_scr[planes * rows_each :, :] = jnp.zeros((tail, w_scr.shape[1]), BF)
    for i, t in enumerate(targets):
        cols = pl.ds(pl.multiple_of((own ^ t) * LANES, LANES), LANES)
        d_cols = pl.ds(pl.multiple_of(wide + (own ^ t) * LANES, LANES), LANES)
        to = slice(i * LANES, (i + 1) * LANES)
        d_scr[:, to] = ups[0][:, d_cols]
        for s in range(planes):
            src = lax.rem(plane + (planes - s), planes)
            at = pl.ds(pl.multiple_of(src * rows_each, rows_each), rows_each)
            w_scr[at, to] = weights[s][:, cols]
    for f in range(fsdp):
        src = lax.rem(core + (fsdp - f), fsdp)
        at = pl.ds(pl.multiple_of(src * slot, 16), slot)
        low = lax.dot_general(
            ups[f][:, :wide], d_scr[...], (((0,), (0,)), ((), ())), preferred_element_type=F32
        )
        w_scr[at, :] = (w_scr[at, :].astype(F32) + adapter_scale * low[:slot]).astype(BF)
    for s in range(half):
        at = pl.ds(pl.multiple_of((mine ^ s) * rows, rows), rows)
        acc = None
        for f in range(fsdp):
            src = lax.rem(core + (fsdp - f), fsdp)
            w_at = pl.ds(pl.multiple_of(src * slot, 16), wide)
            part = nn(grads[s * fsdp + f][...], w_scr[w_at, :])
            acc = part if acc is None else acc + part
        for i in range(len(targets)):
            outs[i][at, :] = acc[:, i * LANES : (i + 1) * LANES].astype(BF)


def score_block(key, query, k0, q0):
    scores = nt(key, query) * (HEAD_WIDTH**-0.5)
    if k0 is None or k0 + key.shape[0] - 1 <= q0:
        return scores
    kpos = k0 + lax.broadcasted_iota(jnp.int32, scores.shape, 0)
    qpos = q0 + lax.broadcasted_iota(jnp.int32, scores.shape, 1)
    return jnp.where(kpos <= qpos, scores, masked)


def forward_body(fsdp, wide, pos_ref, q_ref, kv_ref, far_ref, adapt_ref, o_ref, lse_ref, *refs):
    mid_refs, (vt_scr, oft_scr, mid_ref) = refs[:fsdp], refs[fsdp:]
    core, later, own = pos_ref[2], pos_ref[3], pos_ref[4]
    down = adapt_ref[:, pl.ds(pl.multiple_of(wide + own * LANES, LANES), LANES)]
    tokens = q_ref.shape[0]
    block = min(QUERY_BLOCK, tokens)
    vt_scr[...] = kv_ref[1].T

    def finish(q0, block_out, norm):
        qs = slice(q0, q0 + block)
        out = block_out.T
        o_ref[qs, :] = out
        lse_ref[:, qs] = norm
        mid_ref[qs, :] = nt(out.astype(BF), down)

    def near(q0):
        return score_block(kv_ref[0, : q0 + block, :], q_ref[q0 : q0 + block, :], 0, q0)

    @pl.when(later == 0)
    def _():
        for q0 in range(0, tokens, block):
            scores = near(q0)
            top = jnp.max(scores, axis=0, keepdims=True)
            prob = jnp.exp(scores - top)
            total = jnp.sum(prob, axis=0, keepdims=True)
            out = nn(vt_scr[:, : q0 + block], prob.astype(BF)) / total
            finish(q0, out, top + jnp.log(total))

    @pl.when(later != 0)
    def _():
        oft_scr[...] = far_ref[1].T
        for q0 in range(0, tokens, block):
            scores = near(q0)
            far = score_block(far_ref[0], q_ref[q0 : q0 + block, :], None, q0)
            top = jnp.maximum(
                jnp.max(scores, axis=0, keepdims=True), jnp.max(far, axis=0, keepdims=True)
            )
            prob = jnp.exp(scores - top)
            far_prob = jnp.exp(far - top)
            total = jnp.sum(prob, axis=0, keepdims=True) + jnp.sum(far_prob, axis=0, keepdims=True)
            out = nn(vt_scr[:, : q0 + block], prob.astype(BF)) + nn(
                oft_scr[...], far_prob.astype(BF)
            )
            finish(q0, out / total, top + jnp.log(total))

    rows = tokens // fsdp
    for s in range(fsdp):
        to = lax.rem(core + s, fsdp)
        mid_refs[s][...] = mid_ref[pl.ds(pl.multiple_of(to * rows, rows), rows), :]


def grad_block(key, value, query, grad, norm, delta, k0, q0):
    prob = jnp.exp(score_block(key, query, k0, q0) - norm)
    prob_grad = nt(value, grad)
    score_grad = prob * (prob_grad - delta) * (HEAD_WIDTH**-0.5)
    return prob.astype(BF), score_grad.astype(BF)


def far_body(half, pos_ref, *refs):
    parts = refs[:half]
    q_ref, far_ref, o_ref, norm_ref = refs[half : half + 4]
    far_out, dq_ref, do_ref, delta_ref, kt_scr = refs[half + 4 :]
    later = pos_ref[3]
    tokens = q_ref.shape[0]
    block = min(QUERY_BLOCK, tokens)
    total = parts[0][...].astype(F32)
    for s in range(1, half):
        total = total + parts[s][...].astype(F32)
    grad = total.astype(BF)
    do_ref[...] = grad
    delta_ref[...] = jnp.sum((grad.astype(F32) * o_ref[...]).T, axis=0, keepdims=True)

    @pl.when(later != 0)
    def _():
        kt_scr[...] = far_ref[0].T
        for k0 in range(0, tokens, block):
            ks = slice(k0, k0 + block)
            prob, score_grad = grad_block(
                far_ref[0, ks, :],
                far_ref[1, ks, :],
                q_ref[...],
                do_ref[...],
                norm_ref[...],
                delta_ref[...],
                None,
                0,
            )
            far_out[0, ks, :] = nn(score_grad, q_ref[...]).astype(BF)
            far_out[1, ks, :] = nn(prob, do_ref[...]).astype(BF)
            part = nn(kt_scr[:, ks], score_grad)
            if k0:
                dq_ref[...] += part
            else:
                dq_ref[...] = part

    @pl.when(later == 0)
    def _():
        far_out[...] = jnp.zeros(far_out.shape, BF)
        dq_ref[...] = jnp.zeros(dq_ref.shape, F32)


def near_body(pos_ref, q_ref, kv_ref, do_ref, norm_ref, delta_ref, dq_in, dq_ref, near_ref, kt_scr):
    tokens = q_ref.shape[0]
    block = min(QUERY_BLOCK, tokens)
    kt_scr[...] = kv_ref[0].T
    for q0 in range(0, tokens, block):
        qs = slice(q0, q0 + block)
        depth = q0 + block
        prob, score_grad = grad_block(
            kv_ref[0, :depth, :],
            kv_ref[1, :depth, :],
            q_ref[qs, :],
            do_ref[qs, :],
            norm_ref[:, qs],
            delta_ref[:, qs],
            0,
            q0,
        )
        dk = nn(score_grad, q_ref[qs, :])
        dv = nn(prob, do_ref[qs, :])
        if q0:
            near_ref[0, :q0, :] += dk[:q0]
            near_ref[1, :q0, :] += dv[:q0]
        near_ref[0, qs, :] = dk[q0:]
        near_ref[1, qs, :] = dv[q0:]
        dq = dq_in[:, qs] + nn(kt_scr[:, :depth], score_grad)
        dq_ref[qs, :] = dq.T.astype(BF)


def merge_body(half, pos_ref, dq_ref, near_ref, back_ref, *out_refs):
    mine = pos_ref[0]
    rows = near_ref.shape[1] // half
    for s in range(half):
        at = pl.ds(pl.multiple_of((mine ^ s) * rows, rows), rows)
        out_refs[s][0] = dq_ref[at, :]
        for i in range(2):
            merged = near_ref[i, at, :] + back_ref[i, at, :].astype(F32)
            out_refs[s][1 + i] = merged.astype(BF)


def unpack_body(half, pos_ref, *refs):
    pieces, outs = refs[:half], refs[half:]
    own = pos_ref[4]
    for s in range(half):
        at = pl.ds(pl.multiple_of((own ^ s) * LANES, LANES), LANES)
        for i in range(3):
            outs[i][:, at] = pieces[s][i]


def adapters_body(half, fsdp, pos_ref, o_ref, *refs):
    both, grads, (out_ref, scr) = refs[:fsdp], refs[fsdp : fsdp + half], refs[fsdp + half :]
    mine, core = pos_ref[0], pos_ref[2]
    count, rank_rows = out_ref.shape[:2]
    rank = count * rank_rows
    rows, wide = grads[0].shape
    part_rows = both[0].shape[0]
    for s in range(fsdp):
        src = lax.rem(core + (fsdp - s), fsdp)
        scr[pl.ds(pl.multiple_of(src * part_rows, part_rows), part_rows), :] = both[s][...]
    acc = None
    for s in range(half):
        at = pl.ds(pl.multiple_of((mine ^ s) * rows, rows), rows)
        part = nn(scr[at, :].T[rank:, :], grads[s][...])
        acc = part if acc is None else acc + part
    acc = adapter_scale * acc
    low = nn(scr[...].T[:rank, :], o_ref[...].astype(BF))
    for c in range(count):
        out_ref[c, :, :wide] = acc[c * rank_rows : (c + 1) * rank_rows, :]
        out_ref[c, :, wide:] = low[c * rank_rows : (c + 1) * rank_rows, :]


def on_device(
    sizes,
    rotated_query_rows,
    rotated_key_rows,
    saved_value_rows,
    projection_output_gradient,
    frozen_weight_codes,
    block_scale_index,
    block_scale_table,
    adapter_down_matrix,
    adapter_up_matrix,
):
    n_ctx, fsdp = sizes
    half = HALF_GROUP_DEV
    planes = n_ctx // half
    rows = rotated_query_rows.shape[0]
    heads = rotated_query_rows.shape[1] // HEAD_WIDTH
    assert heads == half
    tokens = rows * half
    w_rows, w_cols = frozen_weight_codes.shape
    grad_cols = projection_output_gradient.shape[1]
    strips = grad_cols // (half * w_rows)
    slot = strips * w_rows
    wide = -(-slot // LANES) * LANES
    rank_rows = adapter_down_matrix.shape[0]
    rank = rank_rows * n_ctx

    def head_of(j, f):
        return j ^ ((f & 1) * (half // 2))

    ctx = lax.axis_index("ctx")
    core = lax.axis_index("fsdp")
    mine = ctx % half
    plane = ctx // half
    own = head_of(mine, core)
    later = jnp.where(own < heads // 2, plane % 2, 1 - plane % 2)
    pos = jnp.stack([mine, plane, core, later, own]).astype(jnp.int32)

    def in_plane(x, s):
        if s == 0:
            return x
        return lax.ppermute(x, "ctx", [(i, i ^ s) for i in range(n_ctx)])

    def along(x, s):
        if s == 0:
            return x
        return lax.ppermute(x, "ctx", [(i, (i + s * half) % n_ctx) for i in range(n_ctx)])

    def across(x, s):
        if s == 0:
            return x
        return lax.ppermute(x, "fsdp", [(i, (i + s) % fsdp) for i in range(fsdp)])

    pairs = []
    for i in range(n_ctx):
        for f in range(fsdp):
            p, j = divmod(i, half)
            if (p % 2 == 0) == (head_of(j, f) < heads // 2):
                pairs.append((i * fsdp + f, (i + half) % n_ctx * fsdp + f))

    def to_later(x):
        return lax.ppermute(x, ("ctx", "fsdp"), pairs)

    def to_earlier(x):
        return lax.ppermute(x, ("ctx", "fsdp"), [(b, a) for a, b in pairs])

    table = block_scale_table.reshape(-1, LANES)
    index = block_scale_index.T
    weight = call(
        dequant_body,
        sds((w_rows, w_cols), BF),
        [pltpu.VMEM(x.shape, x.dtype) for x in (frozen_weight_codes, index, table)]
        + [pltpu.SemaphoreType.DMA((3,))],
        frozen_weight_codes,
        index,
        table,
        in_hbm=True,
    )
    weights = [along(weight, s) for s in range(planes)]

    grads = call(
        functools.partial(pack_grad_body, half, strips),
        [sds((rows, wide), BF)] * half,
        [],
        pos,
        projection_output_gradient,
        n_scalar=1,
    )
    grads = [in_plane(x, s) for s, x in enumerate(grads)]
    swapped = [across(g, f) for g in grads for f in range(fsdp)]

    packed = call(
        functools.partial(pack_heads_body, half),
        [sds((3, rows, LANES), BF)] * half,
        [pltpu.VMEM(rotated_query_rows.shape, BF)] * 3 + [pltpu.SemaphoreType.DMA((3,))],
        pos,
        rotated_query_rows,
        rotated_key_rows,
        saved_value_rows,
        n_scalar=1,
        in_hbm=True,
    )
    packed = [in_plane(x, s) for s, x in enumerate(packed)]
    query, key_value = call(
        functools.partial(assemble_body, half),
        [sds((tokens, LANES), BF), sds((2, tokens, LANES), BF)],
        [],
        pos,
        *packed,
        n_scalar=1,
    )
    far = to_later(key_value)

    chunks = call(
        functools.partial(adapter_chunks_body, half, strips, wide),
        sds((n_ctx, rank_rows, wide + heads * HEAD_WIDTH), BF),
        [],
        adapter_up_matrix,
        adapter_down_matrix,
    )
    adapters = lax.all_to_all(chunks, "ctx", split_axis=0, concat_axis=0, tiled=True)
    adapters = adapters.reshape(rank, -1)
    ups = [across(adapters, f) for f in range(fsdp)]
    lora = call(
        functools.partial(lora_body, half, fsdp),
        sds((tokens, rank), F32),
        [],
        pos,
        *ups,
        *swapped,
        n_scalar=1,
    )

    def project(targets):
        return call(
            functools.partial(project_body, half, planes, fsdp, slot, targets),
            [sds((tokens, LANES), BF)] * len(targets),
            [
                pltpu.VMEM((planes * w_rows + wide - slot, LANES * len(targets)), BF),
                pltpu.VMEM((rank, LANES * len(targets)), BF),
            ],
            pos,
            *ups,
            *swapped,
            *weights,
            n_scalar=1,
        )

    first, second = range(half // 2, half), range(half // 2)
    partial = dict(zip(first, project(tuple(first))))
    partial = {s: in_plane(x, s) for s, x in partial.items()}
    rest = dict(zip(second, project(tuple(second))))
    partial.update({s: in_plane(x, s) for s, x in rest.items()})

    part_rows = tokens // fsdp
    out, norm, *mids = call(
        functools.partial(forward_body, fsdp, wide),
        [sds((tokens, LANES), F32), sds((1, tokens), F32)]
        + [sds((part_rows, rank), F32)] * fsdp,
        [
            pltpu.VMEM((LANES, tokens), BF),
            pltpu.VMEM((LANES, tokens), BF),
            pltpu.VMEM((tokens, rank), F32),
        ],
        pos,
        query,
        key_value,
        far,
        adapters,
        n_scalar=1,
    )
    mids = [across(x, f) for f, x in enumerate(mids)]
    both = call(join_body, sds((part_rows, 2 * rank), BF), [], pos, lora, *mids, n_scalar=1)
    both = [in_plane(both, s) for s in range(half)]
    both = call(total_body, sds((part_rows, 2 * rank), BF), [], *both)
    both = [across(both, f) for f in range(fsdp)]
    adapter_grads = call(
        functools.partial(adapters_body, half, fsdp),
        sds((n_ctx, rank_rows, wide + HEAD_WIDTH), F32),
        [pltpu.VMEM((tokens, 2 * rank), BF)],
        pos,
        out,
        *both,
        *grads,
        n_scalar=1,
    )
    reduced = lax.all_to_all(adapter_grads, "ctx", split_axis=0, concat_axis=0, tiled=True)
    up_grad, down_grad = call(
        functools.partial(adapter_grads_body, half, strips, slot, wide),
        [sds((rank_rows, grad_cols), F32), sds((rank_rows, heads * HEAD_WIDTH), F32)],
        [],
        pos,
        reduced,
        n_scalar=1,
    )

    far_part, dq_far, grad_out, delta = call(
        functools.partial(far_body, half),
        [
            sds((2, tokens, LANES), BF),
            sds((LANES, tokens), F32),
            sds((tokens, LANES), BF),
            sds((1, tokens), F32),
        ],
        [pltpu.VMEM((LANES, tokens), BF)],
        pos,
        *[partial[s] for s in range(half)],
        query,
        far,
        out,
        norm,
        n_scalar=1,
    )
    back = to_earlier(far_part)
    dq, near = call(
        near_body,
        [sds((tokens, LANES), BF), sds((2, tokens, LANES), F32)],
        [pltpu.VMEM((LANES, tokens), BF)],
        pos,
        query,
        key_value,
        grad_out,
        norm,
        delta,
        dq_far,
        n_scalar=1,
    )
    merged = call(
        functools.partial(merge_body, half),
        [sds((3, rows, LANES), BF)] * half,
        [],
        pos,
        dq,
        near,
        back,
        n_scalar=1,
    )
    merged = [in_plane(x, s) for s, x in enumerate(merged)]
    query_grad, key_grad, value_grad = call(
        functools.partial(unpack_body, half),
        [sds((rows, heads * HEAD_WIDTH), BF)] * 3,
        [],
        pos,
        *merged,
        n_scalar=1,
    )
    return query_grad, key_grad, value_grad, down_grad, up_grad


def solution(mesh):
    split = P("ctx", "fsdp")
    in_specs = (split,) * 6 + (P(),) + (split,) * 2

    def body(*args):
        return on_device((mesh.shape["ctx"], mesh.shape["fsdp"]), *args)

    return jax.shard_map(
        body, mesh=mesh, in_specs=in_specs, out_specs=(split,) * 5, check_vma=False
    )
```

```python
import functools

import jax
import jax.numpy as jnp
from jax import lax
from jax.experimental import pallas as pl
from jax.experimental.pallas import tpu as pltpu
from jax.sharding import PartitionSpec as P

HEAD_WIDTH = 128
HALF_GROUP_DEV = 4
LANES = 128
QUERY_BLOCK = 256
KERNEL_VMEM = 16 << 20

nf4_values = (
    -1.0,
    -0.6961928009986877,
    -0.5250730514526367,
    -0.39491748809814453,
    -0.28444138169288635,
    -0.18477343022823334,
    -0.09105003625154495,
    0.0,
    0.07958029955625534,
    0.16093020141124725,
    0.24611230194568634,
    0.33791524171829224,
    0.44070982933044434,
    0.5626170039176941,
    0.7229568362236023,
    1.0,
)
adapter_scale = 0.25
masked = -1e30


BF = jnp.bfloat16
F32 = jnp.float32
VM = pl.BlockSpec(memory_space=pltpu.VMEM)
SM = pl.BlockSpec(memory_space=pltpu.SMEM)
HB = pl.BlockSpec(memory_space=pltpu.HBM)


def sds(shape, dtype):
    return jax.ShapeDtypeStruct(shape, dtype)


def nt(a, b):
    return lax.dot_general(a, b, (((1,), (1,)), ((), ())), preferred_element_type=F32)


def nn(a, b):
    return jnp.dot(a, b, preferred_element_type=F32)


def call(body, outs, scratch, *args, n_scalar=0, in_hbm=False):
    if in_hbm:
        args = args[:n_scalar] + tuple(
            pltpu.with_memory_space_constraint(x, pltpu.HBM) for x in args[n_scalar:]
        )
    spec = HB if in_hbm else VM
    return pl.pallas_call(
        body,
        out_shape=outs,
        in_specs=[SM] * n_scalar + [spec] * (len(args) - n_scalar),
        out_specs=jax.tree.map(lambda _: VM, outs),
        scratch_shapes=scratch,
        compiler_params=pltpu.CompilerParams(vmem_limit_bytes=KERNEL_VMEM),
    )(*args)


def fetch(sources, targets, sem):
    copies = [
        pltpu.make_async_copy(src, to, sem.at[i])
        for i, (src, to) in enumerate(zip(sources, targets))
    ]
    for copy in copies:
        copy.start()
    for copy in copies:
        copy.wait()


def dequant_body(codes_in, index_in, table_in, out_ref, codes_ref, index_ref, table_ref, sem):
    fetch((codes_in, index_in, table_in), (codes_ref, index_ref, table_ref), sem)
    rows, cols = codes_ref.shape
    groups = index_ref.shape[0]
    parts = table_ref.shape[0]
    per_tile = groups * LANES // cols
    width = LANES // per_tile
    tables = [jnp.broadcast_to(table_ref[i : i + 1, :], (groups, LANES)) for i in range(parts)]
    scales = []
    for r0 in range(0, rows, LANES):
        idx = index_ref[:, r0 : min(r0 + LANES, rows)]
        short = LANES - idx.shape[1]
        if short:
            idx = jnp.concatenate([idx, jnp.zeros((groups, short), jnp.int32)], axis=1)
        low = idx % LANES
        scale = jnp.take_along_axis(tables[0], low, axis=1)
        for i in range(1, parts):
            scale = jnp.where(
                idx >= i * LANES, jnp.take_along_axis(tables[i], low, axis=1), scale
            )
        scales.append(scale)
    scales = jnp.concatenate(scales, axis=1).T[:rows, :]
    lane = lax.broadcasted_iota(jnp.int32, (rows, LANES), 1)
    place = lax.broadcasted_iota(jnp.int32, (8, LANES), 1)
    levels = jnp.zeros((8, LANES), F32)
    for i, level in enumerate(nf4_values):
        levels = jnp.where(place == i, level, levels)
    levels = jnp.broadcast_to(levels[:1], (rows, LANES))
    for b in range(cols // LANES):
        code = codes_ref[:, b * LANES : (b + 1) * LANES]
        value = jnp.take_along_axis(levels, code, axis=1)
        at = b * per_tile
        scale = jnp.broadcast_to(scales[:, at : at + 1], (rows, LANES))
        for i in range(1, per_tile):
            scale = jnp.where(lane >= i * width, scales[:, at + i : at + i + 1], scale)
        out_ref[:, b * LANES : (b + 1) * LANES] = (value * scale).astype(BF)


def raw_body(n_ups, *refs):
    ins, out_refs, sem = refs[: n_ups + 1], refs[n_ups + 1 : -1], refs[-1]
    out_ref = out_refs[0]
    at = 0
    copies = []
    for i, ref in enumerate(ins):
        width = ref.shape[1]
        copies.append(pltpu.make_async_copy(ref, out_ref.at[:, at : at + width], sem.at[i]))
        at += width
    for copy in copies:
        copy.start()
    for copy in copies:
        copy.wait()


def chunks_body(half, fsdp, strips, wide, pos_ref, *refs):
    ins, out_refs = refs[:-half], refs[-half:]
    mine = pos_ref[0]
    rank_rows, cols = ins[0].shape
    grad_cols = (cols - half * LANES) // fsdp
    step = grad_cols // strips
    width = step // half
    short = wide - strips * width
    for s in range(half):
        for jv in range(half):

            @pl.when((mine ^ s) == jv)
            def _(s=s, jv=jv):
                for p, ref in enumerate(ins):
                    for f in range(fsdp):
                        base = f * grad_cols + jv * width
                        pieces = [
                            ref[:, base + i * step : base + i * step + width]
                            for i in range(strips)
                        ]
                        if short:
                            pieces.append(jnp.zeros((rank_rows, short), BF))
                        out_refs[s][p, :, f * wide : (f + 1) * wide] = jnp.concatenate(
                            pieces, axis=1
                        )
                    out_refs[s][p, :, fsdp * wide :] = ref[:, fsdp * grad_cols :]


def relay_body(pos_ref, above_ref, below_ref, inner_ref, outer_ref):
    @pl.when(pos_ref[1] == 1)
    def _():
        inner_ref[...] = above_ref[...]
        outer_ref[...] = below_ref[...]

    @pl.when(pos_ref[1] != 1)
    def _():
        inner_ref[...] = below_ref[...]
        outer_ref[...] = above_ref[...]


def pack_grad_body(half, strips, pos_ref, g_ref, *out_refs):
    mine = pos_ref[0]
    rows = g_ref.shape[0]
    step = g_ref.shape[1] // strips
    width = step // half
    for s in range(half):
        to = mine ^ s
        for jv in range(half):

            @pl.when(to == jv)
            def _(s=s, jv=jv):
                pieces = [
                    g_ref[:, i * step + jv * width : i * step + (jv + 1) * width]
                    for i in range(strips)
                ]
                short = out_refs[s].shape[1] - strips * width
                if short:
                    pieces.append(jnp.zeros((rows, short), BF))
                out_refs[s][...] = jnp.concatenate(pieces, axis=1)


def pack_heads_body(half, pos_ref, q_in, k_in, v_in, *refs):
    out_refs, (q_ref, k_ref, v_ref, sem) = refs[:half], refs[half:]
    fetch((q_in, k_in, v_in), (q_ref, k_ref, v_ref), sem)
    own = pos_ref[4]
    for s in range(half):
        cols = pl.ds(pl.multiple_of((own ^ s) * LANES, LANES), LANES)
        out_refs[s][0] = q_ref[:, cols]
        out_refs[s][1] = k_ref[:, cols]
        out_refs[s][2] = v_ref[:, cols]


def assemble_body(half, pos_ref, *refs):
    pieces, (q_out, kv_out) = refs[:half], refs[half:]
    mine = pos_ref[0]
    rows = pieces[0].shape[1]
    for s in range(half):
        at = pl.ds(pl.multiple_of((mine ^ s) * rows, rows), rows)
        q_out[at, :] = pieces[s][0]
        kv_out[0, at, :] = pieces[s][1]
        kv_out[1, at, :] = pieces[s][2]


def ranks_body(half, pos_ref, *refs):
    pieces, (out_ref, scr) = refs[:half], refs[half:]
    mine = pos_ref[0]
    planes = scr.shape[1]
    for s in range(half):
        scr[mine ^ s] = pieces[s][...].astype(F32)
    parts = [scr[j, p] for p in range(planes) for j in range(half)]
    out_ref[...] = jnp.concatenate(parts, axis=0).astype(BF)


def lora_body(half, fsdp, pos_ref, adapt_ref, *refs):
    grads, out_ref = refs[:-1], refs[-1]
    mine = pos_ref[0]
    rows, wide = grads[0].shape
    for s in range(half):
        total = None
        for f in range(fsdp):
            part = nt(grads[s * fsdp + f][...], adapt_ref[:, f * wide : (f + 1) * wide])
            total = part if total is None else total + part
        at = pl.ds(pl.multiple_of((mine ^ s) * rows, rows), rows)
        out_ref[at, :] = adapter_scale * total


def join_body(pos_ref, lora_ref, *refs):
    mids, out_ref = refs[:-1], refs[-1]
    rows = out_ref.shape[0]
    mid = mids[0][...]
    for m in mids[1:]:
        mid = mid + m[...]
    lora = lora_ref[pl.ds(pl.multiple_of(pos_ref[2] * rows, rows), rows), :]
    out_ref[...] = jnp.concatenate([lora, mid], axis=1).astype(BF)


def total_body(*refs):
    total = refs[0][...].astype(F32)
    for ref in refs[1:-1]:
        total = total + ref[...].astype(F32)
    refs[-1][...] = total.astype(BF)


def project_body(half, planes, fsdp, slot, targets, pos_ref, adapt_ref, *refs):
    grads = refs[: half * fsdp]
    weights = refs[half * fsdp : -2 - len(targets)]
    n_weights = len(weights)
    outs = refs[-2 - len(targets) : -2]
    w_scr, d_scr = refs[-2:]
    mine, plane, core, own = pos_ref[0], pos_ref[1], pos_ref[2], pos_ref[4]
    rows_each = weights[0].shape[0]
    rows, wide = grads[0].shape
    tail = w_scr.shape[0] - planes * rows_each
    if tail:
        w_scr[planes * rows_each :, :] = jnp.zeros((tail, w_scr.shape[1]), BF)
    for i, t in enumerate(targets):
        cols = pl.ds(pl.multiple_of((own ^ t) * LANES, LANES), LANES)
        d_cols = pl.ds(pl.multiple_of(fsdp * wide + (own ^ t) * LANES, LANES), LANES)
        to = slice(i * LANES, (i + 1) * LANES)
        d_scr[:, to] = adapt_ref[:, d_cols]
        if n_weights == planes:
            sources = [lax.rem(plane + (planes - s), planes) for s in range(planes)]
        else:
            away = lax.rem(plane + 2, planes)
            inside = (plane == 1) | (plane == 2)
            sources = [plane, lax.rem(plane + planes - 1, planes), lax.rem(plane + 1, planes)]
            sources += [jnp.where(inside, away, -1), jnp.where(inside, -1, away)]
        for piece, src in zip(weights, sources):

            @pl.when(src >= 0)
            def _(piece=piece, src=src, to=to, cols=cols):
                at = pl.ds(pl.multiple_of(src * rows_each, rows_each), rows_each)
                w_scr[at, to] = piece[:, cols]

    for f in range(fsdp):
        src = lax.rem(core + (fsdp - f), fsdp)
        at = pl.ds(pl.multiple_of(src * slot, 16), slot)
        up = adapt_ref[:, f * wide : (f + 1) * wide]
        low = lax.dot_general(
            up, d_scr[...], (((0,), (0,)), ((), ())), preferred_element_type=F32
        )
        w_scr[at, :] = (w_scr[at, :].astype(F32) + adapter_scale * low[:slot]).astype(BF)
    for s in range(half):
        at = pl.ds(pl.multiple_of((mine ^ s) * rows, rows), rows)
        acc = None
        for f in range(fsdp):
            src = lax.rem(core + (fsdp - f), fsdp)
            w_at = pl.ds(pl.multiple_of(src * slot, 16), wide)
            part = nn(grads[s * fsdp + f][...], w_scr[w_at, :])
            acc = part if acc is None else acc + part
        for i in range(len(targets)):
            outs[i][at, :] = acc[:, i * LANES : (i + 1) * LANES].astype(BF)


def score_block(key, query, k0, q0):
    scores = nt(key, query) * (HEAD_WIDTH**-0.5)
    if k0 is None or k0 + key.shape[0] - 1 <= q0:
        return scores
    kpos = k0 + lax.broadcasted_iota(jnp.int32, scores.shape, 0)
    qpos = q0 + lax.broadcasted_iota(jnp.int32, scores.shape, 1)
    return jnp.where(kpos <= qpos, scores, masked)


def middle_body(fsdp, wide, pos_ref, o_ref, adapt_ref, *refs):
    core, own = pos_ref[2], pos_ref[4]
    down = adapt_ref[:, pl.ds(pl.multiple_of(fsdp * wide + own * LANES, LANES), LANES)]
    rows = o_ref.shape[0] // fsdp
    for s in range(fsdp):
        to = lax.rem(core + s, fsdp)
        part = o_ref[pl.ds(pl.multiple_of(to * rows, rows), rows), :]
        refs[s][...] = nt(part.astype(BF), down)


def forward_body(pos_ref, q_ref, kv_ref, far_ref, o_ref, lse_ref, vt_scr, oft_scr):
    later = pos_ref[3]
    tokens = q_ref.shape[0]
    block = min(QUERY_BLOCK, tokens)
    vt_scr[...] = kv_ref[1].T

    def finish(q0, block_out, norm):
        qs = slice(q0, q0 + block)
        out = block_out.T
        o_ref[qs, :] = out
        lse_ref[:, qs] = norm

    def near(q0):
        return score_block(kv_ref[0, : q0 + block, :], q_ref[q0 : q0 + block, :], 0, q0)

    @pl.when(later == 0)
    def _():
        for q0 in range(0, tokens, block):
            scores = near(q0)
            top = jnp.max(scores, axis=0, keepdims=True)
            prob = jnp.exp(scores - top)
            total = jnp.sum(prob, axis=0, keepdims=True)
            out = nn(vt_scr[:, : q0 + block], prob.astype(BF)) / total
            finish(q0, out, top + jnp.log(total))

    @pl.when(later != 0)
    def _():
        oft_scr[...] = far_ref[1].T
        for q0 in range(0, tokens, block):
            scores = near(q0)
            far = score_block(far_ref[0], q_ref[q0 : q0 + block, :], None, q0)
            top = jnp.maximum(
                jnp.max(scores, axis=0, keepdims=True), jnp.max(far, axis=0, keepdims=True)
            )
            prob = jnp.exp(scores - top)
            far_prob = jnp.exp(far - top)
            total = jnp.sum(prob, axis=0, keepdims=True) + jnp.sum(far_prob, axis=0, keepdims=True)
            out = nn(vt_scr[:, : q0 + block], prob.astype(BF)) + nn(
                oft_scr[...], far_prob.astype(BF)
            )
            finish(q0, out / total, top + jnp.log(total))


def grad_block(key, value, query, grad, norm, delta, k0, q0):
    prob = jnp.exp(score_block(key, query, k0, q0) - norm)
    prob_grad = nt(value, grad)
    score_grad = prob * (prob_grad - delta) * (HEAD_WIDTH**-0.5)
    return prob.astype(BF), score_grad.astype(BF)


def far_body(half, pos_ref, *refs):
    parts = refs[:half]
    q_ref, far_ref, o_ref, norm_ref = refs[half : half + 4]
    far_out, dq_ref, do_ref, delta_ref, kt_scr = refs[half + 4 :]
    later = pos_ref[3]
    tokens = q_ref.shape[0]
    block = min(QUERY_BLOCK, tokens)
    total = parts[0][...].astype(F32)
    for s in range(1, half):
        total = total + parts[s][...].astype(F32)
    grad = total.astype(BF)
    do_ref[...] = grad
    delta_ref[...] = jnp.sum((grad.astype(F32) * o_ref[...]).T, axis=0, keepdims=True)

    @pl.when(later != 0)
    def _():
        kt_scr[...] = far_ref[0].T
        for k0 in range(0, tokens, block):
            ks = slice(k0, k0 + block)
            prob, score_grad = grad_block(
                far_ref[0, ks, :],
                far_ref[1, ks, :],
                q_ref[...],
                do_ref[...],
                norm_ref[...],
                delta_ref[...],
                None,
                0,
            )
            far_out[0, ks, :] = nn(score_grad, q_ref[...]).astype(BF)
            far_out[1, ks, :] = nn(prob, do_ref[...]).astype(BF)
            part = nn(kt_scr[:, ks], score_grad)
            if k0:
                dq_ref[...] += part
            else:
                dq_ref[...] = part

    @pl.when(later == 0)
    def _():
        far_out[...] = jnp.zeros(far_out.shape, BF)
        dq_ref[...] = jnp.zeros(dq_ref.shape, F32)


def near_body(pos_ref, q_ref, kv_ref, do_ref, norm_ref, delta_ref, dq_in, dq_ref, near_ref, kt_scr):
    tokens = q_ref.shape[0]
    block = min(QUERY_BLOCK, tokens)
    kt_scr[...] = kv_ref[0].T
    for q0 in range(0, tokens, block):
        qs = slice(q0, q0 + block)
        depth = q0 + block
        prob, score_grad = grad_block(
            kv_ref[0, :depth, :],
            kv_ref[1, :depth, :],
            q_ref[qs, :],
            do_ref[qs, :],
            norm_ref[:, qs],
            delta_ref[:, qs],
            0,
            q0,
        )
        dk = nn(score_grad, q_ref[qs, :])
        dv = nn(prob, do_ref[qs, :])
        if q0:
            near_ref[0, :q0, :] += dk[:q0]
            near_ref[1, :q0, :] += dv[:q0]
        near_ref[0, qs, :] = dk[q0:]
        near_ref[1, qs, :] = dv[q0:]
        dq = dq_in[:, qs] + nn(kt_scr[:, :depth], score_grad)
        dq_ref[qs, :] = dq.T.astype(BF)


def merge_body(half, pos_ref, dq_ref, near_ref, back_ref, *out_refs):
    mine = pos_ref[0]
    rows = near_ref.shape[1] // half
    for s in range(half):
        at = pl.ds(pl.multiple_of((mine ^ s) * rows, rows), rows)
        out_refs[s][0] = dq_ref[at, :]
        for i in range(2):
            merged = near_ref[i, at, :] + back_ref[i, at, :].astype(F32)
            out_refs[s][1 + i] = merged.astype(BF)


def unpack_body(half, pos_ref, *refs):
    pieces, outs = refs[:half], refs[half:]
    own = pos_ref[4]
    for s in range(half):
        at = pl.ds(pl.multiple_of((own ^ s) * LANES, LANES), LANES)
        for i in range(3):
            outs[i][:, at] = pieces[s][i]


def adapter_grads_body(half, strips, slot, wide, pos_ref, in_ref, up_ref, down_ref):
    core = pos_ref[2]
    planes = in_ref.shape[0] // half
    width = slot // strips
    step = half * width
    for j in range(half):
        total = in_ref[j]
        for p in range(1, planes):
            total = total + in_ref[p * half + j]
        for i in range(strips):
            to = i * step + j * width
            up_ref[:, to : to + width] = total[:, i * width : (i + 1) * width]
        head = j ^ ((core & 1) * (half // 2))
        down_ref[:, pl.ds(pl.multiple_of(head * LANES, LANES), LANES)] = total[:, wide:]


def adapters_body(half, fsdp, planes, pos_ref, o_ref, *refs):
    both, grads = refs[:fsdp], refs[fsdp : fsdp + half]
    out_ref, scr = refs[fsdp + half :]
    mine, plane, core = pos_ref[0], pos_ref[1], pos_ref[2]
    rank_rows = out_ref.shape[1]
    rank = planes * half * rank_rows
    rows, wide = grads[0].shape
    part_rows = both[0].shape[0]
    for s in range(fsdp):
        src = lax.rem(core + (fsdp - s), fsdp)
        scr[pl.ds(pl.multiple_of(src * part_rows, part_rows), part_rows), :] = both[s][...]
    acc = None
    for s in range(half):
        at = pl.ds(pl.multiple_of((mine ^ s) * rows, rows), rows)
        part = nn(scr[at, :].T[rank:, :], grads[s][...])
        acc = part if acc is None else acc + part
    acc = adapter_scale * acc
    low = nn(scr[...].T[:rank, :], o_ref[...].astype(BF))
    for p in range(planes):
        for j in range(half):
            at = (p * half + j) * rank_rows
            to = lax.rem(plane + (planes - p), planes) * half + j
            out_ref[to, :, :wide] = acc[at : at + rank_rows, :]
            out_ref[to, :, wide:] = low[at : at + rank_rows, :]


def on_device(
    sizes,
    rotated_query_rows,
    rotated_key_rows,
    saved_value_rows,
    projection_output_gradient,
    frozen_weight_codes,
    block_scale_index,
    block_scale_table,
    adapter_down_matrix,
    adapter_up_matrix,
):
    n_ctx, fsdp = sizes
    half = HALF_GROUP_DEV
    planes = n_ctx // half
    rows = rotated_query_rows.shape[0]
    heads = rotated_query_rows.shape[1] // HEAD_WIDTH
    assert heads == half
    tokens = rows * half
    w_rows, w_cols = frozen_weight_codes.shape
    grad_cols = projection_output_gradient.shape[1]
    strips = grad_cols // (half * w_rows)
    slot = strips * w_rows
    wide = -(-slot // LANES) * LANES
    rank_rows = adapter_down_matrix.shape[0]
    rank = rank_rows * n_ctx

    def head_of(j, f):
        return j ^ ((f & 1) * (half // 2))

    ctx = lax.axis_index("ctx")
    core = lax.axis_index("fsdp")
    mine = ctx % half
    plane = ctx // half
    own = head_of(mine, core)
    later = jnp.where(own < heads // 2, plane % 2, 1 - plane % 2)
    pos = jnp.stack([mine, plane, core, later, own]).astype(jnp.int32)

    def in_plane(x, s):
        if s == 0:
            return x
        return lax.ppermute(x, "ctx", [(i, i ^ s) for i in range(n_ctx)])

    def along(x, s):
        if s == 0:
            return x
        return lax.ppermute(x, "ctx", [(i, (i + s * half) % n_ctx) for i in range(n_ctx)])

    def from_plane(x, *moves):
        route = []
        for group, step in zip(moves[::2], moves[1::2]):
            for p in group:
                route += [(p * half + j, (p + step) * half + j) for j in range(half)]
        return lax.ppermute(x, "ctx", route)

    def across(x, s):
        if s == 0:
            return x
        return lax.ppermute(x, "fsdp", [(i, (i + s) % fsdp) for i in range(fsdp)])

    pairs = []
    for i in range(n_ctx):
        for f in range(fsdp):
            p, j = divmod(i, half)
            if (p % 2 == 0) == (head_of(j, f) < heads // 2):
                pairs.append((i * fsdp + f, (i + half) % n_ctx * fsdp + f))

    def to_later(x):
        return lax.ppermute(x, ("ctx", "fsdp"), pairs)

    def to_earlier(x):
        return lax.ppermute(x, ("ctx", "fsdp"), [(b, a) for a, b in pairs])

    table = block_scale_table.reshape(-1, LANES)
    index = block_scale_index.T
    weight = call(
        dequant_body,
        sds((w_rows, w_cols), BF),
        [pltpu.VMEM(x.shape, x.dtype) for x in (frozen_weight_codes, index, table)]
        + [pltpu.SemaphoreType.DMA((3,))],
        frozen_weight_codes,
        index,
        table,
        in_hbm=True,
    )
    if planes == 4:
        weights = [weight, along(weight, 1), along(weight, planes - 1)]
    else:
        weights = [along(weight, s) for s in range(planes)]
    if planes == 4:
        inner, outer = call(
            relay_body, [sds(weight.shape, BF)] * 2, [], pos, *weights[1:], n_scalar=1
        )
        weights.append(from_plane(inner, (1,), 1, (2,), -1))
        weights.append(from_plane(outer, (1,), -1, (2,), 1))

    grads = call(
        functools.partial(pack_grad_body, half, strips),
        [sds((rows, wide), BF)] * half,
        [],
        pos,
        projection_output_gradient,
        n_scalar=1,
    )
    grads = [in_plane(x, s) for s, x in enumerate(grads)]
    swapped = [across(g, f) for g in grads for f in range(fsdp)]

    raw_ups = [across(adapter_up_matrix, f) for f in range(fsdp)]
    raw = call(
        functools.partial(raw_body, fsdp),
        [sds((rank_rows, fsdp * grad_cols + heads * HEAD_WIDTH), BF)],
        [pltpu.SemaphoreType.DMA((fsdp + 1,))],
        *raw_ups,
        adapter_down_matrix,
        in_hbm=True,
    )[0]
    raws = [along(raw, s) for s in range(planes)]
    adapter_cols = fsdp * wide + heads * HEAD_WIDTH
    chunks = call(
        functools.partial(chunks_body, half, fsdp, strips, wide),
        [sds((planes, rank_rows, adapter_cols), BF)] * half,
        [],
        pos,
        *raws,
        n_scalar=1,
    )
    chunks = [in_plane(x, s) for s, x in enumerate(chunks)]
    adapters = call(
        functools.partial(ranks_body, half),
        sds((rank, adapter_cols), BF),
        [pltpu.VMEM((half, planes, rank_rows, adapter_cols), F32)],
        pos,
        *chunks,
        n_scalar=1,
    )

    packed = call(
        functools.partial(pack_heads_body, half),
        [sds((3, rows, LANES), BF)] * half,
        [pltpu.VMEM(rotated_query_rows.shape, BF)] * 3 + [pltpu.SemaphoreType.DMA((3,))],
        pos,
        rotated_query_rows,
        rotated_key_rows,
        saved_value_rows,
        n_scalar=1,
        in_hbm=True,
    )
    packed = [in_plane(x, s) for s, x in enumerate(packed)]
    query, key_value = call(
        functools.partial(assemble_body, half),
        [sds((tokens, LANES), BF), sds((2, tokens, LANES), BF)],
        [],
        pos,
        *packed,
        n_scalar=1,
    )
    far = to_later(key_value)
    lora = call(
        functools.partial(lora_body, half, fsdp),
        sds((tokens, rank), F32),
        [],
        pos,
        adapters,
        *swapped,
        n_scalar=1,
    )

    def project(targets):
        return call(
            functools.partial(project_body, half, planes, fsdp, slot, targets),
            [sds((tokens, LANES), BF)] * len(targets),
            [
                pltpu.VMEM((planes * w_rows + wide - slot, LANES * len(targets)), BF),
                pltpu.VMEM((rank, LANES * len(targets)), BF),
            ],
            pos,
            adapters,
            *swapped,
            *weights,
            n_scalar=1,
        )

    first, second = range(half // 2, half), range(half // 2)
    partial = dict(zip(first, project(tuple(first))))
    partial = {s: in_plane(x, s) for s, x in partial.items()}
    rest = dict(zip(second, project(tuple(second))))
    partial.update({s: in_plane(x, s) for s, x in rest.items()})

    part_rows = tokens // fsdp
    out, norm = call(
        forward_body,
        [sds((tokens, LANES), F32), sds((1, tokens), F32)],
        [pltpu.VMEM((LANES, tokens), BF), pltpu.VMEM((LANES, tokens), BF)],
        pos,
        query,
        key_value,
        far,
        n_scalar=1,
    )
    mids = call(
        functools.partial(middle_body, fsdp, wide),
        [sds((part_rows, rank), F32)] * fsdp,
        [],
        pos,
        out,
        adapters,
        n_scalar=1,
    )
    mids = [across(x, f) for f, x in enumerate(mids)]
    both = call(join_body, sds((part_rows, 2 * rank), BF), [], pos, lora, *mids, n_scalar=1)
    both = [in_plane(both, s) for s in range(half)]
    both = call(total_body, sds((part_rows, 2 * rank), BF), [], *both)
    both = [across(both, f) for f in range(fsdp)]
    adapter_grads = call(
        functools.partial(adapters_body, half, fsdp, planes),
        sds((n_ctx, rank_rows, wide + HEAD_WIDTH), F32),
        [pltpu.VMEM((tokens, 2 * rank), BF)],
        pos,
        out,
        *both,
        *grads,
        n_scalar=1,
    )
    reduced = lax.all_to_all(adapter_grads, "ctx", split_axis=0, concat_axis=0, tiled=True)
    up_grad, down_grad = call(
        functools.partial(adapter_grads_body, half, strips, slot, wide),
        [sds((rank_rows, grad_cols), F32), sds((rank_rows, heads * HEAD_WIDTH), F32)],
        [],
        pos,
        reduced,
        n_scalar=1,
    )

    far_part, dq_far, grad_out, delta = call(
        functools.partial(far_body, half),
        [
            sds((2, tokens, LANES), BF),
            sds((LANES, tokens), F32),
            sds((tokens, LANES), BF),
            sds((1, tokens), F32),
        ],
        [pltpu.VMEM((LANES, tokens), BF)],
        pos,
        *[partial[s] for s in range(half)],
        query,
        far,
        out,
        norm,
        n_scalar=1,
    )
    back = to_earlier(far_part)
    dq, near = call(
        near_body,
        [sds((tokens, LANES), BF), sds((2, tokens, LANES), F32)],
        [pltpu.VMEM((LANES, tokens), BF)],
        pos,
        query,
        key_value,
        grad_out,
        norm,
        delta,
        dq_far,
        n_scalar=1,
    )
    merged = call(
        functools.partial(merge_body, half),
        [sds((3, rows, LANES), BF)] * half,
        [],
        pos,
        dq,
        near,
        back,
        n_scalar=1,
    )
    merged = [in_plane(x, s) for s, x in enumerate(merged)]
    query_grad, key_grad, value_grad = call(
        functools.partial(unpack_body, half),
        [sds((rows, heads * HEAD_WIDTH), BF)] * 3,
        [],
        pos,
        *merged,
        n_scalar=1,
    )
    return query_grad, key_grad, value_grad, down_grad, up_grad


def solution(mesh):
    split = P("ctx", "fsdp")
    in_specs = (split,) * 6 + (P(),) + (split,) * 2

    def body(*args):
        return on_device((mesh.shape["ctx"], mesh.shape["fsdp"]), *args)

    return jax.shard_map(
        body, mesh=mesh, in_specs=in_specs, out_specs=(split,) * 5, check_vma=False
    )
```

```python
import functools

import jax
import jax.numpy as jnp
from jax import lax
from jax.experimental import pallas as pl
from jax.experimental.pallas import tpu as pltpu
from jax.sharding import PartitionSpec as P

HEAD_WIDTH = 128
HALF_GROUP_DEV = 4
LANES = 128
QUERY_BLOCK = 256
KERNEL_VMEM = 16 << 20

nf4_values = (
    -1.0,
    -0.6961928009986877,
    -0.5250730514526367,
    -0.39491748809814453,
    -0.28444138169288635,
    -0.18477343022823334,
    -0.09105003625154495,
    0.0,
    0.07958029955625534,
    0.16093020141124725,
    0.24611230194568634,
    0.33791524171829224,
    0.44070982933044434,
    0.5626170039176941,
    0.7229568362236023,
    1.0,
)
adapter_scale = 0.25
masked = -1e30


BF = jnp.bfloat16
F32 = jnp.float32
VM = pl.BlockSpec(memory_space=pltpu.VMEM)
SM = pl.BlockSpec(memory_space=pltpu.SMEM)
HB = pl.BlockSpec(memory_space=pltpu.HBM)


def sds(shape, dtype):
    return jax.ShapeDtypeStruct(shape, dtype)


def nt(a, b):
    return lax.dot_general(a, b, (((1,), (1,)), ((), ())), preferred_element_type=F32)


def nn(a, b):
    return jnp.dot(a, b, preferred_element_type=F32)


def call(body, outs, scratch, *args, n_scalar=0, in_hbm=False):
    if in_hbm:
        args = args[:n_scalar] + tuple(
            pltpu.with_memory_space_constraint(x, pltpu.HBM) for x in args[n_scalar:]
        )
    spec = HB if in_hbm else VM
    return pl.pallas_call(
        body,
        out_shape=outs,
        in_specs=[SM] * n_scalar + [spec] * (len(args) - n_scalar),
        out_specs=jax.tree.map(lambda _: VM, outs),
        scratch_shapes=scratch,
        compiler_params=pltpu.CompilerParams(vmem_limit_bytes=KERNEL_VMEM),
    )(*args)


def fetch(sources, targets, sem):
    copies = [
        pltpu.make_async_copy(src, to, sem.at[i])
        for i, (src, to) in enumerate(zip(sources, targets))
    ]
    for copy in copies:
        copy.start()
    for copy in copies:
        copy.wait()


def dequant_body(codes_in, index_in, table_in, out_ref, codes_ref, index_ref, table_ref, sem):
    fetch((codes_in, index_in, table_in), (codes_ref, index_ref, table_ref), sem)
    rows, cols = codes_ref.shape
    groups = index_ref.shape[0]
    parts = table_ref.shape[0]
    per_tile = groups * LANES // cols
    width = LANES // per_tile
    tables = [jnp.broadcast_to(table_ref[i : i + 1, :], (groups, LANES)) for i in range(parts)]
    scales = []
    for r0 in range(0, rows, LANES):
        idx = index_ref[:, r0 : min(r0 + LANES, rows)]
        short = LANES - idx.shape[1]
        if short:
            idx = jnp.concatenate([idx, jnp.zeros((groups, short), jnp.int32)], axis=1)
        low = idx % LANES
        scale = jnp.take_along_axis(tables[0], low, axis=1)
        for i in range(1, parts):
            scale = jnp.where(
                idx >= i * LANES, jnp.take_along_axis(tables[i], low, axis=1), scale
            )
        scales.append(scale)
    scales = jnp.concatenate(scales, axis=1).T[:rows, :]
    lane = lax.broadcasted_iota(jnp.int32, (rows, LANES), 1)
    place = lax.broadcasted_iota(jnp.int32, (8, LANES), 1)
    levels = jnp.zeros((8, LANES), F32)
    for i, level in enumerate(nf4_values):
        levels = jnp.where(place == i, level, levels)
    levels = jnp.broadcast_to(levels[:1], (rows, LANES))
    for b in range(cols // LANES):
        code = codes_ref[:, b * LANES : (b + 1) * LANES]
        value = jnp.take_along_axis(levels, code, axis=1)
        at = b * per_tile
        scale = jnp.broadcast_to(scales[:, at : at + 1], (rows, LANES))
        for i in range(1, per_tile):
            scale = jnp.where(lane >= i * width, scales[:, at + i : at + i + 1], scale)
        out_ref[:, b * LANES : (b + 1) * LANES] = (value * scale).astype(BF)


def relay_body(pos_ref, above_ref, below_ref, inner_ref, outer_ref):
    @pl.when(pos_ref[1] == 1)
    def _():
        inner_ref[...] = above_ref[...]
        outer_ref[...] = below_ref[...]

    @pl.when(pos_ref[1] != 1)
    def _():
        inner_ref[...] = below_ref[...]
        outer_ref[...] = above_ref[...]


def pack_body(half, strips, wide, pos_ref, *refs):
    ins, outs, chunks = refs[:6], refs[6 : 6 + half], refs[6 + half : 6 + 2 * half]
    scr, sem = refs[6 + 2 * half : -1], refs[-1]
    fetch(ins, scr, sem)
    mine, own = pos_ref[0], pos_ref[4]
    up_ref, down_ref = scr[4], scr[5]
    step = up_ref.shape[1] // strips
    width = step // half
    short = wide - strips * width

    def strip(ref, jv):
        pieces = [ref[:, i * step + jv * width : i * step + (jv + 1) * width] for i in range(strips)]
        if short:
            pieces.append(jnp.zeros((ref.shape[0], short), BF))
        return jnp.concatenate(pieces, axis=1)

    for s in range(half):
        out, chunk = outs[s], chunks[s]
        cols = pl.ds(pl.multiple_of((own ^ s) * LANES, LANES), LANES)
        for i in range(3):
            out[:, wide + i * LANES : wide + (i + 1) * LANES] = scr[i][:, cols]
        chunk[:, wide:] = down_ref[...]
        for jv in range(half):

            @pl.when((mine ^ s) == jv)
            def _(out=out, chunk=chunk, jv=jv):
                out[:, :wide] = strip(scr[3], jv)
                chunk[:, :wide] = strip(up_ref, jv)


def stack_body(half, pos_ref, *refs):
    for s in range(half):
        refs[half][pos_ref[0] ^ s] = refs[s][...]


def assemble_body(half, wide, pos_ref, *refs):
    pieces, (q_out, kv_out) = refs[:half], refs[half:]
    mine = pos_ref[0]
    rows = pieces[0].shape[0]
    for s in range(half):
        at = pl.ds(pl.multiple_of((mine ^ s) * rows, rows), rows)
        q_out[at, :] = pieces[s][:, wide : wide + LANES]
        kv_out[0, at, :] = pieces[s][:, wide + LANES : wide + 2 * LANES]
        kv_out[1, at, :] = pieces[s][:, wide + 2 * LANES :]


def ranks_body(*refs):
    parts = [ref[j].astype(F32) for ref in refs[:-1] for j in range(ref.shape[0])]
    refs[-1][...] = jnp.concatenate(parts, axis=0).astype(BF)


def lora_body(half, fsdp, wide, pos_ref, *refs):
    adapts, grads, out_ref = refs[:fsdp], refs[fsdp:-1], refs[-1]
    mine, core = pos_ref[0], pos_ref[2]
    rows = grads[0].shape[0]

    def write(pieces):
        total = None
        for f in range(fsdp):
            left = jnp.concatenate([grads[s * fsdp + f][:, :wide] for s in pieces], axis=0)
            part = nt(left, adapts[f][:, :wide])
            total = part if total is None else total + part
        total = adapter_scale * total
        for i, s in enumerate(pieces):
            at = pl.ds(pl.multiple_of((mine ^ s) * rows, rows), rows)
            out_ref[at, :] = total[i * rows : (i + 1) * rows, :]

    if fsdp == 2:
        for first in range(0, half, 2):

            @pl.when((mine ^ first) // 2 == core)
            def _(first=first):
                write((first, first + 1))

    else:
        write(tuple(range(half)))


def join_body(pos_ref, lora_ref, *refs):
    mids, out_ref = refs[:-1], refs[-1]
    rows = out_ref.shape[0]
    mid = mids[0][...]
    for m in mids[1:]:
        mid = mid + m[...]
    lora = lora_ref[pl.ds(pl.multiple_of(pos_ref[2] * rows, rows), rows), :]
    out_ref[...] = jnp.concatenate([lora, mid], axis=1).astype(BF)


def total_body(*refs):
    total = refs[0][...].astype(F32)
    for ref in refs[1:-1]:
        total = total + ref[...].astype(F32)
    refs[-1][...] = total.astype(BF)


def project_body(half, planes, fsdp, slot, wide, targets, pos_ref, *refs):
    adapts, refs = refs[:fsdp], refs[fsdp:]
    grads = refs[: half * fsdp]
    weights = refs[half * fsdp : -2 - len(targets)]
    n_weights = len(weights)
    outs = refs[-2 - len(targets) : -2]
    w_scr, d_scr = refs[-2:]
    mine, plane, core, own = pos_ref[0], pos_ref[1], pos_ref[2], pos_ref[4]
    rows_each = weights[0].shape[0]
    rows = grads[0].shape[0]
    tail = w_scr.shape[0] - planes * rows_each
    if tail:
        w_scr[planes * rows_each :, :] = jnp.zeros((tail, w_scr.shape[1]), BF)
    for i, t in enumerate(targets):
        cols = pl.ds(pl.multiple_of((own ^ t) * LANES, LANES), LANES)
        d_cols = pl.ds(pl.multiple_of(wide + (own ^ t) * LANES, LANES), LANES)
        to = slice(i * LANES, (i + 1) * LANES)
        d_scr[:, to] = adapts[0][:, d_cols]
        if n_weights == planes:
            sources = [lax.rem(plane + (planes - s), planes) for s in range(planes)]
        else:
            away = lax.rem(plane + 2, planes)
            inside = (plane == 1) | (plane == 2)
            sources = [plane, lax.rem(plane + planes - 1, planes), lax.rem(plane + 1, planes)]
            sources += [jnp.where(inside, away, -1), jnp.where(inside, -1, away)]
        for piece, src in zip(weights, sources):

            @pl.when(src >= 0)
            def _(piece=piece, src=src, to=to, cols=cols):
                at = pl.ds(pl.multiple_of(src * rows_each, rows_each), rows_each)
                w_scr[at, to] = piece[:, cols]

    for f in range(fsdp):
        src = lax.rem(core + (fsdp - f), fsdp)
        at = pl.ds(pl.multiple_of(src * slot, 16), slot)
        up = adapts[f][:, :wide]
        low = lax.dot_general(
            up, d_scr[...], (((0,), (0,)), ((), ())), preferred_element_type=F32
        )
        w_scr[at, :] = (w_scr[at, :].astype(F32) + adapter_scale * low[:slot]).astype(BF)
    acc = None
    for f in range(fsdp):
        src = lax.rem(core + (fsdp - f), fsdp)
        w_at = pl.ds(pl.multiple_of(src * slot, 16), wide)
        left = jnp.concatenate([grads[s * fsdp + f][:, :wide] for s in range(half)], axis=0)
        part = nn(left, w_scr[w_at, :])
        acc = part if acc is None else acc + part
    for s in range(half):
        at = pl.ds(pl.multiple_of((mine ^ s) * rows, rows), rows)
        for i in range(len(targets)):
            block = acc[s * rows : (s + 1) * rows, i * LANES : (i + 1) * LANES]
            outs[i][at, :] = block.astype(BF)


def score_block(key, query, k0, q0):
    scores = nt(key, query) * (HEAD_WIDTH**-0.5)
    if k0 is None or k0 + key.shape[0] - 1 <= q0:
        return scores
    kpos = k0 + lax.broadcasted_iota(jnp.int32, scores.shape, 0)
    qpos = q0 + lax.broadcasted_iota(jnp.int32, scores.shape, 1)
    return jnp.where(kpos <= qpos, scores, masked)


def forward_body(fsdp, wide, pos_ref, q_ref, kv_ref, far_ref, adapt_ref, o_ref, lse_ref, *refs):
    mid_refs, (vt_scr, oft_scr) = refs[:fsdp], refs[fsdp:]
    core, later, own = pos_ref[2], pos_ref[3], pos_ref[4]
    tokens = q_ref.shape[0]
    block = min(QUERY_BLOCK, tokens)
    vt_scr[...] = kv_ref[1].T

    def finish(q0, block_out, norm):
        qs = slice(q0, q0 + block)
        o_ref[qs, :] = block_out.T
        lse_ref[:, qs] = norm

    def near(q0):
        return score_block(kv_ref[0, : q0 + block, :], q_ref[q0 : q0 + block, :], 0, q0)

    @pl.when(later == 0)
    def _():
        for q0 in range(0, tokens, block):
            scores = near(q0)
            top = jnp.max(scores, axis=0, keepdims=True)
            prob = jnp.exp(scores - top)
            total = jnp.sum(prob, axis=0, keepdims=True)
            out = nn(vt_scr[:, : q0 + block], prob.astype(BF)) / total
            finish(q0, out, top + jnp.log(total))

    @pl.when(later != 0)
    def _():
        oft_scr[...] = far_ref[1].T
        for q0 in range(0, tokens, block):
            scores = near(q0)
            far = score_block(far_ref[0], q_ref[q0 : q0 + block, :], None, q0)
            top = jnp.maximum(
                jnp.max(scores, axis=0, keepdims=True), jnp.max(far, axis=0, keepdims=True)
            )
            prob = jnp.exp(scores - top)
            far_prob = jnp.exp(far - top)
            total = jnp.sum(prob, axis=0, keepdims=True) + jnp.sum(far_prob, axis=0, keepdims=True)
            out = nn(vt_scr[:, : q0 + block], prob.astype(BF)) + nn(
                oft_scr[...], far_prob.astype(BF)
            )
            finish(q0, out / total, top + jnp.log(total))

    down = adapt_ref[:, pl.ds(pl.multiple_of(wide + own * LANES, LANES), LANES)]
    rows = tokens // fsdp
    for s in range(fsdp):
        to = lax.rem(core + s, fsdp)
        part = o_ref[pl.ds(pl.multiple_of(to * rows, rows), rows), :]
        mid_refs[s][...] = nt(part.astype(BF), down)


def grad_block(key, value, query, grad, norm, delta, k0, q0):
    prob = jnp.exp(score_block(key, query, k0, q0) - norm)
    prob_grad = nt(value, grad)
    score_grad = prob * (prob_grad - delta) * (HEAD_WIDTH**-0.5)
    return prob.astype(BF), score_grad.astype(BF)


def far_body(half, pos_ref, *refs):
    parts = refs[:half]
    q_ref, far_ref, o_ref, norm_ref = refs[half : half + 4]
    far_out, dq_ref, do_ref, delta_ref, kt_scr = refs[half + 4 :]
    later = pos_ref[3]
    tokens = q_ref.shape[0]
    block = min(QUERY_BLOCK, tokens)
    total = parts[0][...].astype(F32)
    for s in range(1, half):
        total = total + parts[s][...].astype(F32)
    grad = total.astype(BF)
    do_ref[...] = grad
    delta_ref[...] = jnp.sum((grad.astype(F32) * o_ref[...]).T, axis=0, keepdims=True)

    @pl.when(later != 0)
    def _():
        kt_scr[...] = far_ref[0].T
        for k0 in range(0, tokens, block):
            ks = slice(k0, k0 + block)
            prob, score_grad = grad_block(
                far_ref[0, ks, :],
                far_ref[1, ks, :],
                q_ref[...],
                do_ref[...],
                norm_ref[...],
                delta_ref[...],
                None,
                0,
            )
            far_out[0, ks, :] = nn(score_grad, q_ref[...]).astype(BF)
            far_out[1, ks, :] = nn(prob, do_ref[...]).astype(BF)
            part = nn(kt_scr[:, ks], score_grad)
            if k0:
                dq_ref[...] += part
            else:
                dq_ref[...] = part

    @pl.when(later == 0)
    def _():
        far_out[...] = jnp.zeros(far_out.shape, BF)
        dq_ref[...] = jnp.zeros(dq_ref.shape, F32)


def near_body(pos_ref, q_ref, kv_ref, do_ref, norm_ref, delta_ref, dq_in, dq_ref, near_ref, kt_scr):
    tokens = q_ref.shape[0]
    block = min(QUERY_BLOCK, tokens)
    kt_scr[...] = kv_ref[0].T
    for q0 in range(0, tokens, block):
        qs = slice(q0, q0 + block)
        depth = q0 + block
        prob, score_grad = grad_block(
            kv_ref[0, :depth, :],
            kv_ref[1, :depth, :],
            q_ref[qs, :],
            do_ref[qs, :],
            norm_ref[:, qs],
            delta_ref[:, qs],
            0,
            q0,
        )
        dk = nn(score_grad, q_ref[qs, :])
        dv = nn(prob, do_ref[qs, :])
        if q0:
            near_ref[0, :q0, :] += dk[:q0]
            near_ref[1, :q0, :] += dv[:q0]
        near_ref[0, qs, :] = dk[q0:]
        near_ref[1, qs, :] = dv[q0:]
        dq = dq_in[:, qs] + nn(kt_scr[:, :depth], score_grad)
        dq_ref[qs, :] = dq.T.astype(BF)


def merge_body(half, pos_ref, dq_ref, near_ref, back_ref, *out_refs):
    mine = pos_ref[0]
    rows = near_ref.shape[1] // half
    for s in range(half):
        at = pl.ds(pl.multiple_of((mine ^ s) * rows, rows), rows)
        out_refs[s][0] = dq_ref[at, :]
        for i in range(2):
            merged = near_ref[i, at, :] + back_ref[i, at, :].astype(F32)
            out_refs[s][1 + i] = merged.astype(BF)


def unpack_body(half, pos_ref, *refs):
    pieces, outs = refs[:half], refs[half:]
    own = pos_ref[4]
    for s in range(half):
        at = pl.ds(pl.multiple_of((own ^ s) * LANES, LANES), LANES)
        for i in range(3):
            outs[i][:, at] = pieces[s][i]


def adapter_grads_body(half, strips, slot, wide, pos_ref, in_ref, up_ref, down_ref):
    core = pos_ref[2]
    planes = in_ref.shape[0] // half
    width = slot // strips
    step = half * width
    for j in range(half):
        total = in_ref[j]
        for p in range(1, planes):
            total = total + in_ref[p * half + j]
        for i in range(strips):
            to = i * step + j * width
            up_ref[:, to : to + width] = total[:, i * width : (i + 1) * width]
        head = j ^ ((core & 1) * (half // 2))
        down_ref[:, pl.ds(pl.multiple_of(head * LANES, LANES), LANES)] = total[:, wide:]


def adapters_body(half, fsdp, planes, wide, pos_ref, o_ref, *refs):
    both, grads = refs[:fsdp], refs[fsdp : fsdp + half]
    out_ref, scr = refs[fsdp + half :]
    mine, plane, core = pos_ref[0], pos_ref[1], pos_ref[2]
    rank_rows = out_ref.shape[1]
    rank = planes * half * rank_rows
    rows = grads[0].shape[0]
    part_rows = both[0].shape[0]
    for s in range(fsdp):
        src = lax.rem(core + (fsdp - s), fsdp)
        scr[pl.ds(pl.multiple_of(src * part_rows, part_rows), part_rows), :] = both[s][...]
    acc = None
    for s in range(half):
        at = pl.ds(pl.multiple_of((mine ^ s) * rows, rows), rows)
        part = nn(scr[at, :].T[rank:, :], grads[s][:, :wide])
        acc = part if acc is None else acc + part
    acc = adapter_scale * acc
    low = nn(scr[...].T[:rank, :], o_ref[...].astype(BF))
    for p in range(planes):
        for j in range(half):
            at = (p * half + j) * rank_rows
            to = lax.rem(plane + (planes - p), planes) * half + j
            out_ref[to, :, :wide] = acc[at : at + rank_rows, :]
            out_ref[to, :, wide:] = low[at : at + rank_rows, :]


def on_device(
    sizes,
    rotated_query_rows,
    rotated_key_rows,
    saved_value_rows,
    projection_output_gradient,
    frozen_weight_codes,
    block_scale_index,
    block_scale_table,
    adapter_down_matrix,
    adapter_up_matrix,
):
    n_ctx, fsdp = sizes
    half = HALF_GROUP_DEV
    planes = n_ctx // half
    rows = rotated_query_rows.shape[0]
    heads = rotated_query_rows.shape[1] // HEAD_WIDTH
    assert heads == half
    tokens = rows * half
    w_rows, w_cols = frozen_weight_codes.shape
    grad_cols = projection_output_gradient.shape[1]
    strips = grad_cols // (half * w_rows)
    slot = strips * w_rows
    wide = -(-slot // LANES) * LANES
    rank_rows = adapter_down_matrix.shape[0]
    rank = rank_rows * n_ctx

    def head_of(j, f):
        return j ^ ((f & 1) * (half // 2))

    ctx = lax.axis_index("ctx")
    core = lax.axis_index("fsdp")
    mine = ctx % half
    plane = ctx // half
    own = head_of(mine, core)
    later = jnp.where(own < heads // 2, plane % 2, 1 - plane % 2)
    pos = jnp.stack([mine, plane, core, later, own]).astype(jnp.int32)

    def in_plane(x, s):
        if s == 0:
            return x
        return lax.ppermute(x, "ctx", [(i, i ^ s) for i in range(n_ctx)])

    def along(x, s):
        if s == 0:
            return x
        return lax.ppermute(x, "ctx", [(i, (i + s * half) % n_ctx) for i in range(n_ctx)])

    def from_plane(x, *moves):
        route = []
        for group, step in zip(moves[::2], moves[1::2]):
            for p in group:
                route += [(p * half + j, (p + step) * half + j) for j in range(half)]
        return lax.ppermute(x, "ctx", route)

    def across(x, s):
        if s == 0:
            return x
        return lax.ppermute(x, "fsdp", [(i, (i + s) % fsdp) for i in range(fsdp)])

    pairs = []
    for i in range(n_ctx):
        for f in range(fsdp):
            p, j = divmod(i, half)
            if (p % 2 == 0) == (head_of(j, f) < heads // 2):
                pairs.append((i * fsdp + f, (i + half) % n_ctx * fsdp + f))

    def to_later(x):
        return lax.ppermute(x, ("ctx", "fsdp"), pairs)

    def to_earlier(x):
        return lax.ppermute(x, ("ctx", "fsdp"), [(b, a) for a, b in pairs])

    table = block_scale_table.reshape(-1, LANES)
    index = block_scale_index.T
    weight = call(
        dequant_body,
        sds((w_rows, w_cols), BF),
        [pltpu.VMEM(x.shape, x.dtype) for x in (frozen_weight_codes, index, table)]
        + [pltpu.SemaphoreType.DMA((3,))],
        frozen_weight_codes,
        index,
        table,
        in_hbm=True,
    )
    if planes == 4:
        weights = [weight]
        for s in (1, planes - 1):
            weights.append(along(weight, s))
    else:
        weights = [along(weight, s) for s in range(planes)]
    if planes == 4:
        inner, outer = call(
            relay_body, [sds(weight.shape, BF)] * 2, [], pos, *weights[1:], n_scalar=1
        )
        weights.append(from_plane(inner, (1,), 1, (2,), -1))
        weights.append(from_plane(outer, (1,), -1, (2,), 1))

    adapter_cols = wide + heads * HEAD_WIDTH
    sources = (
        rotated_query_rows,
        rotated_key_rows,
        saved_value_rows,
        projection_output_gradient,
        adapter_up_matrix,
        adapter_down_matrix,
    )
    packed = call(
        functools.partial(pack_body, half, strips, wide),
        [sds((rows, wide + 3 * LANES), BF)] * half + [sds((rank_rows, adapter_cols), BF)] * half,
        [pltpu.VMEM(x.shape, BF) for x in sources] + [pltpu.SemaphoreType.DMA((6,))],
        pos,
        *sources,
        n_scalar=1,
        in_hbm=True,
    )
    chunks = [in_plane(x, s) for s, x in enumerate(packed[half:])]
    packed = [in_plane(x, s) for s, x in enumerate(packed[:half])]
    swapped = [across(g, f) for g in packed for f in range(fsdp)]
    adapters = call(
        functools.partial(stack_body, half),
        sds((half, rank_rows, adapter_cols), BF),
        [],
        pos,
        *chunks,
        n_scalar=1,
    )
    adapters = [along(adapters, s) for s in range(planes)]
    adapters = call(ranks_body, sds((rank, adapter_cols), BF), [], *adapters)
    adapts = [across(adapters, f) for f in range(fsdp)]

    query, key_value = call(
        functools.partial(assemble_body, half, wide),
        [sds((tokens, LANES), BF), sds((2, tokens, LANES), BF)],
        [],
        pos,
        *packed,
        n_scalar=1,
    )
    far = to_later(key_value)
    lora = call(
        functools.partial(lora_body, half, fsdp, wide),
        sds((tokens, rank), F32),
        [],
        pos,
        *adapts,
        *swapped,
        n_scalar=1,
    )

    def project(targets):
        return call(
            functools.partial(project_body, half, planes, fsdp, slot, wide, targets),
            [sds((tokens, LANES), BF)] * len(targets),
            [
                pltpu.VMEM((planes * w_rows + wide - slot, LANES * len(targets)), BF),
                pltpu.VMEM((rank, LANES * len(targets)), BF),
            ],
            pos,
            *adapts,
            *swapped,
            *weights,
            n_scalar=1,
        )

    first, second = range(half // 2, half), range(half // 2)
    partial = dict(zip(first, project(tuple(first))))
    partial = {s: in_plane(x, s) for s, x in partial.items()}
    rest = dict(zip(second, project(tuple(second))))
    partial.update({s: in_plane(x, s) for s, x in rest.items()})

    part_rows = tokens // fsdp
    out, norm, *mids = call(
        functools.partial(forward_body, fsdp, wide),
        [sds((tokens, LANES), F32), sds((1, tokens), F32)]
        + [sds((part_rows, rank), F32)] * fsdp,
        [pltpu.VMEM((LANES, tokens), BF), pltpu.VMEM((LANES, tokens), BF)],
        pos,
        query,
        key_value,
        far,
        adapters,
        n_scalar=1,
    )
    mids = [across(x, f) for f, x in enumerate(mids)]
    both = call(join_body, sds((part_rows, 2 * rank), BF), [], pos, lora, *mids, n_scalar=1)
    both = [in_plane(both, s) for s in range(half)]
    both = call(total_body, sds((part_rows, 2 * rank), BF), [], *both)
    both = [across(both, f) for f in range(fsdp)]
    adapter_grads = call(
        functools.partial(adapters_body, half, fsdp, planes, wide),
        sds((n_ctx, rank_rows, wide + HEAD_WIDTH), F32),
        [pltpu.VMEM((tokens, 2 * rank), BF)],
        pos,
        out,
        *both,
        *packed,
        n_scalar=1,
    )
    reduced = lax.all_to_all(adapter_grads, "ctx", split_axis=0, concat_axis=0, tiled=True)
    up_grad, down_grad = call(
        functools.partial(adapter_grads_body, half, strips, slot, wide),
        [sds((rank_rows, grad_cols), F32), sds((rank_rows, heads * HEAD_WIDTH), F32)],
        [],
        pos,
        reduced,
        n_scalar=1,
    )

    far_part, dq_far, grad_out, delta = call(
        functools.partial(far_body, half),
        [
            sds((2, tokens, LANES), BF),
            sds((LANES, tokens), F32),
            sds((tokens, LANES), BF),
            sds((1, tokens), F32),
        ],
        [pltpu.VMEM((LANES, tokens), BF)],
        pos,
        *[partial[s] for s in range(half)],
        query,
        far,
        out,
        norm,
        n_scalar=1,
    )
    back = to_earlier(far_part)
    dq, near = call(
        near_body,
        [sds((tokens, LANES), BF), sds((2, tokens, LANES), F32)],
        [pltpu.VMEM((LANES, tokens), BF)],
        pos,
        query,
        key_value,
        grad_out,
        norm,
        delta,
        dq_far,
        n_scalar=1,
    )
    merged = call(
        functools.partial(merge_body, half),
        [sds((3, rows, LANES), BF)] * half,
        [],
        pos,
        dq,
        near,
        back,
        n_scalar=1,
    )
    merged = [in_plane(x, s) for s, x in enumerate(merged)]
    query_grad, key_grad, value_grad = call(
        functools.partial(unpack_body, half),
        [sds((rows, heads * HEAD_WIDTH), BF)] * 3,
        [],
        pos,
        *merged,
        n_scalar=1,
    )
    return query_grad, key_grad, value_grad, down_grad, up_grad


def solution(mesh):
    split = P("ctx", "fsdp")
    in_specs = (split,) * 6 + (P(),) + (split,) * 2

    def body(*args):
        return on_device((mesh.shape["ctx"], mesh.shape["fsdp"]), *args)

    return jax.shard_map(
        body, mesh=mesh, in_specs=in_specs, out_specs=(split,) * 5, check_vma=False
    )
```

```python
import functools

import jax
import jax.numpy as jnp
from jax import lax
from jax.experimental import pallas as pl
from jax.experimental.pallas import tpu as pltpu
from jax.sharding import PartitionSpec as P

HEAD_WIDTH = 128
HALF_GROUP_DEV = 4
LANES = 128
QUERY_BLOCK = 256
FORWARD_BLOCK = 384
SCORE_SCALE = HEAD_WIDTH**-0.5
KERNEL_VMEM = 16 << 20

nf4_values = (
    -1.0,
    -0.6961928009986877,
    -0.5250730514526367,
    -0.39491748809814453,
    -0.28444138169288635,
    -0.18477343022823334,
    -0.09105003625154495,
    0.0,
    0.07958029955625534,
    0.16093020141124725,
    0.24611230194568634,
    0.33791524171829224,
    0.44070982933044434,
    0.5626170039176941,
    0.7229568362236023,
    1.0,
)
adapter_scale = 0.25
masked = -1e30


BF = jnp.bfloat16
F32 = jnp.float32
VM = pl.BlockSpec(memory_space=pltpu.VMEM)
SM = pl.BlockSpec(memory_space=pltpu.SMEM)
HB = pl.BlockSpec(memory_space=pltpu.HBM)


def sds(shape, dtype):
    return jax.ShapeDtypeStruct(shape, dtype)


def nt(a, b):
    return lax.dot_general(a, b, (((1,), (1,)), ((), ())), preferred_element_type=F32)


def nn(a, b):
    return jnp.dot(a, b, preferred_element_type=F32)


def call(body, outs, scratch, *args, n_scalar=0, in_hbm=False, out_hbm=False):
    if in_hbm:
        args = args[:n_scalar] + tuple(
            pltpu.with_memory_space_constraint(x, pltpu.HBM) for x in args[n_scalar:]
        )
    spec = HB if in_hbm else VM
    return pl.pallas_call(
        body,
        out_shape=outs,
        in_specs=[SM] * n_scalar + [spec] * (len(args) - n_scalar),
        out_specs=jax.tree.map(lambda _: HB if out_hbm else VM, outs),
        scratch_shapes=scratch,
        compiler_params=pltpu.CompilerParams(vmem_limit_bytes=KERNEL_VMEM),
    )(*args)


def fetch(sources, targets, sem):
    copies = [
        pltpu.make_async_copy(src, to, sem.at[i])
        for i, (src, to) in enumerate(zip(sources, targets))
    ]
    for copy in copies:
        copy.start()
    for copy in copies:
        copy.wait()


def dequant_body(codes_in, index_in, table_in, out_ref, codes_ref, index_ref, table_ref, sem):
    fetch((codes_in, index_in, table_in), (codes_ref, index_ref, table_ref), sem)
    rows, cols = codes_ref.shape
    groups = index_ref.shape[0]
    parts = table_ref.shape[0]
    per_tile = groups * LANES // cols
    width = LANES // per_tile
    tables = [jnp.broadcast_to(table_ref[i : i + 1, :], (groups, LANES)) for i in range(parts)]
    scales = []
    for r0 in range(0, rows, LANES):
        idx = index_ref[:, r0 : min(r0 + LANES, rows)]
        short = LANES - idx.shape[1]
        if short:
            idx = jnp.concatenate([idx, jnp.zeros((groups, short), jnp.int32)], axis=1)
        low = idx % LANES
        scale = jnp.take_along_axis(tables[0], low, axis=1)
        for i in range(1, parts):
            scale = jnp.where(
                idx >= i * LANES, jnp.take_along_axis(tables[i], low, axis=1), scale
            )
        scales.append(scale)
    scales = jnp.concatenate(scales, axis=1).T[:rows, :]
    lane = lax.broadcasted_iota(jnp.int32, (rows, LANES), 1)
    place = lax.broadcasted_iota(jnp.int32, (8, LANES), 1)
    levels = jnp.zeros((8, LANES), F32)
    for i, level in enumerate(nf4_values):
        levels = jnp.where(place == i, level, levels)
    levels = jnp.broadcast_to(levels[:1], (rows, LANES))
    for b in range(cols // LANES):
        code = codes_ref[:, b * LANES : (b + 1) * LANES]
        value = jnp.take_along_axis(levels, code, axis=1)
        at = b * per_tile
        scale = jnp.broadcast_to(scales[:, at : at + 1], (rows, LANES))
        for i in range(1, per_tile):
            scale = jnp.where(lane >= i * width, scales[:, at + i : at + i + 1], scale)
        out_ref[:, b * LANES : (b + 1) * LANES] = (value * scale).astype(BF)


def relay_body(pos_ref, above_ref, below_ref, inner_ref, outer_ref):
    @pl.when(pos_ref[1] == 1)
    def _():
        inner_ref[...] = above_ref[...]
        outer_ref[...] = below_ref[...]

    @pl.when(pos_ref[1] != 1)
    def _():
        inner_ref[...] = below_ref[...]
        outer_ref[...] = above_ref[...]


def pack_body(half, strips, wide, pos_ref, *refs):
    ins, outs, chunks = refs[:6], refs[6 : 6 + half], refs[6 + half : 6 + 2 * half]
    scr, sem = refs[6 + 2 * half : -1], refs[-1]
    fetch(ins, scr, sem)
    mine, own = pos_ref[0], pos_ref[4]
    up_ref, down_ref = scr[4], scr[5]
    step = up_ref.shape[1] // strips
    width = step // half
    short = wide - strips * width

    def strip(ref, jv):
        pieces = [ref[:, i * step + jv * width : i * step + (jv + 1) * width] for i in range(strips)]
        if short:
            pieces.append(jnp.zeros((ref.shape[0], short), BF))
        return jnp.concatenate(pieces, axis=1)

    for s in range(half):
        out, chunk = outs[s], chunks[s]
        cols = pl.ds(pl.multiple_of((own ^ s) * LANES, LANES), LANES)
        for i in range(3):
            out[:, wide + i * LANES : wide + (i + 1) * LANES] = scr[i][:, cols]
        chunk[:, wide:] = down_ref[...]
        for jv in range(half):

            @pl.when((mine ^ s) == jv)
            def _(out=out, chunk=chunk, jv=jv):
                out[:, :wide] = strip(scr[3], jv)
                chunk[:, :wide] = strip(up_ref, jv)


def stack_body(half, pos_ref, *refs):
    for s in range(half):
        refs[half][pos_ref[0] ^ s] = refs[s][...]


def assemble_body(half, wide, pos_ref, *refs):
    pieces, (q_out, kv_out) = refs[:half], refs[half:]
    mine = pos_ref[0]
    rows = pieces[0].shape[0]
    for s in range(half):
        at = pl.ds(pl.multiple_of((mine ^ s) * rows, rows), rows)
        q_out[at, :] = pieces[s][:, wide : wide + LANES]
        kv_out[0, at, :] = pieces[s][:, wide + LANES : wide + 2 * LANES]
        kv_out[1, at, :] = pieces[s][:, wide + 2 * LANES :]


def ranks_body(*refs):
    parts = [ref[j].astype(F32) for ref in refs[:-1] for j in range(ref.shape[0])]
    refs[-1][...] = jnp.concatenate(parts, axis=0).astype(BF)


def lora_body(half, fsdp, wide, pos_ref, *refs):
    adapts, grads, out_ref = refs[:fsdp], refs[fsdp:-1], refs[-1]
    mine, core = pos_ref[0], pos_ref[2]
    rows = grads[0].shape[0]

    def write(pieces):
        total = None
        for f in range(fsdp):
            left = jnp.concatenate([grads[s * fsdp + f][:, :wide] for s in pieces], axis=0)
            part = nt(left, adapts[f][:, :wide])
            total = part if total is None else total + part
        total = adapter_scale * total
        for i, s in enumerate(pieces):
            at = pl.ds(pl.multiple_of((mine ^ s) * rows, rows), rows)
            out_ref[at, :] = total[i * rows : (i + 1) * rows, :]

    if fsdp == 2:
        for first in range(0, half, 2):

            @pl.when((mine ^ first) // 2 == core)
            def _(first=first):
                write((first, first + 1))

    else:
        write(tuple(range(half)))


def join_body(pos_ref, lora_ref, *refs):
    mids, out_ref = refs[:-1], refs[-1]
    rows = out_ref.shape[0]
    mid = mids[0][...]
    for m in mids[1:]:
        mid = mid + m[...]
    lora = lora_ref[pl.ds(pl.multiple_of(pos_ref[2] * rows, rows), rows), :]
    out_ref[...] = jnp.concatenate([lora, mid], axis=1).astype(BF)


def total_body(*refs):
    total = refs[0][...].astype(F32)
    for ref in refs[1:-1]:
        total = total + ref[...].astype(F32)
    refs[-1][...] = total.astype(BF)


def project_body(half, planes, fsdp, slot, wide, targets, pos_ref, *refs):
    adapts, refs = refs[:fsdp], refs[fsdp:]
    grads = refs[: half * fsdp]
    weights = refs[half * fsdp : -2 - len(targets)]
    n_weights = len(weights)
    outs = refs[-2 - len(targets) : -2]
    w_scr, d_scr = refs[-2:]
    mine, plane, core, own = pos_ref[0], pos_ref[1], pos_ref[2], pos_ref[4]
    rows_each = weights[0].shape[0]
    rows = grads[0].shape[0]
    tail = w_scr.shape[0] - planes * rows_each
    if tail:
        w_scr[planes * rows_each :, :] = jnp.zeros((tail, w_scr.shape[1]), BF)
    for i, t in enumerate(targets):
        cols = pl.ds(pl.multiple_of((own ^ t) * LANES, LANES), LANES)
        d_cols = pl.ds(pl.multiple_of(wide + (own ^ t) * LANES, LANES), LANES)
        to = slice(i * LANES, (i + 1) * LANES)
        d_scr[:, to] = adapts[0][:, d_cols]
        if n_weights == planes:
            sources = [lax.rem(plane + (planes - s), planes) for s in range(planes)]
        else:
            away = lax.rem(plane + 2, planes)
            inside = (plane == 1) | (plane == 2)
            sources = [plane, lax.rem(plane + planes - 1, planes), lax.rem(plane + 1, planes)]
            sources += [jnp.where(inside, away, -1), jnp.where(inside, -1, away)]
        for piece, src in zip(weights, sources):

            @pl.when(src >= 0)
            def _(piece=piece, src=src, to=to, cols=cols):
                at = pl.ds(pl.multiple_of(src * rows_each, rows_each), rows_each)
                w_scr[at, to] = piece[:, cols]

    for f in range(fsdp):
        src = lax.rem(core + (fsdp - f), fsdp)
        at = pl.ds(pl.multiple_of(src * slot, 16), slot)
        up = adapts[f][:, :wide]
        low = lax.dot_general(
            up, d_scr[...], (((0,), (0,)), ((), ())), preferred_element_type=F32
        )
        w_scr[at, :] = (w_scr[at, :].astype(F32) + adapter_scale * low[:slot]).astype(BF)
    acc = None
    for f in range(fsdp):
        src = lax.rem(core + (fsdp - f), fsdp)
        w_at = pl.ds(pl.multiple_of(src * slot, 16), wide)
        left = jnp.concatenate([grads[s * fsdp + f][:, :wide] for s in range(half)], axis=0)
        part = nn(left, w_scr[w_at, :])
        acc = part if acc is None else acc + part
    for s in range(half):
        at = pl.ds(pl.multiple_of((mine ^ s) * rows, rows), rows)
        for i in range(len(targets)):
            block = acc[s * rows : (s + 1) * rows, i * LANES : (i + 1) * LANES]
            outs[i][at, :] = block.astype(BF)


def score_block(key, query, k0, q0):
    scores = nt(key, query) * SCORE_SCALE
    if k0 is None or k0 + key.shape[0] - 1 <= q0:
        return scores
    kpos = k0 + lax.broadcasted_iota(jnp.int32, scores.shape, 0)
    qpos = q0 + lax.broadcasted_iota(jnp.int32, scores.shape, 1)
    return jnp.where(kpos <= qpos, scores, masked)


def near_forward_body(q_ref, kv_ref, acc_ref, top_ref, total_ref, vt_scr):
    tokens = q_ref.shape[0]
    block = min(FORWARD_BLOCK, tokens)
    vt_scr[...] = kv_ref[1].T
    for q0 in range(0, tokens, block):
        qs = slice(q0, q0 + block)
        depth = q0 + block
        scores = score_block(kv_ref[0, :depth, :], q_ref[qs, :], 0, q0)
        top = jnp.max(scores, axis=0, keepdims=True)
        prob = jnp.exp(scores - top)
        top_ref[:, qs] = top
        total_ref[:, qs] = jnp.sum(prob, axis=0, keepdims=True)
        acc_ref[:, qs] = nn(vt_scr[:, :depth], prob.astype(BF))


def forward_body(fsdp, wide, pos_ref, q_ref, far_ref, acc_ref, top_ref, total_ref, adapt_ref, *refs):
    o_ref, lse_ref, inverse_ref, prob_ref = refs[:4]
    mid_refs, oft_scr = refs[4 : 4 + fsdp], refs[4 + fsdp]
    core, later, own = pos_ref[2], pos_ref[3], pos_ref[4]
    tokens = q_ref.shape[0]
    block = min(FORWARD_BLOCK, tokens)

    @pl.when(later == 0)
    def _():
        inverse = 1.0 / total_ref[...]
        inverse_ref[...] = inverse
        lse_ref[...] = top_ref[...] + jnp.log(total_ref[...])
        o_ref[...] = (acc_ref[...] * inverse).T

    @pl.when(later != 0)
    def _():
        oft_scr[...] = far_ref[1].T
        for q0 in range(0, tokens, block):
            qs = slice(q0, q0 + block)
            far = score_block(far_ref[0], q_ref[qs, :], None, q0)
            top = jnp.maximum(top_ref[:, qs], jnp.max(far, axis=0, keepdims=True))
            prob = jnp.exp(far - top)
            shrink = jnp.exp(top_ref[:, qs] - top)
            total = total_ref[:, qs] * shrink + jnp.sum(prob, axis=0, keepdims=True)
            half_prob = prob.astype(BF)
            prob_ref[:, qs] = half_prob
            inverse = 1.0 / total
            inverse_ref[:, qs] = inverse
            lse_ref[:, qs] = top + jnp.log(total)
            out = (acc_ref[:, qs] * shrink + nn(oft_scr[...], half_prob)) * inverse
            o_ref[qs, :] = out.T

    down = adapt_ref[:, pl.ds(pl.multiple_of(wide + own * LANES, LANES), LANES)]
    rows = tokens // fsdp
    for s in range(fsdp):
        to = lax.rem(core + s, fsdp)
        part = o_ref[pl.ds(pl.multiple_of(to * rows, rows), rows), :]
        mid_refs[s][...] = nt(part.astype(BF), down)


def grad_block(key, value, query, grad, norm, delta, k0, q0):
    prob = jnp.exp(score_block(key, query, k0, q0) - norm)
    prob_grad = nt(value, grad)
    return prob.astype(BF), (prob * (prob_grad - delta)).astype(BF)


def far_body(half, pos_ref, *refs):
    parts = refs[:half]
    q_ref, far_ref, o_ref, inverse_ref, prob_ref = refs[half : half + 5]
    far_out, dq_ref, do_ref, delta_ref, kt_scr = refs[half + 5 :]
    later = pos_ref[3]
    tokens = q_ref.shape[0]
    block = min(QUERY_BLOCK, tokens)
    total = parts[0][...].astype(F32)
    for s in range(1, half):
        total = total + parts[s][...].astype(F32)
    grad = total.astype(BF)
    do_ref[...] = grad
    delta_ref[...] = jnp.sum((grad.astype(F32) * o_ref[...]).T, axis=0, keepdims=True)

    @pl.when(later != 0)
    def _():
        kt_scr[...] = far_ref[0].T
        for k0 in range(0, tokens, block):
            ks = slice(k0, k0 + block)
            full = prob_ref[ks, :].astype(F32) * inverse_ref[...]
            prob_grad = nt(far_ref[1, ks, :], do_ref[...])
            score_grad = (full * (prob_grad - delta_ref[...])).astype(BF)
            prob = full.astype(BF)
            far_out[0, ks, :] = (SCORE_SCALE * nn(score_grad, q_ref[...])).astype(BF)
            far_out[1, ks, :] = nn(prob, do_ref[...]).astype(BF)
            part = nn(kt_scr[:, ks], score_grad)
            if k0:
                dq_ref[...] += part
            else:
                dq_ref[...] = part

    @pl.when(later == 0)
    def _():
        far_out[...] = jnp.zeros(far_out.shape, BF)
        dq_ref[...] = jnp.zeros(dq_ref.shape, F32)


def near_body(pos_ref, q_ref, kv_ref, do_ref, norm_ref, delta_ref, dq_in, dq_ref, near_ref, kt_scr):
    tokens = q_ref.shape[0]
    block = min(QUERY_BLOCK, tokens)
    kt_scr[...] = kv_ref[0].T
    for q0 in range(0, tokens, block):
        qs = slice(q0, q0 + block)
        depth = q0 + block
        prob, score_grad = grad_block(
            kv_ref[0, :depth, :],
            kv_ref[1, :depth, :],
            q_ref[qs, :],
            do_ref[qs, :],
            norm_ref[:, qs],
            delta_ref[:, qs],
            0,
            q0,
        )
        dk = SCORE_SCALE * nn(score_grad, q_ref[qs, :])
        dv = nn(prob, do_ref[qs, :])
        if q0:
            near_ref[0, :q0, :] += dk[:q0]
            near_ref[1, :q0, :] += dv[:q0]
        near_ref[0, qs, :] = dk[q0:]
        near_ref[1, qs, :] = dv[q0:]
        dq = dq_in[:, qs] + nn(kt_scr[:, :depth], score_grad)
        dq_ref[qs, :] = (SCORE_SCALE * dq).T.astype(BF)


def merge_body(half, pos_ref, dq_ref, near_ref, back_ref, *out_refs):
    mine = pos_ref[0]
    rows = near_ref.shape[1] // half
    for s in range(half):
        at = pl.ds(pl.multiple_of((mine ^ s) * rows, rows), rows)
        out_refs[s][0] = dq_ref[at, :]
        for i in range(2):
            merged = near_ref[i, at, :] + back_ref[i, at, :].astype(F32)
            out_refs[s][1 + i] = merged.astype(BF)


def unpack_body(half, pos_ref, *refs):
    pieces, outs, sem = refs[:half], refs[half:-1], refs[-1]
    own = pos_ref[4]
    copies = []
    for s in range(half):
        cols = pl.ds(pl.multiple_of((own ^ s) * LANES, LANES), LANES)
        for i in range(3):
            copies.append(
                pltpu.make_async_copy(pieces[s].at[i], outs[i].at[:, cols], sem.at[s * 3 + i])
            )
    for copy in copies:
        copy.start()
    for copy in copies:
        copy.wait()


def adapter_grads_body(half, strips, slot, wide, pos_ref, in_ref, up_ref, down_ref):
    core = pos_ref[2]
    planes = in_ref.shape[0] // half
    width = slot // strips
    step = half * width
    for j in range(half):
        total = in_ref[j]
        for p in range(1, planes):
            total = total + in_ref[p * half + j]
        for i in range(strips):
            to = i * step + j * width
            up_ref[:, to : to + width] = total[:, i * width : (i + 1) * width]
        head = j ^ ((core & 1) * (half // 2))
        down_ref[:, pl.ds(pl.multiple_of(head * LANES, LANES), LANES)] = total[:, wide:]


def adapters_body(half, fsdp, planes, wide, pos_ref, o_ref, *refs):
    both, grads = refs[:fsdp], refs[fsdp : fsdp + half]
    out_ref, scr = refs[fsdp + half :]
    mine, plane, core = pos_ref[0], pos_ref[1], pos_ref[2]
    rank_rows = out_ref.shape[1]
    rank = planes * half * rank_rows
    rows = grads[0].shape[0]
    part_rows = both[0].shape[0]
    for s in range(fsdp):
        src = lax.rem(core + (fsdp - s), fsdp)
        scr[pl.ds(pl.multiple_of(src * part_rows, part_rows), part_rows), :] = both[s][...]
    acc = None
    for s in range(half):
        at = pl.ds(pl.multiple_of((mine ^ s) * rows, rows), rows)
        part = nn(scr[at, :].T[rank:, :], grads[s][:, :wide])
        acc = part if acc is None else acc + part
    acc = adapter_scale * acc
    low = nn(scr[...].T[:rank, :], o_ref[...].astype(BF))
    for p in range(planes):
        for j in range(half):
            at = (p * half + j) * rank_rows
            to = lax.rem(plane + (planes - p), planes) * half + j
            out_ref[to, :, :wide] = acc[at : at + rank_rows, :]
            out_ref[to, :, wide:] = low[at : at + rank_rows, :]


def on_device(
    sizes,
    rotated_query_rows,
    rotated_key_rows,
    saved_value_rows,
    projection_output_gradient,
    frozen_weight_codes,
    block_scale_index,
    block_scale_table,
    adapter_down_matrix,
    adapter_up_matrix,
):
    n_ctx, fsdp = sizes
    half = HALF_GROUP_DEV
    planes = n_ctx // half
    rows = rotated_query_rows.shape[0]
    heads = rotated_query_rows.shape[1] // HEAD_WIDTH
    assert heads == half
    tokens = rows * half
    w_rows, w_cols = frozen_weight_codes.shape
    grad_cols = projection_output_gradient.shape[1]
    strips = grad_cols // (half * w_rows)
    slot = strips * w_rows
    wide = -(-slot // LANES) * LANES
    rank_rows = adapter_down_matrix.shape[0]
    rank = rank_rows * n_ctx

    def head_of(j, f):
        return j ^ ((f & 1) * (half // 2))

    ctx = lax.axis_index("ctx")
    core = lax.axis_index("fsdp")
    mine = ctx % half
    plane = ctx // half
    own = head_of(mine, core)
    later = jnp.where(own < heads // 2, plane % 2, 1 - plane % 2)
    pos = jnp.stack([mine, plane, core, later, own]).astype(jnp.int32)

    def in_plane(x, s):
        if s == 0:
            return x
        return lax.ppermute(x, "ctx", [(i, i ^ s) for i in range(n_ctx)])

    def along(x, s):
        if s == 0:
            return x
        return lax.ppermute(x, "ctx", [(i, (i + s * half) % n_ctx) for i in range(n_ctx)])

    def from_plane(x, *moves):
        route = []
        for group, step in zip(moves[::2], moves[1::2]):
            for p in group:
                route += [(p * half + j, (p + step) * half + j) for j in range(half)]
        return lax.ppermute(x, "ctx", route)

    def across(x, s):
        if s == 0:
            return x
        return lax.ppermute(x, "fsdp", [(i, (i + s) % fsdp) for i in range(fsdp)])

    pairs = []
    for i in range(n_ctx):
        for f in range(fsdp):
            p, j = divmod(i, half)
            if (p % 2 == 0) == (head_of(j, f) < heads // 2):
                pairs.append((i * fsdp + f, (i + half) % n_ctx * fsdp + f))

    def to_later(x):
        return lax.ppermute(x, ("ctx", "fsdp"), pairs)

    def to_earlier(x):
        return lax.ppermute(x, ("ctx", "fsdp"), [(b, a) for a, b in pairs])

    table = block_scale_table.reshape(-1, LANES)
    index = block_scale_index.T
    weight = call(
        dequant_body,
        sds((w_rows, w_cols), BF),
        [pltpu.VMEM(x.shape, x.dtype) for x in (frozen_weight_codes, index, table)]
        + [pltpu.SemaphoreType.DMA((3,))],
        frozen_weight_codes,
        index,
        table,
        in_hbm=True,
    )
    if planes == 4:
        weights = [weight]
        for s in (1, planes - 1):
            weights.append(along(weight, s))
    else:
        weights = [along(weight, s) for s in range(planes)]
    if planes == 4:
        inner, outer = call(
            relay_body, [sds(weight.shape, BF)] * 2, [], pos, *weights[1:], n_scalar=1
        )
        weights.append(from_plane(inner, (1,), 1, (2,), -1))
        weights.append(from_plane(outer, (1,), -1, (2,), 1))

    adapter_cols = wide + heads * HEAD_WIDTH
    sources = (
        rotated_query_rows,
        rotated_key_rows,
        saved_value_rows,
        projection_output_gradient,
        adapter_up_matrix,
        adapter_down_matrix,
    )
    packed = call(
        functools.partial(pack_body, half, strips, wide),
        [sds((rows, wide + 3 * LANES), BF)] * half + [sds((rank_rows, adapter_cols), BF)] * half,
        [pltpu.VMEM(x.shape, BF) for x in sources] + [pltpu.SemaphoreType.DMA((6,))],
        pos,
        *sources,
        n_scalar=1,
        in_hbm=True,
    )
    chunks = [in_plane(x, s) for s, x in enumerate(packed[half:])]
    packed = [in_plane(x, s) for s, x in enumerate(packed[:half])]
    swapped = [across(g, f) for g in packed for f in range(fsdp)]
    adapters = call(
        functools.partial(stack_body, half),
        sds((half, rank_rows, adapter_cols), BF),
        [],
        pos,
        *chunks,
        n_scalar=1,
    )
    adapters = [along(adapters, s) for s in range(planes)]
    adapters = call(ranks_body, sds((rank, adapter_cols), BF), [], *adapters)
    adapts = [across(adapters, f) for f in range(fsdp)]

    query, key_value = call(
        functools.partial(assemble_body, half, wide),
        [sds((tokens, LANES), BF), sds((2, tokens, LANES), BF)],
        [],
        pos,
        *packed,
        n_scalar=1,
    )
    far = to_later(key_value)
    lora = call(
        functools.partial(lora_body, half, fsdp, wide),
        sds((tokens, rank), F32),
        [],
        pos,
        *adapts,
        *swapped,
        n_scalar=1,
    )

    def project(targets):
        return call(
            functools.partial(project_body, half, planes, fsdp, slot, wide, targets),
            [sds((tokens, LANES), BF)] * len(targets),
            [
                pltpu.VMEM((planes * w_rows + wide - slot, LANES * len(targets)), BF),
                pltpu.VMEM((rank, LANES * len(targets)), BF),
            ],
            pos,
            *adapts,
            *swapped,
            *weights,
            n_scalar=1,
        )

    first, second = range(half // 2, half), range(half // 2)
    partial = dict(zip(first, project(tuple(first))))
    partial = {s: in_plane(x, s) for s, x in partial.items()}
    rest = dict(zip(second, project(tuple(second))))
    partial.update({s: in_plane(x, s) for s, x in rest.items()})

    part_rows = tokens // fsdp
    row = sds((1, tokens), F32)
    near_acc, near_top, near_total = call(
        near_forward_body,
        [sds((LANES, tokens), F32), row, row],
        [pltpu.VMEM((LANES, tokens), BF)],
        query,
        key_value,
    )
    out, norm, inverse, far_prob, *mids = call(
        functools.partial(forward_body, fsdp, wide),
        [sds((tokens, LANES), F32), row, row, sds((tokens, tokens), BF)]
        + [sds((part_rows, rank), F32)] * fsdp,
        [pltpu.VMEM((LANES, tokens), BF)],
        pos,
        query,
        far,
        near_acc,
        near_top,
        near_total,
        adapters,
        n_scalar=1,
    )
    mids = [across(x, f) for f, x in enumerate(mids)]
    both = call(join_body, sds((part_rows, 2 * rank), BF), [], pos, lora, *mids, n_scalar=1)
    both = [in_plane(both, s) for s in range(half)]
    both = call(total_body, sds((part_rows, 2 * rank), BF), [], *both)
    both = [across(both, f) for f in range(fsdp)]
    adapter_grads = call(
        functools.partial(adapters_body, half, fsdp, planes, wide),
        sds((n_ctx, rank_rows, wide + HEAD_WIDTH), F32),
        [pltpu.VMEM((tokens, 2 * rank), BF)],
        pos,
        out,
        *both,
        *packed,
        n_scalar=1,
    )
    reduced = lax.all_to_all(adapter_grads, "ctx", split_axis=0, concat_axis=0, tiled=True)
    up_grad, down_grad = call(
        functools.partial(adapter_grads_body, half, strips, slot, wide),
        [sds((rank_rows, grad_cols), F32), sds((rank_rows, heads * HEAD_WIDTH), F32)],
        [],
        pos,
        reduced,
        n_scalar=1,
    )

    far_part, dq_far, grad_out, delta = call(
        functools.partial(far_body, half),
        [
            sds((2, tokens, LANES), BF),
            sds((LANES, tokens), F32),
            sds((tokens, LANES), BF),
            sds((1, tokens), F32),
        ],
        [pltpu.VMEM((LANES, tokens), BF)],
        pos,
        *[partial[s] for s in range(half)],
        query,
        far,
        out,
        inverse,
        far_prob,
        n_scalar=1,
    )
    back = to_earlier(far_part)
    dq, near = call(
        near_body,
        [sds((tokens, LANES), BF), sds((2, tokens, LANES), F32)],
        [pltpu.VMEM((LANES, tokens), BF)],
        pos,
        query,
        key_value,
        grad_out,
        norm,
        delta,
        dq_far,
        n_scalar=1,
    )
    merged = call(
        functools.partial(merge_body, half),
        [sds((3, rows, LANES), BF)] * half,
        [],
        pos,
        dq,
        near,
        back,
        n_scalar=1,
    )
    merged = [in_plane(x, s) for s, x in enumerate(merged)]
    query_grad, key_grad, value_grad = call(
        functools.partial(unpack_body, half),
        [sds((rows, heads * HEAD_WIDTH), BF)] * 3,
        [pltpu.SemaphoreType.DMA((3 * half,))],
        pos,
        *merged,
        n_scalar=1,
        out_hbm=True,
    )
    return query_grad, key_grad, value_grad, down_grad, up_grad


def solution(mesh):
    split = P("ctx", "fsdp")
    in_specs = (split,) * 6 + (P(),) + (split,) * 2

    def body(*args):
        return on_device((mesh.shape["ctx"], mesh.shape["fsdp"]), *args)

    return jax.shard_map(
        body, mesh=mesh, in_specs=in_specs, out_specs=(split,) * 5, check_vma=False
    )
```

```python
import functools

import jax
import jax.numpy as jnp
from jax import lax
from jax.experimental import pallas as pl
from jax.experimental.pallas import tpu as pltpu
from jax.sharding import PartitionSpec as P

HEAD_WIDTH = 128
HALF_GROUP_DEV = 4
LANES = 128
QUERY_BLOCK = 256
FORWARD_BLOCK = 768
SCORE_SCALE = HEAD_WIDTH**-0.5
KERNEL_VMEM = 16 << 20

nf4_values = (
    -1.0,
    -0.6961928009986877,
    -0.5250730514526367,
    -0.39491748809814453,
    -0.28444138169288635,
    -0.18477343022823334,
    -0.09105003625154495,
    0.0,
    0.07958029955625534,
    0.16093020141124725,
    0.24611230194568634,
    0.33791524171829224,
    0.44070982933044434,
    0.5626170039176941,
    0.7229568362236023,
    1.0,
)
adapter_scale = 0.25
masked = -1e30


BF = jnp.bfloat16
F32 = jnp.float32
VM = pl.BlockSpec(memory_space=pltpu.VMEM)
SM = pl.BlockSpec(memory_space=pltpu.SMEM)
HB = pl.BlockSpec(memory_space=pltpu.HBM)


def sds(shape, dtype):
    return jax.ShapeDtypeStruct(shape, dtype)


def nt(a, b):
    return lax.dot_general(a, b, (((1,), (1,)), ((), ())), preferred_element_type=F32)


def nn(a, b):
    return jnp.dot(a, b, preferred_element_type=F32)


def call(body, outs, scratch, *args, n_scalar=0, in_hbm=False, out_hbm=False):
    if in_hbm:
        args = args[:n_scalar] + tuple(
            pltpu.with_memory_space_constraint(x, pltpu.HBM) for x in args[n_scalar:]
        )
    spec = HB if in_hbm else VM
    return pl.pallas_call(
        body,
        out_shape=outs,
        in_specs=[SM] * n_scalar + [spec] * (len(args) - n_scalar),
        out_specs=jax.tree.map(lambda _: HB if out_hbm else VM, outs),
        scratch_shapes=scratch,
        compiler_params=pltpu.CompilerParams(vmem_limit_bytes=KERNEL_VMEM),
    )(*args)


def fetch(sources, targets, sem):
    copies = [
        pltpu.make_async_copy(src, to, sem.at[i])
        for i, (src, to) in enumerate(zip(sources, targets))
    ]
    for copy in copies:
        copy.start()
    for copy in copies:
        copy.wait()


def dequant_body(codes_in, index_in, table_in, out_ref, codes_ref, index_ref, table_ref, sem):
    fetch((codes_in, index_in, table_in), (codes_ref, index_ref, table_ref), sem)
    rows, cols = codes_ref.shape
    groups = index_ref.shape[0]
    parts = table_ref.shape[0]
    per_tile = groups * LANES // cols
    width = LANES // per_tile
    tables = [jnp.broadcast_to(table_ref[i : i + 1, :], (groups, LANES)) for i in range(parts)]
    scales = []
    for r0 in range(0, rows, LANES):
        idx = index_ref[:, r0 : min(r0 + LANES, rows)]
        short = LANES - idx.shape[1]
        if short:
            idx = jnp.concatenate([idx, jnp.zeros((groups, short), jnp.int32)], axis=1)
        low = idx % LANES
        scale = jnp.take_along_axis(tables[0], low, axis=1)
        for i in range(1, parts):
            scale = jnp.where(
                idx >= i * LANES, jnp.take_along_axis(tables[i], low, axis=1), scale
            )
        scales.append(scale)
    scales = jnp.concatenate(scales, axis=1).T[:rows, :]
    lane = lax.broadcasted_iota(jnp.int32, (rows, LANES), 1)
    place = lax.broadcasted_iota(jnp.int32, (8, LANES), 1)
    levels = jnp.zeros((8, LANES), F32)
    for i, level in enumerate(nf4_values):
        levels = jnp.where(place == i, level, levels)
    levels = jnp.broadcast_to(levels[:1], (rows, LANES))
    for b in range(cols // LANES):
        code = codes_ref[:, b * LANES : (b + 1) * LANES]
        value = jnp.take_along_axis(levels, code, axis=1)
        at = b * per_tile
        scale = jnp.broadcast_to(scales[:, at : at + 1], (rows, LANES))
        for i in range(1, per_tile):
            scale = jnp.where(lane >= i * width, scales[:, at + i : at + i + 1], scale)
        out_ref[:, b * LANES : (b + 1) * LANES] = (value * scale).astype(BF)


def relay_body(pos_ref, above_ref, below_ref, inner_ref, outer_ref):
    @pl.when(pos_ref[1] == 1)
    def _():
        inner_ref[...] = above_ref[...]
        outer_ref[...] = below_ref[...]

    @pl.when(pos_ref[1] != 1)
    def _():
        inner_ref[...] = below_ref[...]
        outer_ref[...] = above_ref[...]


def pack_body(half, strips, wide, pos_ref, *refs):
    ins, outs, chunks = refs[:6], refs[6 : 6 + half], refs[6 + half : 6 + 2 * half]
    scr, sem = refs[6 + 2 * half : -1], refs[-1]
    fetch(ins, scr, sem)
    mine, own = pos_ref[0], pos_ref[4]
    up_ref, down_ref = scr[4], scr[5]
    step = up_ref.shape[1] // strips
    width = step // half
    short = wide - strips * width

    def strip(ref, jv):
        pieces = [ref[:, i * step + jv * width : i * step + (jv + 1) * width] for i in range(strips)]
        if short:
            pieces.append(jnp.zeros((ref.shape[0], short), BF))
        return jnp.concatenate(pieces, axis=1)

    for s in range(half):
        out, chunk = outs[s], chunks[s]
        cols = pl.ds(pl.multiple_of((own ^ s) * LANES, LANES), LANES)
        for i in range(3):
            out[:, wide + i * LANES : wide + (i + 1) * LANES] = scr[i][:, cols]
        chunk[:, wide:] = down_ref[...]
        for jv in range(half):

            @pl.when((mine ^ s) == jv)
            def _(out=out, chunk=chunk, jv=jv):
                out[:, :wide] = strip(scr[3], jv)
                chunk[:, :wide] = strip(up_ref, jv)


def stack_body(half, pos_ref, *refs):
    for s in range(half):
        refs[half][pos_ref[0] ^ s] = refs[s][...]


def assemble_body(half, wide, pos_ref, *refs):
    pieces, (q_out, kv_out) = refs[:half], refs[half:]
    mine = pos_ref[0]
    rows = pieces[0].shape[0]
    for s in range(half):
        at = pl.ds(pl.multiple_of((mine ^ s) * rows, rows), rows)
        q_out[at, :] = pieces[s][:, wide : wide + LANES]
        kv_out[0, at, :] = pieces[s][:, wide + LANES : wide + 2 * LANES]
        kv_out[1, at, :] = pieces[s][:, wide + 2 * LANES :]


def ranks_body(*refs):
    parts = [ref[j].astype(F32) for ref in refs[:-1] for j in range(ref.shape[0])]
    refs[-1][...] = jnp.concatenate(parts, axis=0).astype(BF)


def lora_body(half, fsdp, wide, pos_ref, *refs):
    adapts, grads, out_ref = refs[:fsdp], refs[fsdp:-1], refs[-1]
    mine, core = pos_ref[0], pos_ref[2]
    rows = grads[0].shape[0]

    def write(pieces):
        total = None
        for f in range(fsdp):
            left = jnp.concatenate([grads[s * fsdp + f][:, :wide] for s in pieces], axis=0)
            part = nt(left, adapts[f][:, :wide])
            total = part if total is None else total + part
        total = adapter_scale * total
        for i, s in enumerate(pieces):
            at = pl.ds(pl.multiple_of((mine ^ s) * rows, rows), rows)
            out_ref[at, :] = total[i * rows : (i + 1) * rows, :]

    if fsdp == 2:
        for first in range(0, half, 2):

            @pl.when((mine ^ first) // 2 == core)
            def _(first=first):
                write((first, first + 1))

    else:
        write(tuple(range(half)))


def join_body(pos_ref, lora_ref, *refs):
    mids, out_ref = refs[:-1], refs[-1]
    rows = out_ref.shape[0]
    mid = mids[0][...]
    for m in mids[1:]:
        mid = mid + m[...]
    lora = lora_ref[pl.ds(pl.multiple_of(pos_ref[2] * rows, rows), rows), :]
    out_ref[...] = jnp.concatenate([lora, mid], axis=1).astype(BF)


def total_body(*refs):
    total = refs[0][...].astype(F32)
    for ref in refs[1:-1]:
        total = total + ref[...].astype(F32)
    refs[-1][...] = total.astype(BF)


def project_body(half, planes, fsdp, slot, wide, targets, pos_ref, *refs):
    adapts, refs = refs[:fsdp], refs[fsdp:]
    grads = refs[: half * fsdp]
    weights = refs[half * fsdp : -2 - len(targets)]
    n_weights = len(weights)
    outs = refs[-2 - len(targets) : -2]
    w_scr, d_scr = refs[-2:]
    mine, plane, core, own = pos_ref[0], pos_ref[1], pos_ref[2], pos_ref[4]
    rows_each = weights[0].shape[0]
    rows = grads[0].shape[0]
    tail = w_scr.shape[0] - planes * rows_each
    if tail:
        w_scr[planes * rows_each :, :] = jnp.zeros((tail, w_scr.shape[1]), BF)
    for i, t in enumerate(targets):
        cols = pl.ds(pl.multiple_of((own ^ t) * LANES, LANES), LANES)
        d_cols = pl.ds(pl.multiple_of(wide + (own ^ t) * LANES, LANES), LANES)
        to = slice(i * LANES, (i + 1) * LANES)
        d_scr[:, to] = adapts[0][:, d_cols]
        if n_weights == planes:
            sources = [lax.rem(plane + (planes - s), planes) for s in range(planes)]
        else:
            away = lax.rem(plane + 2, planes)
            inside = (plane == 1) | (plane == 2)
            sources = [plane, lax.rem(plane + planes - 1, planes), lax.rem(plane + 1, planes)]
            sources += [jnp.where(inside, away, -1), jnp.where(inside, -1, away)]
        for piece, src in zip(weights, sources):

            @pl.when(src >= 0)
            def _(piece=piece, src=src, to=to, cols=cols):
                at = pl.ds(pl.multiple_of(src * rows_each, rows_each), rows_each)
                w_scr[at, to] = piece[:, cols]

    for f in range(fsdp):
        src = lax.rem(core + (fsdp - f), fsdp)
        at = pl.ds(pl.multiple_of(src * slot, 16), slot)
        up = adapts[f][:, :wide]
        low = lax.dot_general(
            up, d_scr[...], (((0,), (0,)), ((), ())), preferred_element_type=F32
        )
        w_scr[at, :] = (w_scr[at, :].astype(F32) + adapter_scale * low[:slot]).astype(BF)
    acc = None
    for f in range(fsdp):
        src = lax.rem(core + (fsdp - f), fsdp)
        w_at = pl.ds(pl.multiple_of(src * slot, 16), wide)
        left = jnp.concatenate([grads[s * fsdp + f][:, :wide] for s in range(half)], axis=0)
        part = nn(left, w_scr[w_at, :])
        acc = part if acc is None else acc + part
    for s in range(half):
        at = pl.ds(pl.multiple_of((mine ^ s) * rows, rows), rows)
        for i in range(len(targets)):
            block = acc[s * rows : (s + 1) * rows, i * LANES : (i + 1) * LANES]
            outs[i][at, :] = block.astype(BF)


def score_block(key, query, k0, q0):
    scores = nt(key, query) * SCORE_SCALE
    if k0 is None or k0 + key.shape[0] - 1 <= q0:
        return scores
    kpos = k0 + lax.broadcasted_iota(jnp.int32, scores.shape, 0)
    qpos = q0 + lax.broadcasted_iota(jnp.int32, scores.shape, 1)
    return jnp.where(kpos <= qpos, scores, masked)


def near_forward_body(q_ref, kv_ref, acc_ref, top_ref, total_ref, prob_ref, vt_scr):
    tokens = q_ref.shape[0]
    block = min(FORWARD_BLOCK, tokens)
    vt_scr[...] = kv_ref[1].T
    for q0 in range(0, tokens, block):
        qs = slice(q0, q0 + block)
        depth = q0 + block
        scores = score_block(kv_ref[0, :depth, :], q_ref[qs, :], 0, q0)
        top = jnp.max(scores, axis=0, keepdims=True)
        prob = jnp.exp(scores - top)
        top_ref[:, qs] = top
        total_ref[:, qs] = jnp.sum(prob, axis=0, keepdims=True)
        half_prob = prob.astype(BF)
        prob_ref[:depth, qs] = half_prob
        acc_ref[:, qs] = nn(vt_scr[:, :depth], half_prob)


def forward_body(fsdp, wide, pos_ref, q_ref, far_ref, acc_ref, top_ref, total_ref, adapt_ref, *refs):
    o_ref, scale_ref, inverse_ref, prob_ref = refs[:4]
    mid_refs, oft_scr = refs[4 : 4 + fsdp], refs[4 + fsdp]
    core, later, own = pos_ref[2], pos_ref[3], pos_ref[4]
    tokens = q_ref.shape[0]
    block = min(FORWARD_BLOCK, tokens)

    @pl.when(later == 0)
    def _():
        inverse = 1.0 / total_ref[...]
        inverse_ref[...] = inverse
        scale_ref[...] = inverse
        o_ref[...] = (acc_ref[...] * inverse).T

    @pl.when(later != 0)
    def _():
        oft_scr[...] = far_ref[1].T
        for q0 in range(0, tokens, block):
            qs = slice(q0, q0 + block)
            far = score_block(far_ref[0], q_ref[qs, :], None, q0)
            top = jnp.maximum(top_ref[:, qs], jnp.max(far, axis=0, keepdims=True))
            prob = jnp.exp(far - top)
            shrink = jnp.exp(top_ref[:, qs] - top)
            total = total_ref[:, qs] * shrink + jnp.sum(prob, axis=0, keepdims=True)
            half_prob = prob.astype(BF)
            prob_ref[:, qs] = half_prob
            inverse = 1.0 / total
            inverse_ref[:, qs] = inverse
            scale_ref[:, qs] = shrink * inverse
            out = (acc_ref[:, qs] * shrink + nn(oft_scr[...], half_prob)) * inverse
            o_ref[qs, :] = out.T

    down = adapt_ref[:, pl.ds(pl.multiple_of(wide + own * LANES, LANES), LANES)]
    rows = tokens // fsdp
    for s in range(fsdp):
        to = lax.rem(core + s, fsdp)
        part = o_ref[pl.ds(pl.multiple_of(to * rows, rows), rows), :]
        mid_refs[s][...] = nt(part.astype(BF), down)


def far_body(half, pos_ref, *refs):
    parts = refs[:half]
    q_ref, far_ref, o_ref, inverse_ref, prob_ref = refs[half : half + 5]
    far_out, dq_ref, do_ref, delta_ref, kt_scr = refs[half + 5 :]
    later = pos_ref[3]
    tokens = q_ref.shape[0]
    block = min(QUERY_BLOCK, tokens)
    total = parts[0][...].astype(F32)
    for s in range(1, half):
        total = total + parts[s][...].astype(F32)
    grad = total.astype(BF)
    do_ref[...] = grad
    delta_ref[...] = jnp.sum((grad.astype(F32) * o_ref[...]).T, axis=0, keepdims=True)

    @pl.when(later != 0)
    def _():
        kt_scr[...] = far_ref[0].T
        for k0 in range(0, tokens, block):
            ks = slice(k0, k0 + block)
            full = prob_ref[ks, :].astype(F32) * inverse_ref[...]
            prob_grad = nt(far_ref[1, ks, :], do_ref[...])
            score_grad = (full * (prob_grad - delta_ref[...])).astype(BF)
            prob = full.astype(BF)
            far_out[0, ks, :] = (SCORE_SCALE * nn(score_grad, q_ref[...])).astype(BF)
            far_out[1, ks, :] = nn(prob, do_ref[...]).astype(BF)
            part = nn(kt_scr[:, ks], score_grad)
            if k0:
                dq_ref[...] += part
            else:
                dq_ref[...] = part

    @pl.when(later == 0)
    def _():
        far_out[...] = jnp.zeros(far_out.shape, BF)
        dq_ref[...] = jnp.zeros(dq_ref.shape, F32)


def near_body(
    q_ref, kv_ref, do_ref, prob_ref, scale_ref, delta_ref, dq_in, dq_ref, near_ref, kt_scr
):
    tokens = q_ref.shape[0]
    block = min(QUERY_BLOCK, tokens)
    kt_scr[...] = kv_ref[0].T
    for q0 in range(0, tokens, block):
        qs = slice(q0, q0 + block)
        depth = q0 + block
        full = prob_ref[:depth, qs].astype(F32) * scale_ref[:, qs]
        prob_grad = nt(kv_ref[1, :depth, :], do_ref[qs, :])
        score_grad = (full * (prob_grad - delta_ref[:, qs])).astype(BF)
        dk = SCORE_SCALE * nn(score_grad, q_ref[qs, :])
        dv = nn(full.astype(BF), do_ref[qs, :])
        if q0:
            near_ref[0, :q0, :] += dk[:q0]
            near_ref[1, :q0, :] += dv[:q0]
        near_ref[0, qs, :] = dk[q0:]
        near_ref[1, qs, :] = dv[q0:]
        dq = dq_in[:, qs] + nn(kt_scr[:, :depth], score_grad)
        dq_ref[qs, :] = (SCORE_SCALE * dq).T.astype(BF)


def merge_body(half, pos_ref, dq_ref, near_ref, back_ref, *out_refs):
    mine = pos_ref[0]
    rows = near_ref.shape[1] // half
    for s in range(half):
        at = pl.ds(pl.multiple_of((mine ^ s) * rows, rows), rows)
        out_refs[s][0] = dq_ref[at, :]
        for i in range(2):
            merged = near_ref[i, at, :] + back_ref[i, at, :].astype(F32)
            out_refs[s][1 + i] = merged.astype(BF)


def unpack_body(half, pos_ref, *refs):
    pieces, outs, sem = refs[:half], refs[half:-1], refs[-1]
    own = pos_ref[4]
    copies = []
    for s in range(half):
        cols = pl.ds(pl.multiple_of((own ^ s) * LANES, LANES), LANES)
        for i in range(3):
            copies.append(
                pltpu.make_async_copy(pieces[s].at[i], outs[i].at[:, cols], sem.at[s * 3 + i])
            )
    for copy in copies:
        copy.start()
    for copy in copies:
        copy.wait()


def adapter_grads_body(half, strips, slot, wide, pos_ref, in_ref, up_ref, down_ref):
    core = pos_ref[2]
    planes = in_ref.shape[0] // half
    width = slot // strips
    step = half * width
    for j in range(half):
        total = in_ref[j]
        for p in range(1, planes):
            total = total + in_ref[p * half + j]
        for i in range(strips):
            to = i * step + j * width
            up_ref[:, to : to + width] = total[:, i * width : (i + 1) * width]
        head = j ^ ((core & 1) * (half // 2))
        down_ref[:, pl.ds(pl.multiple_of(head * LANES, LANES), LANES)] = total[:, wide:]


def adapters_body(half, fsdp, planes, wide, pos_ref, o_ref, *refs):
    both, grads = refs[:fsdp], refs[fsdp : fsdp + half]
    out_ref, scr = refs[fsdp + half :]
    mine, plane, core = pos_ref[0], pos_ref[1], pos_ref[2]
    rank_rows = out_ref.shape[1]
    rank = planes * half * rank_rows
    rows = grads[0].shape[0]
    part_rows = both[0].shape[0]
    for s in range(fsdp):
        src = lax.rem(core + (fsdp - s), fsdp)
        scr[pl.ds(pl.multiple_of(src * part_rows, part_rows), part_rows), :] = both[s][...]
    acc = None
    for s in range(half):
        at = pl.ds(pl.multiple_of((mine ^ s) * rows, rows), rows)
        part = nn(scr[at, :].T[rank:, :], grads[s][:, :wide])
        acc = part if acc is None else acc + part
    acc = adapter_scale * acc
    low = nn(scr[...].T[:rank, :], o_ref[...].astype(BF))
    for p in range(planes):
        for j in range(half):
            at = (p * half + j) * rank_rows
            to = lax.rem(plane + (planes - p), planes) * half + j
            out_ref[to, :, :wide] = acc[at : at + rank_rows, :]
            out_ref[to, :, wide:] = low[at : at + rank_rows, :]


def on_device(
    sizes,
    rotated_query_rows,
    rotated_key_rows,
    saved_value_rows,
    projection_output_gradient,
    frozen_weight_codes,
    block_scale_index,
    block_scale_table,
    adapter_down_matrix,
    adapter_up_matrix,
):
    n_ctx, fsdp = sizes
    half = HALF_GROUP_DEV
    planes = n_ctx // half
    rows = rotated_query_rows.shape[0]
    heads = rotated_query_rows.shape[1] // HEAD_WIDTH
    assert heads == half
    tokens = rows * half
    w_rows, w_cols = frozen_weight_codes.shape
    grad_cols = projection_output_gradient.shape[1]
    strips = grad_cols // (half * w_rows)
    slot = strips * w_rows
    wide = -(-slot // LANES) * LANES
    rank_rows = adapter_down_matrix.shape[0]
    rank = rank_rows * n_ctx

    def head_of(j, f):
        return j ^ ((f & 1) * (half // 2))

    ctx = lax.axis_index("ctx")
    core = lax.axis_index("fsdp")
    mine = ctx % half
    plane = ctx // half
    own = head_of(mine, core)
    later = jnp.where(own < heads // 2, plane % 2, 1 - plane % 2)
    pos = jnp.stack([mine, plane, core, later, own]).astype(jnp.int32)

    def in_plane(x, s):
        if s == 0:
            return x
        return lax.ppermute(x, "ctx", [(i, i ^ s) for i in range(n_ctx)])

    def along(x, s):
        if s == 0:
            return x
        return lax.ppermute(x, "ctx", [(i, (i + s * half) % n_ctx) for i in range(n_ctx)])

    def from_plane(x, *moves):
        route = []
        for group, step in zip(moves[::2], moves[1::2]):
            for p in group:
                route += [(p * half + j, (p + step) * half + j) for j in range(half)]
        return lax.ppermute(x, "ctx", route)

    def across(x, s):
        if s == 0:
            return x
        return lax.ppermute(x, "fsdp", [(i, (i + s) % fsdp) for i in range(fsdp)])

    pairs = []
    for i in range(n_ctx):
        for f in range(fsdp):
            p, j = divmod(i, half)
            if (p % 2 == 0) == (head_of(j, f) < heads // 2):
                pairs.append((i * fsdp + f, (i + half) % n_ctx * fsdp + f))

    def to_later(x):
        return lax.ppermute(x, ("ctx", "fsdp"), pairs)

    def to_earlier(x):
        return lax.ppermute(x, ("ctx", "fsdp"), [(b, a) for a, b in pairs])

    table = block_scale_table.reshape(-1, LANES)
    index = block_scale_index.T
    weight = call(
        dequant_body,
        sds((w_rows, w_cols), BF),
        [pltpu.VMEM(x.shape, x.dtype) for x in (frozen_weight_codes, index, table)]
        + [pltpu.SemaphoreType.DMA((3,))],
        frozen_weight_codes,
        index,
        table,
        in_hbm=True,
    )
    if planes == 4:
        weights = [weight]
        for s in (1, planes - 1):
            weights.append(along(weight, s))
    else:
        weights = [along(weight, s) for s in range(planes)]
    if planes == 4:
        inner, outer = call(
            relay_body, [sds(weight.shape, BF)] * 2, [], pos, *weights[1:], n_scalar=1
        )
        weights.append(from_plane(inner, (1,), 1, (2,), -1))
        weights.append(from_plane(outer, (1,), -1, (2,), 1))

    adapter_cols = wide + heads * HEAD_WIDTH
    sources = (
        rotated_query_rows,
        rotated_key_rows,
        saved_value_rows,
        projection_output_gradient,
        adapter_up_matrix,
        adapter_down_matrix,
    )
    packed = call(
        functools.partial(pack_body, half, strips, wide),
        [sds((rows, wide + 3 * LANES), BF)] * half + [sds((rank_rows, adapter_cols), BF)] * half,
        [pltpu.VMEM(x.shape, BF) for x in sources] + [pltpu.SemaphoreType.DMA((6,))],
        pos,
        *sources,
        n_scalar=1,
        in_hbm=True,
    )
    chunks = [in_plane(x, s) for s, x in enumerate(packed[half:])]
    packed = [in_plane(x, s) for s, x in enumerate(packed[:half])]
    swapped = [across(g, f) for g in packed for f in range(fsdp)]
    adapters = call(
        functools.partial(stack_body, half),
        sds((half, rank_rows, adapter_cols), BF),
        [],
        pos,
        *chunks,
        n_scalar=1,
    )
    adapters = [along(adapters, s) for s in range(planes)]
    adapters = call(ranks_body, sds((rank, adapter_cols), BF), [], *adapters)
    adapts = [across(adapters, f) for f in range(fsdp)]

    query, key_value = call(
        functools.partial(assemble_body, half, wide),
        [sds((tokens, LANES), BF), sds((2, tokens, LANES), BF)],
        [],
        pos,
        *packed,
        n_scalar=1,
    )
    far = to_later(key_value)
    lora = call(
        functools.partial(lora_body, half, fsdp, wide),
        sds((tokens, rank), F32),
        [],
        pos,
        *adapts,
        *swapped,
        n_scalar=1,
    )

    def project(targets):
        return call(
            functools.partial(project_body, half, planes, fsdp, slot, wide, targets),
            [sds((tokens, LANES), BF)] * len(targets),
            [
                pltpu.VMEM((planes * w_rows + wide - slot, LANES * len(targets)), BF),
                pltpu.VMEM((rank, LANES * len(targets)), BF),
            ],
            pos,
            *adapts,
            *swapped,
            *weights,
            n_scalar=1,
        )

    first, second = range(half // 2, half), range(half // 2)
    partial = dict(zip(first, project(tuple(first))))
    partial = {s: in_plane(x, s) for s, x in partial.items()}
    rest = dict(zip(second, project(tuple(second))))
    partial.update({s: in_plane(x, s) for s, x in rest.items()})

    part_rows = tokens // fsdp
    row = sds((1, tokens), F32)
    near_acc, near_top, near_total, near_prob = call(
        near_forward_body,
        [sds((LANES, tokens), F32), row, row, sds((tokens, tokens), BF)],
        [pltpu.VMEM((LANES, tokens), BF)],
        query,
        key_value,
    )
    out, near_scale, inverse, far_prob, *mids = call(
        functools.partial(forward_body, fsdp, wide),
        [sds((tokens, LANES), F32), row, row, sds((tokens, tokens), BF)]
        + [sds((part_rows, rank), F32)] * fsdp,
        [pltpu.VMEM((LANES, tokens), BF)],
        pos,
        query,
        far,
        near_acc,
        near_top,
        near_total,
        adapters,
        n_scalar=1,
    )
    mids = [across(x, f) for f, x in enumerate(mids)]
    both = call(join_body, sds((part_rows, 2 * rank), BF), [], pos, lora, *mids, n_scalar=1)
    both = [in_plane(both, s) for s in range(half)]
    both = call(total_body, sds((part_rows, 2 * rank), BF), [], *both)
    both = [across(both, f) for f in range(fsdp)]
    adapter_grads = call(
        functools.partial(adapters_body, half, fsdp, planes, wide),
        sds((n_ctx, rank_rows, wide + HEAD_WIDTH), F32),
        [pltpu.VMEM((tokens, 2 * rank), BF)],
        pos,
        out,
        *both,
        *packed,
        n_scalar=1,
    )
    reduced = lax.all_to_all(adapter_grads, "ctx", split_axis=0, concat_axis=0, tiled=True)
    up_grad, down_grad = call(
        functools.partial(adapter_grads_body, half, strips, slot, wide),
        [sds((rank_rows, grad_cols), F32), sds((rank_rows, heads * HEAD_WIDTH), F32)],
        [],
        pos,
        reduced,
        n_scalar=1,
    )

    far_part, dq_far, grad_out, delta = call(
        functools.partial(far_body, half),
        [
            sds((2, tokens, LANES), BF),
            sds((LANES, tokens), F32),
            sds((tokens, LANES), BF),
            sds((1, tokens), F32),
        ],
        [pltpu.VMEM((LANES, tokens), BF)],
        pos,
        *[partial[s] for s in range(half)],
        query,
        far,
        out,
        inverse,
        far_prob,
        n_scalar=1,
    )
    back = to_earlier(far_part)
    dq, near = call(
        near_body,
        [sds((tokens, LANES), BF), sds((2, tokens, LANES), F32)],
        [pltpu.VMEM((LANES, tokens), BF)],
        query,
        key_value,
        grad_out,
        near_prob,
        near_scale,
        delta,
        dq_far,
    )
    merged = call(
        functools.partial(merge_body, half),
        [sds((3, rows, LANES), BF)] * half,
        [],
        pos,
        dq,
        near,
        back,
        n_scalar=1,
    )
    merged = [in_plane(x, s) for s, x in enumerate(merged)]
    query_grad, key_grad, value_grad = call(
        functools.partial(unpack_body, half),
        [sds((rows, heads * HEAD_WIDTH), BF)] * 3,
        [pltpu.SemaphoreType.DMA((3 * half,))],
        pos,
        *merged,
        n_scalar=1,
        out_hbm=True,
    )
    return query_grad, key_grad, value_grad, down_grad, up_grad


def solution(mesh):
    split = P("ctx", "fsdp")
    in_specs = (split,) * 6 + (P(),) + (split,) * 2

    def body(*args):
        return on_device((mesh.shape["ctx"], mesh.shape["fsdp"]), *args)

    return jax.shard_map(
        body, mesh=mesh, in_specs=in_specs, out_specs=(split,) * 5, check_vma=False
    )
```

```python
import functools

import jax
import jax.numpy as jnp
from jax import lax
from jax.experimental import pallas as pl
from jax.experimental.pallas import tpu as pltpu
from jax.sharding import PartitionSpec as P

HEAD_WIDTH = 128
HALF_GROUP_DEV = 4
LANES = 128
QUERY_BLOCK = 256
FORWARD_BLOCK = 768
SCORE_SCALE = HEAD_WIDTH**-0.5
KERNEL_VMEM = 16 << 20

nf4_values = (
    -1.0,
    -0.6961928009986877,
    -0.5250730514526367,
    -0.39491748809814453,
    -0.28444138169288635,
    -0.18477343022823334,
    -0.09105003625154495,
    0.0,
    0.07958029955625534,
    0.16093020141124725,
    0.24611230194568634,
    0.33791524171829224,
    0.44070982933044434,
    0.5626170039176941,
    0.7229568362236023,
    1.0,
)
adapter_scale = 0.25
masked = -1e30


BF = jnp.bfloat16
F32 = jnp.float32
VM = pl.BlockSpec(memory_space=pltpu.VMEM)
SM = pl.BlockSpec(memory_space=pltpu.SMEM)
HB = pl.BlockSpec(memory_space=pltpu.HBM)


def sds(shape, dtype):
    return jax.ShapeDtypeStruct(shape, dtype)


def nt(a, b):
    return lax.dot_general(a, b, (((1,), (1,)), ((), ())), preferred_element_type=F32)


def nn(a, b):
    return jnp.dot(a, b, preferred_element_type=F32)


def call(body, outs, scratch, *args, n_scalar=0, in_hbm=False, out_hbm=False):
    if in_hbm:
        args = args[:n_scalar] + tuple(
            pltpu.with_memory_space_constraint(x, pltpu.HBM) for x in args[n_scalar:]
        )
    spec = HB if in_hbm else VM
    return pl.pallas_call(
        body,
        out_shape=outs,
        in_specs=[SM] * n_scalar + [spec] * (len(args) - n_scalar),
        out_specs=jax.tree.map(lambda _: HB if out_hbm else VM, outs),
        scratch_shapes=scratch,
        compiler_params=pltpu.CompilerParams(vmem_limit_bytes=KERNEL_VMEM),
    )(*args)


def fetch(sources, targets, sem):
    copies = [
        pltpu.make_async_copy(src, to, sem.at[i])
        for i, (src, to) in enumerate(zip(sources, targets))
    ]
    for copy in copies:
        copy.start()
    for copy in copies:
        copy.wait()


def dequant_body(codes_in, index_in, table_in, out_ref, codes_ref, index_ref, table_ref, sem):
    fetch((codes_in, index_in, table_in), (codes_ref, index_ref, table_ref), sem)
    rows, cols = codes_ref.shape
    groups = index_ref.shape[0]
    parts = table_ref.shape[0]
    per_tile = groups * LANES // cols
    width = LANES // per_tile
    tables = [jnp.broadcast_to(table_ref[i : i + 1, :], (groups, LANES)) for i in range(parts)]
    scales = []
    for r0 in range(0, rows, LANES):
        idx = index_ref[:, r0 : min(r0 + LANES, rows)]
        short = LANES - idx.shape[1]
        if short:
            idx = jnp.concatenate([idx, jnp.zeros((groups, short), jnp.int32)], axis=1)
        low = idx % LANES
        scale = jnp.take_along_axis(tables[0], low, axis=1)
        for i in range(1, parts):
            scale = jnp.where(
                idx >= i * LANES, jnp.take_along_axis(tables[i], low, axis=1), scale
            )
        scales.append(scale)
    scales = jnp.concatenate(scales, axis=1).T[:rows, :]
    lane = lax.broadcasted_iota(jnp.int32, (rows, LANES), 1)
    place = lax.broadcasted_iota(jnp.int32, (8, LANES), 1)
    levels = jnp.zeros((8, LANES), F32)
    for i, level in enumerate(nf4_values):
        levels = jnp.where(place == i, level, levels)
    levels = jnp.broadcast_to(levels[:1], (rows, LANES))
    for b in range(cols // LANES):
        code = codes_ref[:, b * LANES : (b + 1) * LANES]
        value = jnp.take_along_axis(levels, code, axis=1)
        at = b * per_tile
        scale = jnp.broadcast_to(scales[:, at : at + 1], (rows, LANES))
        for i in range(1, per_tile):
            scale = jnp.where(lane >= i * width, scales[:, at + i : at + i + 1], scale)
        out_ref[:, b * LANES : (b + 1) * LANES] = (value * scale).astype(BF)


def relay_body(pos_ref, above_ref, below_ref, inner_ref, outer_ref):
    @pl.when(pos_ref[1] == 1)
    def _():
        inner_ref[...] = above_ref[...]
        outer_ref[...] = below_ref[...]

    @pl.when(pos_ref[1] != 1)
    def _():
        inner_ref[...] = below_ref[...]
        outer_ref[...] = above_ref[...]


def pack_body(half, strips, wide, pos_ref, *refs):
    ins, outs, chunks = refs[:6], refs[6 : 6 + half], refs[6 + half : 6 + 2 * half]
    scr, sem = refs[6 + 2 * half : -1], refs[-1]
    fetch(ins, scr, sem)
    mine, own = pos_ref[0], pos_ref[4]
    up_ref, down_ref = scr[4], scr[5]
    step = up_ref.shape[1] // strips
    width = step // half
    short = wide - strips * width

    def strip(ref, jv):
        pieces = [ref[:, i * step + jv * width : i * step + (jv + 1) * width] for i in range(strips)]
        if short:
            pieces.append(jnp.zeros((ref.shape[0], short), BF))
        return jnp.concatenate(pieces, axis=1)

    for s in range(half):
        out, chunk = outs[s], chunks[s]
        cols = pl.ds(pl.multiple_of((own ^ s) * LANES, LANES), LANES)
        for i in range(3):
            out[:, wide + i * LANES : wide + (i + 1) * LANES] = scr[i][:, cols]
        chunk[:, wide:] = down_ref[...]
        for jv in range(half):

            @pl.when((mine ^ s) == jv)
            def _(out=out, chunk=chunk, jv=jv):
                out[:, :wide] = strip(scr[3], jv)
                chunk[:, :wide] = strip(up_ref, jv)


def stack_body(half, pos_ref, *refs):
    for s in range(half):
        refs[half][pos_ref[0] ^ s] = refs[s][...]


def assemble_body(half, wide, pos_ref, *refs):
    pieces, (q_out, kv_out) = refs[:half], refs[half:]
    mine = pos_ref[0]
    rows = pieces[0].shape[0]
    for s in range(half):
        at = pl.ds(pl.multiple_of((mine ^ s) * rows, rows), rows)
        q_out[at, :] = pieces[s][:, wide : wide + LANES]
        kv_out[0, at, :] = pieces[s][:, wide + LANES : wide + 2 * LANES]
        kv_out[1, at, :] = pieces[s][:, wide + 2 * LANES :]


def ranks_body(*refs):
    parts = [ref[j].astype(F32) for ref in refs[:-1] for j in range(ref.shape[0])]
    refs[-1][...] = jnp.concatenate(parts, axis=0).astype(BF)


def lora_body(half, fsdp, wide, pos_ref, *refs):
    adapts, grads, out_ref = refs[:fsdp], refs[fsdp:-1], refs[-1]
    mine, core = pos_ref[0], pos_ref[2]
    rows = grads[0].shape[0]

    def write(pieces):
        total = None
        for f in range(fsdp):
            left = jnp.concatenate([grads[s * fsdp + f][:, :wide] for s in pieces], axis=0)
            part = nt(left, adapts[f][:, :wide])
            total = part if total is None else total + part
        total = adapter_scale * total
        for i, s in enumerate(pieces):
            at = pl.ds(pl.multiple_of((mine ^ s) * rows, rows), rows)
            out_ref[at, :] = total[i * rows : (i + 1) * rows, :]

    if fsdp == 2:
        for first in range(0, half, 2):

            @pl.when((mine ^ first) // 2 == core)
            def _(first=first):
                write((first, first + 1))

    else:
        write(tuple(range(half)))


def join_body(pos_ref, lora_ref, *refs):
    mids, out_ref = refs[:-1], refs[-1]
    rows = out_ref.shape[0]
    mid = mids[0][...]
    for m in mids[1:]:
        mid = mid + m[...]
    lora = lora_ref[pl.ds(pl.multiple_of(pos_ref[2] * rows, rows), rows), :]
    out_ref[...] = jnp.concatenate([lora, mid], axis=1).astype(BF)


def total_body(*refs):
    total = refs[0][...].astype(F32)
    for ref in refs[1:-1]:
        total = total + ref[...].astype(F32)
    refs[-1][...] = total.astype(BF)


def project_body(half, planes, fsdp, slot, wide, targets, pos_ref, *refs):
    adapts, refs = refs[:fsdp], refs[fsdp:]
    grads = refs[: half * fsdp]
    weights = refs[half * fsdp : -2 - len(targets)]
    n_weights = len(weights)
    outs = refs[-2 - len(targets) : -2]
    w_scr, d_scr = refs[-2:]
    mine, plane, core, own = pos_ref[0], pos_ref[1], pos_ref[2], pos_ref[4]
    rows_each = weights[0].shape[0]
    rows = grads[0].shape[0]
    tail = w_scr.shape[0] - planes * rows_each
    if tail:
        w_scr[planes * rows_each :, :] = jnp.zeros((tail, w_scr.shape[1]), BF)
    for i, t in enumerate(targets):
        cols = pl.ds(pl.multiple_of((own ^ t) * LANES, LANES), LANES)
        d_cols = pl.ds(pl.multiple_of(wide + (own ^ t) * LANES, LANES), LANES)
        to = slice(i * LANES, (i + 1) * LANES)
        d_scr[:, to] = adapts[0][:, d_cols]
        if n_weights == planes:
            sources = [lax.rem(plane + (planes - s), planes) for s in range(planes)]
        else:
            away = lax.rem(plane + 2, planes)
            inside = (plane == 1) | (plane == 2)
            sources = [plane, lax.rem(plane + planes - 1, planes), lax.rem(plane + 1, planes)]
            sources += [jnp.where(inside, away, -1), jnp.where(inside, -1, away)]
        for piece, src in zip(weights, sources):

            @pl.when(src >= 0)
            def _(piece=piece, src=src, to=to, cols=cols):
                at = pl.ds(pl.multiple_of(src * rows_each, rows_each), rows_each)
                w_scr[at, to] = piece[:, cols]

    for f in range(fsdp):
        src = lax.rem(core + (fsdp - f), fsdp)
        at = pl.ds(pl.multiple_of(src * slot, 16), slot)
        up = adapts[f][:, :wide]
        low = lax.dot_general(
            up, d_scr[...], (((0,), (0,)), ((), ())), preferred_element_type=F32
        )
        w_scr[at, :] = (w_scr[at, :].astype(F32) + adapter_scale * low[:slot]).astype(BF)
    acc = None
    for f in range(fsdp):
        src = lax.rem(core + (fsdp - f), fsdp)
        w_at = pl.ds(pl.multiple_of(src * slot, 16), wide)
        left = jnp.concatenate([grads[s * fsdp + f][:, :wide] for s in range(half)], axis=0)
        part = nn(left, w_scr[w_at, :])
        acc = part if acc is None else acc + part
    for s in range(half):
        at = pl.ds(pl.multiple_of((mine ^ s) * rows, rows), rows)
        for i in range(len(targets)):
            block = acc[s * rows : (s + 1) * rows, i * LANES : (i + 1) * LANES]
            outs[i][at, :] = block.astype(BF)


def score_block(key, query, k0, q0):
    scores = nt(key, query) * SCORE_SCALE
    if k0 is None or k0 + key.shape[0] - 1 <= q0:
        return scores
    kpos = k0 + lax.broadcasted_iota(jnp.int32, scores.shape, 0)
    qpos = q0 + lax.broadcasted_iota(jnp.int32, scores.shape, 1)
    return jnp.where(kpos <= qpos, scores, masked)


def near_forward_body(q_ref, kv_ref, acc_ref, top_ref, total_ref, prob_ref, vt_scr):
    tokens = q_ref.shape[0]
    block = min(FORWARD_BLOCK, tokens)
    vt_scr[...] = kv_ref[1].T
    for q0 in range(0, tokens, block):
        qs = slice(q0, q0 + block)
        depth = q0 + block
        scores = score_block(kv_ref[0, :depth, :], q_ref[qs, :], 0, q0)
        top = jnp.max(scores, axis=0, keepdims=True)
        prob = jnp.exp(scores - top)
        top_ref[:, qs] = top
        total_ref[:, qs] = jnp.sum(prob, axis=0, keepdims=True)
        half_prob = prob.astype(BF)
        prob_ref[:depth, qs] = half_prob
        acc_ref[:, qs] = nn(vt_scr[:, :depth], half_prob)


def forward_body(fsdp, wide, pos_ref, q_ref, far_ref, acc_ref, top_ref, total_ref, adapt_ref, *refs):
    o_ref, scale_ref, inverse_ref, prob_ref = refs[:4]
    mid_refs, oft_scr = refs[4 : 4 + fsdp], refs[4 + fsdp]
    core, later, own = pos_ref[2], pos_ref[3], pos_ref[4]
    tokens = q_ref.shape[0]
    block = min(FORWARD_BLOCK, tokens)

    @pl.when(later == 0)
    def _():
        inverse = 1.0 / total_ref[...]
        inverse_ref[...] = inverse
        scale_ref[...] = inverse
        o_ref[...] = (acc_ref[...] * inverse).T

    @pl.when(later != 0)
    def _():
        oft_scr[...] = far_ref[1].T
        for q0 in range(0, tokens, block):
            qs = slice(q0, q0 + block)
            far = score_block(far_ref[0], q_ref[qs, :], None, q0)
            top = jnp.maximum(top_ref[:, qs], jnp.max(far, axis=0, keepdims=True))
            prob = jnp.exp(far - top)
            shrink = jnp.exp(top_ref[:, qs] - top)
            total = total_ref[:, qs] * shrink + jnp.sum(prob, axis=0, keepdims=True)
            half_prob = prob.astype(BF)
            prob_ref[:, qs] = half_prob
            inverse = 1.0 / total
            inverse_ref[:, qs] = inverse
            scale_ref[:, qs] = shrink * inverse
            out = (acc_ref[:, qs] * shrink + nn(oft_scr[...], half_prob)) * inverse
            o_ref[qs, :] = out.T

    down = adapt_ref[:, pl.ds(pl.multiple_of(wide + own * LANES, LANES), LANES)]
    rows = tokens // fsdp
    for s in range(fsdp):
        to = lax.rem(core + s, fsdp)
        part = o_ref[pl.ds(pl.multiple_of(to * rows, rows), rows), :]
        mid_refs[s][...] = nt(part.astype(BF), down)


def far_body(half, pos_ref, *refs):
    parts = refs[:half]
    q_ref, far_ref, o_ref, inverse_ref, prob_ref = refs[half : half + 5]
    far_out, dq_ref, do_ref, delta_ref, kt_scr = refs[half + 5 :]
    later = pos_ref[3]
    tokens = q_ref.shape[0]
    block = min(QUERY_BLOCK, tokens)
    total = parts[0][...].astype(F32)
    for s in range(1, half):
        total = total + parts[s][...].astype(F32)
    grad = total.astype(BF)
    do_ref[...] = grad
    delta_ref[...] = jnp.sum((grad.astype(F32) * o_ref[...]).T, axis=0, keepdims=True)

    @pl.when(later != 0)
    def _():
        kt_scr[...] = far_ref[0].T
        for k0 in range(0, tokens, block):
            ks = slice(k0, k0 + block)
            full = prob_ref[ks, :].astype(F32) * inverse_ref[...]
            prob_grad = nt(far_ref[1, ks, :], do_ref[...])
            score_grad = (full * (prob_grad - delta_ref[...])).astype(BF)
            prob = full.astype(BF)
            far_out[0, ks, :] = (SCORE_SCALE * nn(score_grad, q_ref[...])).astype(BF)
            far_out[1, ks, :] = nn(prob, do_ref[...]).astype(BF)
            part = nn(kt_scr[:, ks], score_grad)
            if k0:
                dq_ref[...] += part
            else:
                dq_ref[...] = part

    @pl.when(later == 0)
    def _():
        far_out[...] = jnp.zeros(far_out.shape, BF)
        dq_ref[...] = jnp.zeros(dq_ref.shape, F32)


def near_body(
    q_ref, kv_ref, do_ref, prob_ref, scale_ref, delta_ref, dq_in, dq_ref, near_ref, kt_scr
):
    tokens = q_ref.shape[0]
    block = min(QUERY_BLOCK, tokens)
    kt_scr[...] = kv_ref[0].T
    for q0 in range(0, tokens, block):
        qs = slice(q0, q0 + block)
        depth = q0 + block
        full = prob_ref[:depth, qs].astype(F32) * scale_ref[:, qs]
        prob_grad = nt(kv_ref[1, :depth, :], do_ref[qs, :])
        score_grad = (full * (prob_grad - delta_ref[:, qs])).astype(BF)
        dk = SCORE_SCALE * nn(score_grad, q_ref[qs, :])
        dv = nn(full.astype(BF), do_ref[qs, :])
        if q0:
            near_ref[0, :q0, :] += dk[:q0]
            near_ref[1, :q0, :] += dv[:q0]
        near_ref[0, qs, :] = dk[q0:]
        near_ref[1, qs, :] = dv[q0:]
        dq = dq_in[:, qs] + nn(kt_scr[:, :depth], score_grad)
        dq_ref[qs, :] = (SCORE_SCALE * dq).T.astype(BF)


def merge_body(half, pos_ref, dq_ref, near_ref, back_ref, *out_refs):
    mine = pos_ref[0]
    rows = near_ref.shape[1] // half
    for s in range(half):
        at = pl.ds(pl.multiple_of((mine ^ s) * rows, rows), rows)
        out_refs[s][0] = dq_ref[at, :]
        for i in range(2):
            merged = near_ref[i, at, :] + back_ref[i, at, :].astype(F32)
            out_refs[s][1 + i] = merged.astype(BF)


def unpack_body(half, pos_ref, *refs):
    pieces, outs, sem = refs[:half], refs[half:-1], refs[-1]
    own = pos_ref[4]
    copies = []
    for s in range(half):
        cols = pl.ds(pl.multiple_of((own ^ s) * LANES, LANES), LANES)
        for i in range(3):
            copies.append(
                pltpu.make_async_copy(pieces[s].at[i], outs[i].at[:, cols], sem.at[s * 3 + i])
            )
    for copy in copies:
        copy.start()
    for copy in copies:
        copy.wait()


def adapter_grads_body(half, strips, slot, wide, pos_ref, in_ref, up_ref, down_ref):
    core = pos_ref[2]
    planes = in_ref.shape[0] // half
    width = slot // strips
    step = half * width
    for j in range(half):
        total = in_ref[j]
        for p in range(1, planes):
            total = total + in_ref[p * half + j]
        for i in range(strips):
            to = i * step + j * width
            up_ref[:, to : to + width] = total[:, i * width : (i + 1) * width]
        head = j ^ ((core & 1) * (half // 2))
        down_ref[:, pl.ds(pl.multiple_of(head * LANES, LANES), LANES)] = total[:, wide:]


def adapters_body(half, fsdp, planes, wide, pos_ref, o_ref, *refs):
    both, grads = refs[:fsdp], refs[fsdp : fsdp + half]
    out_ref, scr = refs[fsdp + half :]
    mine, plane, core = pos_ref[0], pos_ref[1], pos_ref[2]
    rank_rows = out_ref.shape[1]
    rank = planes * half * rank_rows
    rows = grads[0].shape[0]
    part_rows = both[0].shape[0]
    for s in range(fsdp):
        src = lax.rem(core + (fsdp - s), fsdp)
        scr[pl.ds(pl.multiple_of(src * part_rows, part_rows), part_rows), :] = both[s][...]
    order = [pl.ds(pl.multiple_of((mine ^ s) * rows, rows), rows) for s in range(half)]
    left = jnp.concatenate([scr[at, rank:] for at in order], axis=0)
    right = jnp.concatenate([ref[:, :wide] for ref in grads], axis=0)
    acc = adapter_scale * nn(left.T, right)
    low = nn(scr[...].T[:rank, :], o_ref[...].astype(BF))
    for p in range(planes):
        for j in range(half):
            at = (p * half + j) * rank_rows
            to = lax.rem(plane + (planes - p), planes) * half + j
            out_ref[to, :, :wide] = acc[at : at + rank_rows, :]
            out_ref[to, :, wide:] = low[at : at + rank_rows, :]


def on_device(
    sizes,
    rotated_query_rows,
    rotated_key_rows,
    saved_value_rows,
    projection_output_gradient,
    frozen_weight_codes,
    block_scale_index,
    block_scale_table,
    adapter_down_matrix,
    adapter_up_matrix,
):
    n_ctx, fsdp = sizes
    half = HALF_GROUP_DEV
    planes = n_ctx // half
    rows = rotated_query_rows.shape[0]
    heads = rotated_query_rows.shape[1] // HEAD_WIDTH
    assert heads == half
    tokens = rows * half
    w_rows, w_cols = frozen_weight_codes.shape
    grad_cols = projection_output_gradient.shape[1]
    strips = grad_cols // (half * w_rows)
    slot = strips * w_rows
    wide = -(-slot // LANES) * LANES
    rank_rows = adapter_down_matrix.shape[0]
    rank = rank_rows * n_ctx

    def head_of(j, f):
        return j ^ ((f & 1) * (half // 2))

    ctx = lax.axis_index("ctx")
    core = lax.axis_index("fsdp")
    mine = ctx % half
    plane = ctx // half
    own = head_of(mine, core)
    later = jnp.where(own < heads // 2, plane % 2, 1 - plane % 2)
    pos = jnp.stack([mine, plane, core, later, own]).astype(jnp.int32)

    def in_plane(x, s):
        if s == 0:
            return x
        return lax.ppermute(x, "ctx", [(i, i ^ s) for i in range(n_ctx)])

    def along(x, s):
        if s == 0:
            return x
        return lax.ppermute(x, "ctx", [(i, (i + s * half) % n_ctx) for i in range(n_ctx)])

    def from_plane(x, *moves):
        route = []
        for group, step in zip(moves[::2], moves[1::2]):
            for p in group:
                route += [(p * half + j, (p + step) * half + j) for j in range(half)]
        return lax.ppermute(x, "ctx", route)

    def across(x, s):
        if s == 0:
            return x
        return lax.ppermute(x, "fsdp", [(i, (i + s) % fsdp) for i in range(fsdp)])

    pairs = []
    for i in range(n_ctx):
        for f in range(fsdp):
            p, j = divmod(i, half)
            if (p % 2 == 0) == (head_of(j, f) < heads // 2):
                pairs.append((i * fsdp + f, (i + half) % n_ctx * fsdp + f))

    def to_later(x):
        return lax.ppermute(x, ("ctx", "fsdp"), pairs)

    def to_earlier(x):
        return lax.ppermute(x, ("ctx", "fsdp"), [(b, a) for a, b in pairs])

    table = block_scale_table.reshape(-1, LANES)
    index = block_scale_index.T
    weight = call(
        dequant_body,
        sds((w_rows, w_cols), BF),
        [pltpu.VMEM(x.shape, x.dtype) for x in (frozen_weight_codes, index, table)]
        + [pltpu.SemaphoreType.DMA((3,))],
        frozen_weight_codes,
        index,
        table,
        in_hbm=True,
    )
    if planes == 4:
        weights = [weight]
        for s in (1, planes - 1):
            weights.append(along(weight, s))
    else:
        weights = [along(weight, s) for s in range(planes)]
    if planes == 4:
        inner, outer = call(
            relay_body, [sds(weight.shape, BF)] * 2, [], pos, *weights[1:], n_scalar=1
        )
        weights.append(from_plane(inner, (1,), 1, (2,), -1))
        weights.append(from_plane(outer, (1,), -1, (2,), 1))

    adapter_cols = wide + heads * HEAD_WIDTH
    sources = (
        rotated_query_rows,
        rotated_key_rows,
        saved_value_rows,
        projection_output_gradient,
        adapter_up_matrix,
        adapter_down_matrix,
    )
    packed = call(
        functools.partial(pack_body, half, strips, wide),
        [sds((rows, wide + 3 * LANES), BF)] * half + [sds((rank_rows, adapter_cols), BF)] * half,
        [pltpu.VMEM(x.shape, BF) for x in sources] + [pltpu.SemaphoreType.DMA((6,))],
        pos,
        *sources,
        n_scalar=1,
        in_hbm=True,
    )
    chunks = [in_plane(x, s) for s, x in enumerate(packed[half:])]
    packed = [in_plane(x, s) for s, x in enumerate(packed[:half])]
    swapped = [across(g, f) for g in packed for f in range(fsdp)]
    adapters = call(
        functools.partial(stack_body, half),
        sds((half, rank_rows, adapter_cols), BF),
        [],
        pos,
        *chunks,
        n_scalar=1,
    )
    adapters = [along(adapters, s) for s in range(planes)]
    adapters = call(ranks_body, sds((rank, adapter_cols), BF), [], *adapters)
    adapts = [across(adapters, f) for f in range(fsdp)]

    query, key_value = call(
        functools.partial(assemble_body, half, wide),
        [sds((tokens, LANES), BF), sds((2, tokens, LANES), BF)],
        [],
        pos,
        *packed,
        n_scalar=1,
    )
    far = to_later(key_value)
    lora = call(
        functools.partial(lora_body, half, fsdp, wide),
        sds((tokens, rank), F32),
        [],
        pos,
        *adapts,
        *swapped,
        n_scalar=1,
    )

    def project(targets):
        return call(
            functools.partial(project_body, half, planes, fsdp, slot, wide, targets),
            [sds((tokens, LANES), BF)] * len(targets),
            [
                pltpu.VMEM((planes * w_rows + wide - slot, LANES * len(targets)), BF),
                pltpu.VMEM((rank, LANES * len(targets)), BF),
            ],
            pos,
            *adapts,
            *swapped,
            *weights,
            n_scalar=1,
        )

    first, second = range(half // 2, half), range(half // 2)
    partial = dict(zip(first, project(tuple(first))))
    partial = {s: in_plane(x, s) for s, x in partial.items()}
    rest = dict(zip(second, project(tuple(second))))
    partial.update({s: in_plane(x, s) for s, x in rest.items()})

    part_rows = tokens // fsdp
    row = sds((1, tokens), F32)
    near_acc, near_top, near_total, near_prob = call(
        near_forward_body,
        [sds((LANES, tokens), F32), row, row, sds((tokens, tokens), BF)],
        [pltpu.VMEM((LANES, tokens), BF)],
        query,
        key_value,
    )
    out, near_scale, inverse, far_prob, *mids = call(
        functools.partial(forward_body, fsdp, wide),
        [sds((tokens, LANES), F32), row, row, sds((tokens, tokens), BF)]
        + [sds((part_rows, rank), F32)] * fsdp,
        [pltpu.VMEM((LANES, tokens), BF)],
        pos,
        query,
        far,
        near_acc,
        near_top,
        near_total,
        adapters,
        n_scalar=1,
    )
    mids = [across(x, f) for f, x in enumerate(mids)]
    both = call(join_body, sds((part_rows, 2 * rank), BF), [], pos, lora, *mids, n_scalar=1)
    both = [in_plane(both, s) for s in range(half)]
    both = call(total_body, sds((part_rows, 2 * rank), BF), [], *both)
    both = [across(both, f) for f in range(fsdp)]
    adapter_grads = call(
        functools.partial(adapters_body, half, fsdp, planes, wide),
        sds((n_ctx, rank_rows, wide + HEAD_WIDTH), F32),
        [pltpu.VMEM((tokens, 2 * rank), BF)],
        pos,
        out,
        *both,
        *packed,
        n_scalar=1,
    )
    reduced = lax.all_to_all(adapter_grads, "ctx", split_axis=0, concat_axis=0, tiled=True)
    up_grad, down_grad = call(
        functools.partial(adapter_grads_body, half, strips, slot, wide),
        [sds((rank_rows, grad_cols), F32), sds((rank_rows, heads * HEAD_WIDTH), F32)],
        [],
        pos,
        reduced,
        n_scalar=1,
    )

    far_part, dq_far, grad_out, delta = call(
        functools.partial(far_body, half),
        [
            sds((2, tokens, LANES), BF),
            sds((LANES, tokens), F32),
            sds((tokens, LANES), BF),
            sds((1, tokens), F32),
        ],
        [pltpu.VMEM((LANES, tokens), BF)],
        pos,
        *[partial[s] for s in range(half)],
        query,
        far,
        out,
        inverse,
        far_prob,
        n_scalar=1,
    )
    back = to_earlier(far_part)
    dq, near = call(
        near_body,
        [sds((tokens, LANES), BF), sds((2, tokens, LANES), F32)],
        [pltpu.VMEM((LANES, tokens), BF)],
        query,
        key_value,
        grad_out,
        near_prob,
        near_scale,
        delta,
        dq_far,
    )
    merged = call(
        functools.partial(merge_body, half),
        [sds((3, rows, LANES), BF)] * half,
        [],
        pos,
        dq,
        near,
        back,
        n_scalar=1,
    )
    merged = [in_plane(x, s) for s, x in enumerate(merged)]
    query_grad, key_grad, value_grad = call(
        functools.partial(unpack_body, half),
        [sds((rows, heads * HEAD_WIDTH), BF)] * 3,
        [pltpu.SemaphoreType.DMA((3 * half,))],
        pos,
        *merged,
        n_scalar=1,
        out_hbm=True,
    )
    return query_grad, key_grad, value_grad, down_grad, up_grad


def solution(mesh):
    split = P("ctx", "fsdp")
    in_specs = (split,) * 6 + (P(),) + (split,) * 2

    def body(*args):
        return on_device((mesh.shape["ctx"], mesh.shape["fsdp"]), *args)

    return jax.shard_map(
        body, mesh=mesh, in_specs=in_specs, out_specs=(split,) * 5, check_vma=False
    )
```
